32 devices in a mesh: body: 8 (over z, y), across: 4 (over x, core).
Axes of the slice: x: 2, y: 2, z: 4, core: 2. Of those that a mesh axis runs over, the one named last changes fastest.
Arguments:
- cotangent: float32 [3, 64, 128, 256], P(None, 'body', 'across'), may hold values from -6 to 6
- shear_modulus: float32 [64, 128, 256], P('body', 'across'), may hold values from 0.3 to 3
- lame_first: float32 [64, 128, 256], P('body', 'across'), may hold values from 0.3 to 3
- inertia: float32 [64, 128, 256], P('body', 'across'), may hold values from 0.02 to 0.2
- surface_points: float32 [8, 4, 16, 3, 128], P('body', 'across'), may hold values from -0.3 to 1, as said below
- point_counts: int32 [8, 4, 16], P('body', 'across'), may hold values from 64 to 128, as said below
- surface_maps: int32 [8, 4, 16, 128], P('body', 'across'), may hold values from 0 to 65535, as said below
- contact_pairs: int32 [8, 4, 3, 32], P('body', 'across'), may hold values from 0 to 15, as said below
Outputs:
- displacement: float32 [3, 64, 128, 256], P(None, 'body', 'across')
- residual: float32 [3, 64, 128, 256], P(None, 'body', 'across')
The draws below stay inside these ranges and needn't reach their ends.
Inputs may be any that keep to these rules, and one draw needn't show every extreme that they name: `surface_points`: coordinates 0 and 1 lie in [0, 1]; coordinate 2 lies in [0.3, 0.6] for even-numbered blocks and in [-0.3, 0] for odd-numbered blocks. `point_counts`: every device has a block with all 128 points active. `surface_maps`: the cells of one device's points are distinct. `contact_pairs`: row 0 holds even block numbers and row 2 odd block numbers below 16; row 1 is a first-split index, and the partner shares the device's second-split index. Every device names every first-split index, its own included, exactly 4 times.
All inputs are finite; a program needn't handle non-finite values.
Results may differ from the reference program's by a relative error of at most 0.0003.
Values sent between devices are 32-bit elements; how exact they have to be, the bound alone decides.
No kernel may reach another device: no remote copies, remote signals or barrier semaphores. Data moves between devices by JAX's collectives and lax.ppermute only.
A program may use at most 192 MiB of HBM per device.

```python
import math
import jax
import jax.numpy as jnp
from jax import lax

SX = 8
SY = 32
SZ = 256
PTS = 128
BLK_DEV = 16
CAP = 4
ITERS = 2
SLABS = 8
ACROSS = 4
FINGER_SLABS = 2
PAIR_DEV = 32
NX = 64
NY = 128
NZ = 256
CELLS = 65536


def draw_surface_points(key, part):
    key_list = jax.random.split(key, 2)
    planar = jax.random.uniform(key_list[0], (SLABS, ACROSS, BLK_DEV, 2, PTS), jnp.float32)
    height_draw = jax.random.uniform(key_list[1], (SLABS, ACROSS, BLK_DEV, 1, PTS), jnp.float32)
    upper = (jnp.arange(BLK_DEV) % 2 == 0)[None, None, :, None, None]
    height = jnp.where(upper, 0.3 + 0.3 * height_draw, -0.3 * height_draw)
    return jnp.concatenate([planar, height], axis=3).astype(jnp.float32)


def draw_point_counts(key, part):
    counts = jax.random.randint(key, (SLABS, ACROSS, BLK_DEV), PTS // 2, PTS + 1, dtype=jnp.int32)
    counts = counts.at[:, :, 0].set(PTS)
    counts = counts.at[:, :, 1].set(PTS // 2)
    return counts


def draw_surface_maps(key, part):

    def one_device(device_index):
        device_key = jax.random.fold_in(key, device_index)
        key_list = jax.random.split(device_key, 2)
        inner_cells = jax.random.permutation(key_list[0], CELLS - 2)[:BLK_DEV * PTS - 2] + 1
        chosen = jnp.concatenate([jnp.array([0, CELLS - 1], dtype=jnp.int32), inner_cells.astype(jnp.int32)])
        return jax.random.permutation(key_list[1], chosen).reshape(BLK_DEV, PTS).astype(jnp.int32)
    return jax.vmap(one_device)(jnp.arange(SLABS * ACROSS, dtype=jnp.int32)).reshape(SLABS, ACROSS, BLK_DEV, PTS)


def draw_contact_pairs(key, part):

    def one_device(device_index):
        device_key = jax.random.fold_in(key, device_index)
        key_list = jax.random.split(device_key, 3)
        partner_rows = (jax.random.permutation(key_list[0], PAIR_DEV) // CAP).astype(jnp.int32)
        own_blocks = 2 * jax.random.randint(key_list[1], (PAIR_DEV,), 0, BLK_DEV // 2, dtype=jnp.int32)
        partner_blocks = 2 * jax.random.randint(key_list[2], (PAIR_DEV,), 0, BLK_DEV // 2, dtype=jnp.int32) + 1
        own_blocks = own_blocks.at[0].set(0)
        partner_blocks = partner_blocks.at[0].set(BLK_DEV - 1)
        return jnp.stack([own_blocks, partner_rows, partner_blocks]).astype(jnp.int32)
    return jax.vmap(one_device)(jnp.arange(SLABS * ACROSS, dtype=jnp.int32)).reshape(SLABS, ACROSS, 3, PAIR_DEV)


def shard_levels(key, extent, shards, smallest, largest):
    loudness, own = 1.0, jax.random.fold_in(key, 6)
    for axis_at, shards_of in shards:
        draws = jnp.exp(jax.random.uniform(jax.random.fold_in(own, axis_at), (shards_of,), jnp.float32, smallest / len(shards), largest / len(shards)))
        loudness = loudness * jnp.repeat(draws, extent[axis_at] // shards_of).reshape([-1 if axis == axis_at else 1 for axis in range(len(extent))])
    return loudness


def centred(rng, extent, width, bound, shards=(), kind=jnp.bfloat16):
    values = jax.random.normal(rng, extent, jnp.float32) * width
    if len(shards) > 0:
        values = shard_levels(rng, extent, shards, -0.22, 0.18) * values
    return jnp.clip(values, min=-bound, max=bound).astype(kind)


def setup_inputs(seed: int = 0) -> dict:
    keys = jax.random.split(jax.random.key(seed), 9)
    cotangent = centred(keys[0], (3, NX, NY, NZ), 1.0, 6.0, ((1, 8), (2, 4)), jnp.float32)
    shear_modulus = jnp.clip(jnp.exp(math.log(3.0) - 2.3025851 * jax.random.uniform(keys[1], (NX, NY, NZ), jnp.float32) ** shard_levels(keys[1], (NX, NY, NZ), ((0, 8), (1, 4)), -0.2, 0.2)), 0.3, 3.0)
    lame_first = jnp.clip(jnp.exp(math.log(3.0) - 2.3025851 * jax.random.uniform(keys[2], (NX, NY, NZ), jnp.float32) ** shard_levels(keys[2], (NX, NY, NZ), ((0, 8), (1, 4)), -0.2, 0.2)), 0.3, 3.0)
    inertia = jnp.clip(jnp.exp(math.log(0.2) - 2.3025851 * jax.random.uniform(keys[3], (NX, NY, NZ), jnp.float32) ** shard_levels(keys[3], (NX, NY, NZ), ((0, 8), (1, 4)), -0.2, 0.2)), 0.02, 0.2)
    surface_points = draw_surface_points(jax.random.fold_in(keys[8], 71), 0)
    point_counts = draw_point_counts(jax.random.fold_in(keys[8], 71), 0)
    surface_maps = draw_surface_maps(jax.random.fold_in(keys[8], 71), 0)
    contact_pairs = draw_contact_pairs(jax.random.fold_in(keys[8], 71), 0)
    return dict(cotangent=cotangent, shear_modulus=shear_modulus, lame_first=lame_first, inertia=inertia, surface_points=surface_points, point_counts=point_counts, surface_maps=surface_maps, contact_pairs=contact_pairs)


barrier_reach = 1.0
barrier_scale = 0.005


def shifted(padded, direction, offset):
    leading = padded.ndim - 3
    selection = [slice(None)] * leading + [slice(1, -1)] * 3
    length = padded.shape[leading + direction]
    selection[leading + direction] = slice(1 + offset, length - 1 + offset)
    return padded[tuple(selection)]


def stencil_apply(vector, padded_vector, shear, lame, padded_shear, padded_lame, inertia, global_rows, cut_row):
    result = inertia[None] * vector
    for direction in range(3):
        selector = (jnp.arange(3) == direction).astype(jnp.float32)[:, None, None, None]
        stiffness = shear[None] + (lame + shear)[None] * selector
        for offset in (1, -1):
            near_vector = shifted(padded_vector, direction, offset)
            near_shear = shifted(padded_shear, direction, offset)
            near_lame = shifted(padded_lame, direction, offset)
            near_stiffness = near_shear[None] + (near_lame + near_shear)[None] * selector
            face_weight = 0.5 * (stiffness + near_stiffness)
            if direction == 0:
                blocked_row = cut_row - 1 if offset == 1 else cut_row
                keep_rows = jnp.where(global_rows == blocked_row, 0.0, 1.0).astype(jnp.float32)
                face_weight = face_weight * keep_rows[None, :, None, None]
            result = result + face_weight * (vector - near_vector)
    return result


def barrier_weights(first_points, second_points, first_count, second_count, live_flag):
    offsets = first_points[:, :, None] - second_points[:, None, :]
    squared = jnp.sum(offsets * offsets, axis=0)
    point_width = first_points.shape[1]
    point_ranks = jnp.arange(point_width, dtype=jnp.int32)
    active = (point_ranks[:, None] < first_count) & (point_ranks[None, :] < second_count)
    active = active & (squared < barrier_reach) & (live_flag > 0)
    safe = jnp.where(active, squared, barrier_reach)
    excess = safe - barrier_reach
    return barrier_scale * (-2.0 * jnp.log(safe / barrier_reach) - 4.0 * excess / safe + (excess * excess) / (safe * safe))


def pair_forces(weights, first_moves, second_moves):
    first_side = first_moves * jnp.sum(weights, axis=1)[None, :] - jnp.einsum("ij,cj->ci", weights, second_moves, precision=lax.Precision.HIGHEST)
    second_side = second_moves * jnp.sum(weights, axis=0)[None, :] - jnp.einsum("ij,ci->cj", weights, first_moves, precision=lax.Precision.HIGHEST)
    return first_side, second_side


def pair_task(packed):
    first_points, second_points, first_moves, second_moves, first_count, second_count, live_flag = packed
    weights = barrier_weights(first_points, second_points, first_count, second_count, live_flag)
    return pair_forces(weights, first_moves, second_moves)


def device_view(vector):
    return vector.reshape(3, SLABS, SX, ACROSS, SY, SZ).transpose(1, 3, 0, 2, 4, 5).reshape(SLABS, ACROSS, 3, SX * SY * SZ)


def grid_view(blocks):
    return blocks.reshape(SLABS, ACROSS, 3, SX, SY, SZ).transpose(2, 0, 3, 1, 4, 5).reshape(3, NX, NY, NZ)


def pick_points(values, cell_maps):
    return values[:, cell_maps].transpose(1, 0, 2)


def place_points(values, cell_maps, forces):
    return values.at[:, cell_maps].add(forces.transpose(1, 0, 2))


def contact(vector, surface_points, point_counts, surface_maps, contact_pairs):
    block_moves = jax.vmap(jax.vmap(pick_points))(device_view(vector), surface_maps)
    slab_ids = jnp.broadcast_to(jnp.arange(SLABS, dtype=jnp.int32)[:, None, None], (SLABS, ACROSS, PAIR_DEV)).reshape(-1)
    across_ids = jnp.broadcast_to(jnp.arange(ACROSS, dtype=jnp.int32)[None, :, None], (SLABS, ACROSS, PAIR_DEV)).reshape(-1)
    own_blocks = contact_pairs[:, :, 0, :].reshape(-1)
    partner_rows = contact_pairs[:, :, 1, :].reshape(-1)
    partner_blocks = contact_pairs[:, :, 2, :].reshape(-1)
    packed = (surface_points[slab_ids, across_ids, own_blocks],
              surface_points[partner_rows, across_ids, partner_blocks],
              block_moves[slab_ids, across_ids, own_blocks],
              block_moves[partner_rows, across_ids, partner_blocks],
              point_counts[slab_ids, across_ids, own_blocks],
              point_counts[partner_rows, across_ids, partner_blocks],
              jnp.ones_like(own_blocks))
    first_side, second_side = lax.map(pair_task, packed, batch_size=64)
    forces = jnp.zeros_like(block_moves).at[slab_ids, across_ids, own_blocks].add(first_side)
    forces = forces.at[partner_rows, across_ids, partner_blocks].add(second_side)
    spread = jax.vmap(jax.vmap(place_points))(jnp.zeros((SLABS, ACROSS, 3, SX * SY * SZ), jnp.float32), surface_maps, forces)
    return grid_view(spread)


def reference(cotangent, shear_modulus, lame_first, inertia, surface_points, point_counts, surface_maps, contact_pairs):
    padded_shear = jnp.pad(shear_modulus, 1)
    padded_lame = jnp.pad(lame_first, 1)
    global_rows = jnp.arange(NX, dtype=jnp.int32)
    cut_row = FINGER_SLABS * SX

    def apply_system(vector):
        padded_vector = jnp.pad(vector, ((0, 0), (1, 1), (1, 1), (1, 1)))
        elastic = stencil_apply(vector, padded_vector, shear_modulus, lame_first, padded_shear, padded_lame, inertia, global_rows, cut_row)
        return elastic + contact(vector, surface_points, point_counts, surface_maps, contact_pairs)

    displacement = jnp.zeros_like(cotangent)
    residual = cotangent
    direction = cotangent
    norm_now = jnp.sum(residual * residual)
    for iteration in range(ITERS):
        applied = apply_system(direction)
        step_length = norm_now / jnp.sum(direction * applied)
        displacement = displacement + step_length * direction
        residual = residual - step_length * applied
        norm_next = jnp.sum(residual * residual)
        direction = residual + (norm_next / norm_now) * direction
        norm_now = norm_next
    return displacement, residual
```

```python
import jax
import jax.numpy as jnp
from jax import lax
from jax.experimental import pallas as pl
from jax.experimental.pallas import tpu as pltpu
from jax.sharding import PartitionSpec as P

F32 = jnp.float32
BF16 = jnp.bfloat16
I32 = jnp.int32

barrier_reach = 1.0
barrier_scale = 0.005
FAR = 1000.0

VMEM = pl.BlockSpec(memory_space=pltpu.VMEM)
SMEM = pl.BlockSpec(memory_space=pltpu.SMEM)


def sds(shape, dtype=F32):
    return jax.ShapeDtypeStruct(shape, dtype)


def call(body, name, in_specs, out_specs, out_shape, scratch=(), cost=2.0):
    estimate = pl.CostEstimate(flops=int(cost * 1e8), transcendentals=0, bytes_accessed=int(cost * 3e6))
    return pl.pallas_call(
        body,
        name=name,
        in_specs=in_specs,
        out_specs=out_specs,
        out_shape=out_shape,
        scratch_shapes=list(scratch),
        cost_estimate=estimate,
        compiler_params=pltpu.CompilerParams(vmem_limit_bytes=56 << 20),
    )


def split(values):
    high = values.astype(BF16)
    low = (values - high.astype(F32)).astype(BF16)
    return high, low


def even_faces(block, axis_parity, last):
    first = jnp.where(axis_parity == 0, last, 0)
    return first, last - first


def write_faces(sources, xe_ref, xo_ref, ye_ref, yo_ref):
    bpar = lax.rem(lax.axis_index("body"), 2)
    apar = lax.rem(lax.axis_index("across"), 2)
    for k, (ref, lead) in enumerate(sources):
        at = (lambda x: ref[lead, x]) if lead is not None else (lambda x: ref[x])
        rows = ref.shape[-3]
        cols = ref.shape[-2]
        xi = jnp.where(bpar == 0, rows - 1, 0)
        xe_ref[k] = at(xi)
        xo_ref[k] = at(rows - 1 - xi)
        for x in range(rows):
            slab = at(x)
            low = slab[0:1]
            high = slab[cols - 1 : cols]
            ye_ref[k, x : x + 1] = jnp.where(apar == 0, high, low)
            yo_ref[k, x : x + 1] = jnp.where(apar == 0, low, high)


def prepare_kernel(
    r_ref, sh_ref, la_ref, pt_ref, cnt_ref, pair_ref,
    xe_ref, xo_ref, ye_ref, yo_ref, msg_ref, own_ref, table_ref, fill_ref,
):
    bodies, width = msg_ref.shape[0], msg_ref.shape[1]
    blocks = pt_ref.shape[0]
    odd_total = blocks // 2
    cap = width - odd_total
    pairs = pair_ref.shape[1]
    lane = lax.broadcasted_iota(I32, (1, pt_ref.shape[2]), 1)
    for d in range(bodies):
        fill_ref[d] = 0

    def masked(k, far):
        return jnp.where(lane < cnt_ref[k], pt_ref[k], far)

    for k in range(blocks):
        own_ref[k, 0:3, :] = masked(k, -FAR)
        own_ref[k, 3:4, :] = jnp.ones_like(lane, F32)

    def odd_blocks(d, carry):
        for j in range(odd_total):
            msg_ref[d, cap + j, 0:3, :] = masked(2 * j + 1, FAR)
            msg_ref[d, cap + j, 3:4, :] = jnp.zeros_like(lane, F32)
        return carry

    lax.fori_loop(0, bodies, odd_blocks, 0)

    def place(n, carry):
        first = pair_ref[0, n]
        dest = pair_ref[1, n]
        second = pair_ref[2, n]
        rank = fill_ref[dest]
        fill_ref[dest] = rank + 1
        msg_ref[dest, rank, 0:3, :] = masked(first, FAR)
        msg_ref[dest, rank, 3:4, :] = jnp.full((1, lane.shape[1]), second.astype(F32))
        table_ref[0, dest * cap + rank] = first
        table_ref[1, dest * cap + rank] = second
        return carry

    lax.fori_loop(0, pairs, place, 0)
    sources = [(r_ref, 0), (r_ref, 1), (r_ref, 2), (sh_ref, None), (la_ref, None)]
    write_faces(sources, xe_ref, xo_ref, ye_ref, yo_ref)


def cell_parts(cells, depth):
    if depth & (depth - 1) == 0:
        shift = depth.bit_length() - 1
        return lax.shift_right_logical(cells, shift), jnp.bitwise_and(cells, depth - 1)
    row = cells // depth
    return row, cells - row * depth


def gather_into(load, rows, depth, map_ref, hi_ref, lo_ref, out_ref):
    for c in range(3):
        value = load(c)
        high, low = split(value)
        hi_ref[c * rows : (c + 1) * rows, :] = high
        lo_ref[c * rows : (c + 1) * rows, :] = low
    span = map_ref.shape[2]
    blocks = out_ref.shape[0]
    per = blocks // map_ref.shape[0]
    points = span // per
    depth_iota = lax.broadcasted_iota(I32, (depth, span), 0)
    row_iota = lax.broadcasted_iota(I32, (rows, span), 0)

    def chunk(j, carry):
        row, deep = cell_parts(map_ref[j], depth)
        onehot = jnp.where(depth_iota == deep, 1.0, 0.0).astype(BF16)
        picked = jnp.dot(hi_ref[...], onehot, preferred_element_type=F32)
        picked = picked + jnp.dot(lo_ref[...], onehot, preferred_element_type=F32)
        here = row_iota == row
        for c in range(3):
            part = jnp.where(here, picked[c * rows : (c + 1) * rows], 0.0)
            line = jnp.sum(part, axis=0, keepdims=True)
            for b in range(per):
                out_ref[j * per + b, c : c + 1, :] = line[:, b * points : (b + 1) * points]
        for b in range(per):
            out_ref[j * per + b, 3:4, :] = jnp.ones((1, points), F32)
        return carry

    lax.fori_loop(0, map_ref.shape[0], chunk, 0)


def gather_kernel(r_ref, map_ref, table_ref, move_ref, msg_ref, hi_ref, lo_ref):
    rows = r_ref.shape[1] * r_ref.shape[2]
    depth = r_ref.shape[3]
    gather_into(
        lambda c: r_ref[c].reshape(rows, depth), rows, depth, map_ref, hi_ref, lo_ref, move_ref
    )
    bodies, width = msg_ref.shape[0], msg_ref.shape[1]
    odd_total = move_ref.shape[0] // 2
    cap = width - odd_total

    def pack(d, carry):
        for s in range(cap):
            msg_ref[d, s] = move_ref[table_ref[0, d * cap + s]]
        for j in range(odd_total):
            msg_ref[d, cap + j] = move_ref[2 * j + 1]
        return carry

    lax.fori_loop(0, bodies, pack, 0)


def weights_kernel(got_ref, own_ref, table_ref, w_ref, target_ref):
    bodies, width = got_ref.shape[0], got_ref.shape[1]
    odd_total = own_ref.shape[0] // 2
    cap = width - odd_total
    pairs = bodies * cap
    points = own_ref.shape[2]

    def find(d, carry):
        for s in range(cap):
            target_ref[d * cap + s] = jnp.max(got_ref[d, s, 3:4, :]).astype(I32)
            target_ref[pairs + d * cap + s] = table_ref[0, d * cap + s]
        return carry

    lax.fori_loop(0, bodies, find, 0)

    def weigh(n, source, target):
        columns = jnp.transpose(jnp.concatenate([source, source], axis=0))
        squared = None
        for c in range(3):
            gap = columns[:, c : c + 1] - target[c : c + 1, :]
            squared = gap * gap if squared is None else squared + gap * gap
        inverse = 1.0 / squared
        q = 1.0 - inverse
        weight = barrier_scale * (-2.0 * jnp.log(squared) - 4.0 * q + q * q)
        weight = jnp.where(squared < barrier_reach, weight, 0.0)
        high, low = split(weight)
        w_ref[n, :, 0:points] = high
        w_ref[n, :, points:] = low

    def device(d, carry):
        for s in range(cap):
            n = d * cap + s
            weigh(n, got_ref[d, s], own_ref[target_ref[n]])
            odd = lax.shift_right_logical(table_ref[1, n], 1)
            weigh(pairs + n, got_ref[d, cap + odd], own_ref[table_ref[0, n]])
        return carry

    lax.fori_loop(0, bodies, device, 0)


def pair_forces(got_ref, slot_of, w_ref, target_ref, acc_ref):
    bodies = got_ref.shape[0]
    pairs = target_ref.shape[0] // 2
    cap = pairs // bodies
    points = got_ref.shape[3]
    acc_ref[...] = jnp.zeros_like(acc_ref)

    def one(n, moves):
        high = moves.astype(BF16).astype(F32)
        lhs = jnp.concatenate([high, moves - high], axis=0).astype(BF16)
        out = jnp.dot(lhs, w_ref[n], preferred_element_type=F32)
        part = (out[0:4, :points] + out[4:8, :points]) + (out[0:4, points:] + out[4:8, points:])
        return target_ref[n], part

    def device(d, carry):
        results = []
        for s in range(cap):
            n = d * cap + s
            results.append(one(n, got_ref[d, s]))
            results.append(one(pairs + n, got_ref[d, slot_of(d, s, n)]))
        for at, part in results:
            acc_ref[at] = acc_ref[at] + part
        return carry

    lax.fori_loop(0, bodies, device, 0)


def forces_one_kernel(
    got_ref, w_ref, target_ref, table_ref, move_ref, next_ref, force_ref, sum_ref, msg_ref, acc_ref
):
    bodies, width = got_ref.shape[0], got_ref.shape[1]
    blocks = move_ref.shape[0]
    cap = width - blocks // 2
    pairs = bodies * cap
    pair_forces(
        got_ref,
        lambda d, s, n: cap + lax.shift_right_logical(table_ref[1, n], 1),
        w_ref, target_ref, acc_ref,
    )
    for k in range(blocks):
        acc = acc_ref[k]
        force = move_ref[k] * acc[3:4] - acc
        force_ref[k] = force
        moved = next_ref[k]
        row = lax.broadcasted_iota(I32, moved.shape, 0)
        sum_ref[k] = jnp.where(row < 3, moved + force, 1.0)

    def pack(d, carry):
        for s in range(cap):
            n = d * cap + s
            msg_ref[d, s] = sum_ref[table_ref[0, n]]
            msg_ref[d, cap + s] = sum_ref[target_ref[n]]
        return carry

    lax.fori_loop(0, bodies, pack, 0)


def forces_two_kernel(got_ref, w_ref, target_ref, move_ref, dots_ref, force_ref, red_ref, acc_ref):
    cap = got_ref.shape[1] // 2
    pair_forces(got_ref, lambda d, s, n: cap + s, w_ref, target_ref, acc_ref)
    total = jnp.zeros((1, move_ref.shape[2]), F32)
    for k in range(move_ref.shape[0]):
        acc = acc_ref[k]
        moved = move_ref[k]
        force = moved * acc[3:4] - acc
        force_ref[k] = force
        total = total + jnp.sum((moved * force)[0:3], axis=0, keepdims=True)
    line = dots_ref[...]
    row = lax.broadcasted_iota(I32, line.shape, 0)
    line = line + jnp.where(row == 3, total, 0.0)
    for d in range(red_ref.shape[0]):
        red_ref[d] = line


def scatter_sum(base, rows, depth, map_ref, force_ref, left_ref, right_ref):
    span = map_ref.shape[2]
    per = force_ref.shape[0] // map_ref.shape[0]
    depth_iota = lax.broadcasted_iota(I32, (depth, span), 0)
    row_iota = lax.broadcasted_iota(I32, (rows, span), 0)
    chunks = map_ref.shape[0]
    for j in range(chunks):
        row, deep = cell_parts(map_ref[j], depth)
        onehot = jnp.where(depth_iota == deep, 1.0, 0.0).astype(BF16)
        right_ref[:, j * span : (j + 1) * span] = onehot
        right_ref[:, (chunks + j) * span : (chunks + j + 1) * span] = onehot
        here = row_iota == row
        for c in range(3):
            line = jnp.concatenate(
                [force_ref[j * per + b, c : c + 1, :] for b in range(per)], axis=1
            )
            high = line.astype(BF16).astype(F32)
            at = slice(c * rows, (c + 1) * rows)
            left_ref[at, j * span : (j + 1) * span] = jnp.where(here, high, 0.0).astype(BF16)
            left_ref[at, (chunks + j) * span : (chunks + j + 1) * span] = jnp.where(
                here, line - high, 0.0
            ).astype(BF16)
    spread = lax.dot_general(
        left_ref[...], right_ref[...], (((1,), (1,)), ((), ())), preferred_element_type=F32
    )
    return [base(c) + spread[c * rows : (c + 1) * rows] for c in range(3)]


def scatter_one_kernel(
    e_ref, force_ref, map_ref, w1_ref, xe_ref, xo_ref, ye_ref, yo_ref, left_ref, right_ref
):
    shape = e_ref.shape[1:]
    rows, depth = shape[0] * shape[1], shape[2]
    sums = scatter_sum(
        lambda c: e_ref[c].reshape(rows, depth), rows, depth, map_ref, force_ref, left_ref, right_ref
    )
    for c in range(3):
        w1_ref[c] = sums[c].reshape(shape)
    write_faces([(w1_ref, 0), (w1_ref, 1), (w1_ref, 2)], xe_ref, xo_ref, ye_ref, yo_ref)


def scatter_two_kernel(e_ref, force_ref, map_ref, w2_ref, left_ref, right_ref):
    shape = e_ref.shape[1:]
    rows, depth = shape[0] * shape[1], shape[2]
    sums = scatter_sum(
        lambda c: e_ref[c].reshape(rows, depth), rows, depth, map_ref, force_ref, left_ref, right_ref
    )
    for c in range(3):
        w2_ref[c] = sums[c].reshape(shape)


def elastic(v_ref, sh_ref, la_ref, in_ref, vector_halo, stiff_halo, emit):
    rows, cols, depth = sh_ref.shape
    b, a = lax.axis_index("body"), lax.axis_index("across")
    bodies, acrosses = lax.axis_size("body"), lax.axis_size("across")
    bpar, apar = lax.rem(b, 2), lax.rem(a, 2)
    cut = bodies // 4
    x_low = jnp.where(b != 0, 1.0, 0.0).astype(F32)
    x_high = jnp.where(b != bodies - 1, 1.0, 0.0).astype(F32)
    keep_low = jnp.where(b != cut, 1.0, 0.0).astype(F32)
    keep_high = jnp.where(b + 1 != cut, 1.0, 0.0).astype(F32)
    y_low = jnp.where(a != 0, 1.0, 0.0).astype(F32)
    y_high = jnp.where(a != acrosses - 1, 1.0, 0.0).astype(F32)
    vxe, vxo, vye, vyo = vector_halo
    sxe, sxo, sye, syo = stiff_halo
    row = lax.broadcasted_iota(I32, (cols, depth), 0)
    lane = lax.broadcasted_iota(I32, (cols, depth), 1)
    z_mask = jnp.where(lane == depth - 1, 0.0, 1.0)
    start = lane == 0
    top = row == cols - 1
    bottom = row == 0

    def stiffness(shear, lame):
        return 0.5 * shear, shear + 0.5 * lame

    def pick(parity, even, odd):
        return jnp.where(parity == 0, even, odd)

    def x_halo(high):
        e, o = (sxe, sxo) if high else (sxo, sxe)
        there = x_high if high else x_low
        shear, lame = pick(bpar, e[3], o[3]), pick(bpar, e[4], o[4])
        e, o = (vxe, vxo) if high else (vxo, vxe)
        values = [there * pick(bpar, e[c], o[c]) for c in range(3)]
        return stiffness(there * shear, there * lame), values

    def y_halo(high, x):
        e, o = (sye, syo) if high else (syo, sye)
        there = y_high if high else y_low
        at = slice(x, x + 1)
        shear, lame = pick(apar, e[3, at], o[3, at]), pick(apar, e[4, at], o[4, at])
        e, o = (vye, vyo) if high else (vyo, vye)
        values = [there * pick(apar, e[c, at], o[c, at]) for c in range(3)]
        return stiffness(there * shear, there * lame), values

    def slab(x):
        return stiffness(sh_ref[x], la_ref[x]), [v_ref[c, x] for c in range(3)]

    def flux(near, far, along, mask):
        (off, diag), values = near
        (far_off, far_diag), far_values = far
        side, front = off + far_off, diag + far_diag
        if mask is not None:
            side, front = side * mask, front * mask
        return [
            (front if c == along else side) * (values[c] - far_values[c]) for c in range(3)
        ]

    before = flux(x_halo(False), slab(0), 0, keep_low)
    here = slab(0)
    for x in range(rows):
        after = slab(x + 1) if x + 1 < rows else x_halo(True)
        out = flux(here, after, 0, None if x + 1 < rows else keep_high)
        (off, diag), values = here
        inertia = in_ref[x]
        total = [inertia * values[c] + (out[c] - before[c]) for c in range(3)]
        before = out

        def up(value, edge):
            return jnp.where(top, edge, pltpu.roll(value, cols - 1, 0))

        (h_off, h_diag), h_values = y_halo(True, x)
        shifted = (up(off, h_off), up(diag, h_diag)), [up(values[c], h_values[c]) for c in range(3)]
        out = flux(here, shifted, 1, None)
        first = (off[0:1], diag[0:1]), [values[c][0:1] for c in range(3)]
        edge = flux(y_halo(False, x), first, 1, None)
        total = [
            total[c] + (out[c] - jnp.where(bottom, edge[c], pltpu.roll(out[c], 1, 0)))
            for c in range(3)
        ]

        def right(value):
            return z_mask * pltpu.roll(value, depth - 1, 1)

        shifted = (right(off), right(diag)), [right(values[c]) for c in range(3)]
        out = flux(here, shifted, 2, None)
        edge = [-(diag if c == 2 else off) * values[c] for c in range(3)]
        total = [
            total[c] + (out[c] - jnp.where(start, edge[c], pltpu.roll(out[c], 1, 1)))
            for c in range(3)
        ]
        emit(x, total)
        here = after


def stencil_one_kernel(
    r_ref, sh_ref, la_ref, in_ref, xe, xo, ye, yo, map_ref, e_ref, next_ref, hi_ref, lo_ref
):
    def emit(x, total):
        for c in range(3):
            e_ref[c, x] = total[c]

    elastic(r_ref, sh_ref, la_ref, in_ref, (xe, xo, ye, yo), (xe, xo, ye, yo), emit)
    rows, depth = e_ref.shape[1] * e_ref.shape[2], e_ref.shape[3]
    gather_into(
        lambda c: e_ref[c].reshape(rows, depth), rows, depth, map_ref, hi_ref, lo_ref, next_ref
    )


def fold(value):
    cols, depth = value.shape
    total = None
    for k in range(depth // 128):
        part = value[:, k * 128 : (k + 1) * 128]
        part = jnp.sum(part.reshape(cols // 8, 8, 128), axis=0)
        total = part if total is None else total + part
    return total


def stencil_two_kernel(
    w_ref, sh_ref, la_ref, in_ref, xe, xo, ye, yo, cxe, cxo, cye, cyo, r_ref, e_ref, dots_ref
):
    sums = [jnp.zeros((8, 128), F32) for _ in range(4)]

    def emit(x, total):
        for c in range(3):
            e_ref[c, x] = total[c]
            r, w = r_ref[c, x], w_ref[c, x]
            sums[0] = sums[0] + fold(r * r)
            sums[1] = sums[1] + fold(r * w)
            sums[2] = sums[2] + fold(w * w)
            sums[3] = sums[3] + fold(w * total[c])

    elastic(w_ref, sh_ref, la_ref, in_ref, (xe, xo, ye, yo), (cxe, cxo, cye, cyo), emit)
    for k in range(4):
        dots_ref[k : k + 1, :] = jnp.sum(sums[k], axis=0, keepdims=True)


def final_kernel(r_ref, w1_ref, w2_ref, red_ref, x_ref, res_ref):
    line = jnp.sum(red_ref[...], axis=0)
    moment = [
        jnp.broadcast_to(jnp.sum(line[k : k + 1], axis=1, keepdims=True), (8, 128)) for k in range(4)
    ]
    m0, m1, m2, m3 = moment
    step = m0 / m1
    norm = (m0 - step * m1) + step * (step * m2 - m1)
    ratio = norm / m0
    grown = 1.0 + ratio
    curve = grown * (grown * m1 - 2.0 * step * m2) + step * step * m3
    next_step = norm / curve
    alpha = step + next_step * grown
    gamma = next_step * step
    cols, depth = r_ref.shape[2], r_ref.shape[3]
    alpha = jnp.broadcast_to(alpha[0:1, 0:1], (cols, depth))
    gamma = jnp.broadcast_to(gamma[0:1, 0:1], (cols, depth))
    for c in range(3):
        for x in range(r_ref.shape[1]):
            r, w1 = r_ref[c, x], w1_ref[c, x]
            x_ref[c, x] = alpha * r - gamma * w1
            res_ref[c, x] = r - alpha * w1 + gamma * w2_ref[c, x]


def exchange(xe, xo, ye, yo):
    def pairs(axis, start):
        count = lax.axis_size(axis)
        chosen = []
        for i in range(count):
            partner = i + 1 if (i - start) % 2 == 0 else i - 1
            chosen.append((i, partner if 0 <= partner < count else i))
        return chosen

    return (
        lax.ppermute(xe, "body", pairs("body", 0)),
        lax.ppermute(xo, "body", pairs("body", 1)),
        lax.ppermute(ye, "across", pairs("across", 0)),
        lax.ppermute(yo, "across", pairs("across", 1)),
    )


def on_device(
    cotangent, shear, lame, inertia, surface_points, point_counts, surface_maps, contact_pairs
):
    rows, cols, depth = shear.shape
    points = surface_points[0, 0]
    counts = point_counts[0, 0]
    cell_maps = surface_maps[0, 0]
    pair_table = contact_pairs[0, 0]
    blocks, _, width = points.shape
    pairs = pair_table.shape[1]
    bodies, acrosses = lax.axis_size("body"), lax.axis_size("across")
    devices = bodies * acrosses
    cap = pairs // bodies
    slots = cap + blocks // 2
    chunks = blocks // 2
    cell_maps = cell_maps.reshape(chunks, 1, 2 * width)
    flat = rows * cols
    vector = sds((3, rows, cols, depth))

    def faces(count):
        return (
            sds((count, cols, depth)), sds((count, cols, depth)),
            sds((count, rows, depth)), sds((count, rows, depth)),
        )

    moves = sds((blocks, 4, width))
    halves = (pltpu.VMEM((3 * flat, depth), BF16), pltpu.VMEM((3 * flat, depth), BF16))
    wide = 2 * blocks * width
    sides = (pltpu.VMEM((3 * flat, wide), BF16), pltpu.VMEM((depth, wide), BF16))

    xe, xo, ye, yo, static_message, own_points, table = call(
        prepare_kernel, "prepare",
        [VMEM] * 4 + [SMEM] * 2,
        [VMEM] * 6 + [SMEM],
        faces(5) + (sds((bodies, slots, 4, width)), moves, sds((2, pairs), I32)),
        scratch=(pltpu.SMEM((bodies,), I32),), cost=1.0,
    )(cotangent, shear, lame, points, counts, pair_table)
    got_static = lax.all_to_all(static_message, "body", 0, 0, tiled=True)
    first_moves, message = call(
        gather_kernel, "gather", [VMEM] * 2 + [SMEM], [VMEM] * 2,
        (moves, sds((bodies, slots, 4, width))), scratch=halves, cost=3.0,
    )(cotangent, cell_maps, table)
    got_moves = lax.all_to_all(message, "body", 0, 0, tiled=True)
    halo = exchange(xe, xo, ye, yo)
    weights, targets = call(
        weights_kernel, "weights", [VMEM] * 2 + [SMEM], [VMEM, SMEM],
        (sds((2 * pairs, width, 2 * width), BF16), sds((2 * pairs,), I32)), cost=6.0,
    )(got_static, own_points, table)
    elastic_one, next_moves = call(
        stencil_one_kernel, "stencil_one", [VMEM] * 9, [VMEM] * 2, (vector, moves),
        scratch=halves, cost=5.0,
    )(cotangent, shear, lame, inertia, *halo, cell_maps)
    force_one, second_moves, message = call(
        forces_one_kernel, "forces_one", [VMEM] * 2 + [SMEM] * 2 + [VMEM] * 2, [VMEM] * 3,
        (moves, moves, sds((bodies, 2 * cap, 4, width))),
        scratch=(pltpu.VMEM((blocks, 4, width), F32),), cost=2.0,
    )(got_moves, weights, targets, table, first_moves, next_moves)
    got_moves = lax.all_to_all(message, "body", 0, 0, tiled=True)
    w1, xe, xo, ye, yo = call(
        scatter_one_kernel, "scatter_one", [VMEM] * 3, [VMEM] * 5, (vector,) + faces(3),
        scratch=sides, cost=3.0,
    )(elastic_one, force_one, cell_maps)
    halo_two = exchange(xe, xo, ye, yo)
    elastic_two, dots = call(
        stencil_two_kernel, "stencil_two", [VMEM] * 13, [VMEM] * 2, (vector, sds((4, 128))), cost=3.0,
    )(w1, shear, lame, inertia, *halo_two, *halo, cotangent)
    force_two, partial = call(
        forces_two_kernel, "forces_two", [VMEM] * 2 + [SMEM] + [VMEM] * 2, [VMEM] * 2,
        (moves, sds((devices, 4, 128))),
        scratch=(pltpu.VMEM((blocks, 4, width), F32),), cost=2.0,
    )(got_moves, weights, targets, second_moves, dots)
    sums = lax.all_to_all(partial, ("body", "across"), 0, 0, tiled=True)
    w2 = call(
        scatter_two_kernel, "scatter_two", [VMEM] * 3, VMEM, vector, scratch=sides, cost=3.0,
    )(elastic_two, force_two, cell_maps)
    return call(
        final_kernel, "final", [VMEM] * 4, [VMEM] * 2, (vector, vector), cost=1.0,
    )(cotangent, w1, w2, sums)


def solution(mesh):
    placed = (
        P(None, "body", "across", None),
        P("body", "across", None),
        P("body", "across", None),
        P("body", "across", None),
        P("body", "across", None, None, None),
        P("body", "across", None),
        P("body", "across", None, None),
        P("body", "across", None, None),
    )
    return jax.shard_map(
        on_device,
        mesh=mesh,
        in_specs=placed,
        out_specs=(P(None, "body", "across", None), P(None, "body", "across", None)),
        check_vma=False,
    )
```

```python
import jax
import jax.numpy as jnp
from jax import lax
from jax.experimental import pallas as pl
from jax.experimental.pallas import tpu as pltpu
from jax.sharding import PartitionSpec as P

F32 = jnp.float32
BF16 = jnp.bfloat16
I32 = jnp.int32

barrier_reach = 1.0
barrier_scale = 0.005
FAR = 1000.0

VMEM = pl.BlockSpec(memory_space=pltpu.VMEM)
SMEM = pl.BlockSpec(memory_space=pltpu.SMEM)
HBM = pl.BlockSpec(memory_space=pltpu.HBM)


def sds(shape, dtype=F32):
    return jax.ShapeDtypeStruct(shape, dtype)


def call(body, name, in_specs, out_specs, out_shape, scratch=(), cost=2.0, mib=8):
    estimate = pl.CostEstimate(flops=int(cost * 1e8), transcendentals=0, bytes_accessed=int(cost * 3e6))
    return pl.pallas_call(
        body,
        name=name,
        in_specs=in_specs,
        out_specs=out_specs,
        out_shape=out_shape,
        scratch_shapes=list(scratch),
        cost_estimate=estimate,
        compiler_params=pltpu.CompilerParams(vmem_limit_bytes=mib << 20),
    )


def in_hbm(*arrays):
    return tuple(pltpu.with_memory_space_constraint(array, pltpu.HBM) for array in arrays)


def split(values):
    high = values.astype(BF16)
    low = (values - high.astype(F32)).astype(BF16)
    return high, low


def even_faces(block, axis_parity, last):
    first = jnp.where(axis_parity == 0, last, 0)
    return first, last - first


def write_faces(sources, xe_ref, xo_ref, ye_ref, yo_ref):
    bpar = lax.rem(lax.axis_index("body"), 2)
    apar = lax.rem(lax.axis_index("across"), 2)
    for k, (ref, lead) in enumerate(sources):
        at = (lambda x: ref[lead, x]) if lead is not None else (lambda x: ref[x])
        rows = ref.shape[-3]
        cols = ref.shape[-2]
        xi = jnp.where(bpar == 0, rows - 1, 0)
        xe_ref[k] = at(xi)
        xo_ref[k] = at(rows - 1 - xi)
        for x in range(rows):
            slab = at(x)
            low = slab[0:1]
            high = slab[cols - 1 : cols]
            ye_ref[k, x : x + 1] = jnp.where(apar == 0, high, low)
            yo_ref[k, x : x + 1] = jnp.where(apar == 0, low, high)


def cell_parts(cells, depth):
    if depth & (depth - 1) == 0:
        shift = depth.bit_length() - 1
        return lax.shift_right_logical(cells, shift), jnp.bitwise_and(cells, depth - 1)
    row = cells // depth
    return row, cells - row * depth


def gather_into(load, rows, depth, map_ref, both_ref, write):
    for c in range(3):
        high, low = split(load(c))
        both_ref[c * rows : (c + 1) * rows, 0:depth] = high
        both_ref[c * rows : (c + 1) * rows, depth:] = low
    chunks, _, span = map_ref.shape
    depth_iota = lax.broadcasted_iota(I32, (depth, span), 0)
    row_iota = lax.broadcasted_iota(I32, (rows, span), 0)

    def chunk(j, carry):
        row, deep = cell_parts(map_ref[j], depth)
        onehot = jnp.where(depth_iota == deep, 1.0, 0.0).astype(BF16)
        onehot = jnp.concatenate([onehot, onehot], axis=0)
        picked = jnp.dot(both_ref[...], onehot, preferred_element_type=F32)
        here = row_iota == row
        for c in range(3):
            part = jnp.where(here, picked[c * rows : (c + 1) * rows], 0.0)
            write(j, c, jnp.sum(part, axis=0, keepdims=True))
        return carry

    lax.fori_loop(0, chunks, chunk, 0)


def open_kernel(
    r_hbm, sh_hbm, la_hbm, in_hbm, pt_hbm, cnt_hbm, pair_hbm, map_hbm,
    r_ref, sh_ref, la_ref, in_ref, map_ref,
    xe_ref, xo_ref, ye_ref, yo_ref, own_ref, move_ref, msg_ref, table_ref,
    pt_ref, cnt_ref, pair_ref, fill_ref, sent_ref, both_ref, sem,
):
    copies = [
        pltpu.make_async_copy(source, target, sem.at[k])
        for k, (source, target) in enumerate([
            (cnt_hbm, cnt_ref), (pair_hbm, pair_ref), (pt_hbm, pt_ref), (map_hbm, map_ref),
            (r_hbm.at[0], r_ref.at[0]), (r_hbm.at[1], r_ref.at[1]), (r_hbm.at[2], r_ref.at[2]),
            (sh_hbm, sh_ref), (la_hbm, la_ref), (in_hbm, in_ref),
        ])
    ]
    for copy in copies:
        copy.start()
    bodies, width = msg_ref.shape[0], msg_ref.shape[1]
    blocks = own_ref.shape[0]
    odd_total = blocks // 2
    cap = width - odd_total
    pairs = table_ref.shape[1]
    points = own_ref.shape[2]
    lane = lax.broadcasted_iota(I32, (1, points), 1)
    row = lax.broadcasted_iota(I32, (8, points), 0)
    for copy in copies[:4]:
        copy.wait()
    for d in range(bodies):
        fill_ref[d] = 0

    def place(n, carry):
        dest = pair_ref[1, 0, n]
        rank = fill_ref[dest]
        fill_ref[dest] = rank + 1
        table_ref[0, dest * cap + rank] = pair_ref[0, 0, n]
        table_ref[1, dest * cap + rank] = pair_ref[2, 0, n]
        return carry

    lax.fori_loop(0, pairs, place, 0)
    blank = jnp.zeros((1, points), F32)
    for k in range(blocks):
        tile = jnp.concatenate([pt_ref[c, k : k + 1, :] for c in range(3)] + [blank], axis=0)
        own_ref[k] = jnp.where(lane < cnt_ref[k], tile, -FAR)
        sent_ref[k, 4:8, :] = jnp.where(lane < cnt_ref[k], tile, FAR)
        sent_ref[k, 3:4, :] = blank + 1.0
        move_ref[k, 3:4, :] = blank + 1.0
    for copy in copies[4:]:
        copy.wait()
    rows, depth = r_ref.shape[1] * r_ref.shape[2], r_ref.shape[3]

    def write(j, c, line):
        per = line.shape[1] // points
        for b in range(per):
            part = line[:, b * points : (b + 1) * points]
            move_ref[j * per + b, c : c + 1, :] = part
            sent_ref[j * per + b, c : c + 1, :] = part

    gather_into(lambda c: r_ref[c].reshape(rows, depth), rows, depth, map_ref, both_ref, write)

    def pack(d, carry):
        for s in range(cap):
            second = table_ref[1, d * cap + s].astype(F32)
            msg_ref[d, s] = jnp.where(row == 7, second, sent_ref[table_ref[0, d * cap + s]])
        for j in range(odd_total):
            msg_ref[d, cap + j] = sent_ref[2 * j + 1]
        return carry

    lax.fori_loop(0, bodies, pack, 0)
    sources = [(r_ref, 0), (r_ref, 1), (r_ref, 2), (sh_ref, None), (la_ref, None)]
    write_faces(sources, xe_ref, xo_ref, ye_ref, yo_ref)


def weigh(tile, target):
    columns = jnp.transpose(tile)
    squared = None
    for c in range(3):
        gap = columns[:, 4 + c : 5 + c] - target[c : c + 1, :]
        squared = gap * gap if squared is None else squared + gap * gap
    q = 1.0 - 1.0 / squared
    weight = barrier_scale * (-2.0 * jnp.log(squared) - 4.0 * q + q * q)
    return jnp.where(squared < barrier_reach, weight, 0.0)


def pair_part(moves, weights):
    points = moves.shape[1]
    high = moves.astype(BF16).astype(F32)
    lhs = jnp.concatenate([high, moves - high], axis=0).astype(BF16)
    out = jnp.dot(lhs, weights, preferred_element_type=F32)
    return (out[0:4, :points] + out[4:8, :points]) + (out[0:4, points:] + out[4:8, points:])


def forces_one_kernel(
    got_ref, own_ref, table_ref, move_ref, next_ref,
    force_ref, sum_ref, msg_ref, target_ref, w_hbm, w_ref, acc_ref, sem,
):
    bodies, width = got_ref.shape[0], got_ref.shape[1]
    blocks, _, points = move_ref.shape
    cap = width - blocks // 2
    acc_ref[...] = jnp.zeros_like(acc_ref)

    def keep(d):
        return pltpu.make_async_copy(w_ref.at[d], w_hbm.at[d], sem.at[d])

    def device(d, carry):
        work = []
        for s in range(cap):
            n = d * cap + s
            tile = got_ref[d, s]
            at = jnp.max(tile[7:8]).astype(I32)
            target_ref[n] = at
            work.append((tile, at))
            first = table_ref[0, n]
            odd = lax.shift_right_logical(table_ref[1, n], 1)
            work.append((got_ref[d, cap + odd], first))
        parts = []
        for k, (tile, at) in enumerate(work):
            high, low = split(weigh(tile, own_ref[at]))
            both = jnp.concatenate([high, low], axis=1)
            w_ref[d, k] = both
            parts.append(pair_part(tile[0:4], both))
        for (_, at), part in zip(work, parts):
            acc_ref[at] = acc_ref[at] + part
        keep(d).start()
        return carry

    lax.fori_loop(0, bodies, device, 0)
    row = lax.broadcasted_iota(I32, (4, points), 0)
    inner = jnp.zeros((4, points), F32)
    for k in range(blocks):
        acc = acc_ref[k]
        force = move_ref[k] * acc[3:4] - acc
        force_ref[k] = force
        sum_ref[k] = jnp.where(row < 3, next_ref[k] + force, 1.0)
        inner = inner + move_ref[k] * force
    inner = jnp.sum(inner[0:3], axis=0, keepdims=True)
    sum_ref[blocks] = next_ref[blocks] + jnp.where(row == 1, inner, 0.0)

    def pack(d, carry):
        for s in range(cap):
            n = d * cap + s
            msg_ref[d, s] = sum_ref[table_ref[0, n]]
            msg_ref[d, cap + s] = sum_ref[target_ref[n]]
        return carry

    lax.fori_loop(0, bodies, pack, 0)

    def finish(d, carry):
        keep(d).wait()
        return carry

    lax.fori_loop(0, bodies, finish, 0)


def scatter_sum(base, rows, depth, map_ref, force_ref, left_ref, right_ref):
    span = map_ref.shape[2]
    per = force_ref.shape[0] // map_ref.shape[0]
    depth_iota = lax.broadcasted_iota(I32, (depth, span), 0)
    row_iota = lax.broadcasted_iota(I32, (rows, span), 0)
    chunks = map_ref.shape[0]
    for j in range(chunks):
        row, deep = cell_parts(map_ref[j], depth)
        onehot = jnp.where(depth_iota == deep, 1.0, 0.0).astype(BF16)
        right_ref[:, j * span : (j + 1) * span] = onehot
        right_ref[:, (chunks + j) * span : (chunks + j + 1) * span] = onehot
        here = row_iota == row
        for c in range(3):
            line = jnp.concatenate(
                [force_ref[j * per + b, c : c + 1, :] for b in range(per)], axis=1
            )
            high = line.astype(BF16).astype(F32)
            at = slice(c * rows, (c + 1) * rows)
            left_ref[at, j * span : (j + 1) * span] = jnp.where(here, high, 0.0).astype(BF16)
            left_ref[at, (chunks + j) * span : (chunks + j + 1) * span] = jnp.where(
                here, line - high, 0.0
            ).astype(BF16)
    spread = lax.dot_general(
        left_ref[...], right_ref[...], (((1,), (1,)), ((), ())), preferred_element_type=F32
    )
    return [base(c) + spread[c * rows : (c + 1) * rows] for c in range(3)]


def scatter_one_kernel(
    e_ref, force_ref, map_ref, w1_ref, xe_ref, xo_ref, ye_ref, yo_ref, left_ref, right_ref
):
    shape = e_ref.shape[1:]
    rows, depth = shape[0] * shape[1], shape[2]
    sums = scatter_sum(
        lambda c: e_ref[c].reshape(rows, depth), rows, depth, map_ref, force_ref, left_ref, right_ref
    )
    for c in range(3):
        w1_ref[c] = sums[c].reshape(shape)
    write_faces([(w1_ref, 0), (w1_ref, 1), (w1_ref, 2)], xe_ref, xo_ref, ye_ref, yo_ref)


def scatter_two_kernel(
    e_ref, force_ref, map_ref, r_hbm, w2_ref, r_ref, left_ref, right_ref, sem
):
    copy = pltpu.make_async_copy(r_hbm, r_ref, sem)
    copy.start()
    shape = e_ref.shape[1:]
    rows, depth = shape[0] * shape[1], shape[2]
    sums = scatter_sum(
        lambda c: e_ref[c].reshape(rows, depth), rows, depth, map_ref, force_ref, left_ref, right_ref
    )
    for c in range(3):
        w2_ref[c] = sums[c].reshape(shape)
    copy.wait()


def elastic(v_ref, sh_ref, la_ref, in_ref, vector_halo, stiff_halo, emit):
    rows, cols, depth = sh_ref.shape
    b, a = lax.axis_index("body"), lax.axis_index("across")
    bodies, acrosses = lax.axis_size("body"), lax.axis_size("across")
    bpar, apar = lax.rem(b, 2), lax.rem(a, 2)
    cut = bodies // 4
    x_low = jnp.where(b != 0, 1.0, 0.0).astype(F32)
    x_high = jnp.where(b != bodies - 1, 1.0, 0.0).astype(F32)
    keep_low = jnp.where(b != cut, 1.0, 0.0).astype(F32)
    keep_high = jnp.where(b + 1 != cut, 1.0, 0.0).astype(F32)
    y_low = jnp.where(a != 0, 1.0, 0.0).astype(F32)
    y_high = jnp.where(a != acrosses - 1, 1.0, 0.0).astype(F32)
    vxe, vxo, vye, vyo = vector_halo
    sxe, sxo, sye, syo = stiff_halo
    row = lax.broadcasted_iota(I32, (cols, depth), 0)
    lane = lax.broadcasted_iota(I32, (cols, depth), 1)
    z_mask = jnp.where(lane == depth - 1, 0.0, 1.0)
    start = lane == 0
    top = row == cols - 1
    bottom = row == 0

    def stiffness(shear, lame):
        return 0.5 * shear, shear + 0.5 * lame

    def pick(parity, even, odd):
        return jnp.where(parity == 0, even, odd)

    def x_halo(high):
        e, o = (sxe, sxo) if high else (sxo, sxe)
        there = x_high if high else x_low
        shear, lame = pick(bpar, e[3], o[3]), pick(bpar, e[4], o[4])
        e, o = (vxe, vxo) if high else (vxo, vxe)
        values = [there * pick(bpar, e[c], o[c]) for c in range(3)]
        return stiffness(there * shear, there * lame), values

    def y_halo(high, x):
        e, o = (sye, syo) if high else (syo, sye)
        there = y_high if high else y_low
        at = slice(x, x + 1)
        shear, lame = pick(apar, e[3, at], o[3, at]), pick(apar, e[4, at], o[4, at])
        e, o = (vye, vyo) if high else (vyo, vye)
        values = [there * pick(apar, e[c, at], o[c, at]) for c in range(3)]
        return stiffness(there * shear, there * lame), values

    def slab(x):
        return stiffness(sh_ref[x], la_ref[x]), [v_ref[c, x] for c in range(3)]

    def flux(near, far, along, mask):
        (off, diag), values = near
        (far_off, far_diag), far_values = far
        side, front = off + far_off, diag + far_diag
        if mask is not None:
            side, front = side * mask, front * mask
        return [
            (front if c == along else side) * (values[c] - far_values[c]) for c in range(3)
        ]

    before = flux(x_halo(False), slab(0), 0, keep_low)
    here = slab(0)
    for x in range(rows):
        after = slab(x + 1) if x + 1 < rows else x_halo(True)
        out = flux(here, after, 0, None if x + 1 < rows else keep_high)
        (off, diag), values = here
        inertia = in_ref[x]
        total = [inertia * values[c] + (out[c] - before[c]) for c in range(3)]
        before = out

        def up(value, edge):
            return jnp.where(top, edge, pltpu.roll(value, cols - 1, 0))

        (h_off, h_diag), h_values = y_halo(True, x)
        shifted = (up(off, h_off), up(diag, h_diag)), [up(values[c], h_values[c]) for c in range(3)]
        out = flux(here, shifted, 1, None)
        first = (off[0:1], diag[0:1]), [values[c][0:1] for c in range(3)]
        edge = flux(y_halo(False, x), first, 1, None)
        total = [
            total[c] + (out[c] - jnp.where(bottom, edge[c], pltpu.roll(out[c], 1, 0)))
            for c in range(3)
        ]

        def right(value):
            return z_mask * pltpu.roll(value, depth - 1, 1)

        shifted = (right(off), right(diag)), [right(values[c]) for c in range(3)]
        out = flux(here, shifted, 2, None)
        edge = [-(diag if c == 2 else off) * values[c] for c in range(3)]
        total = [
            total[c] + (out[c] - jnp.where(start, edge[c], pltpu.roll(out[c], 1, 1)))
            for c in range(3)
        ]
        emit(x, total)
        here = after


def stencil_one_kernel(
    r_ref, sh_ref, la_ref, in_ref, xe, xo, ye, yo, map_ref, e_ref, next_ref, both_ref
):
    sums = [jnp.zeros((8, 128), F32) for _ in range(2)]

    def emit(x, total):
        for c in range(3):
            e_ref[c, x] = total[c]
            r = r_ref[c, x]
            sums[0] = sums[0] + fold(r * r)
            sums[1] = sums[1] + fold(r * total[c])

    elastic(r_ref, sh_ref, la_ref, in_ref, (xe, xo, ye, yo), (xe, xo, ye, yo), emit)
    rows, depth = e_ref.shape[1] * e_ref.shape[2], e_ref.shape[3]
    points = next_ref.shape[2]

    def write(j, c, line):
        per = line.shape[1] // points
        for b in range(per):
            next_ref[j * per + b, c : c + 1, :] = line[:, b * points : (b + 1) * points]

    blocks = next_ref.shape[0] - 1
    for k in range(blocks):
        next_ref[k, 3:4, :] = jnp.zeros((1, points), F32)
    lines = [jnp.sum(value, axis=0, keepdims=True) for value in sums]
    next_ref[blocks] = jnp.concatenate(lines + [jnp.zeros((2, points), F32)], axis=0)
    gather_into(lambda c: e_ref[c].reshape(rows, depth), rows, depth, map_ref, both_ref, write)


def fold(value):
    cols, depth = value.shape
    total = None
    for k in range(depth // 128):
        part = value[:, k * 128 : (k + 1) * 128]
        part = jnp.sum(part.reshape(cols // 8, 8, 128), axis=0)
        total = part if total is None else total + part
    return total


def apply_two_kernel(
    w1_ref, sh_ref, la_ref, in_ref, xe, xo, ye, yo, cxe, cxo, cye, cyo,
    got_ref, target_ref, table_ref, move_ref, w_hbm,
    e_ref, force_ref, red_ref, w_ref, acc_ref, sem,
):
    bodies, width = got_ref.shape[0], got_ref.shape[1]
    cap = width // 2
    blocks, points = move_ref.shape[0] - 1, move_ref.shape[2]

    def fetch(d):
        return pltpu.make_async_copy(w_hbm.at[d], w_ref.at[d], sem.at[d])

    def begin(d, carry):
        fetch(d).start()
        return carry

    lax.fori_loop(0, bodies, begin, 0)
    sums = [jnp.zeros((8, 128), F32) for _ in range(2)]

    def emit(x, total):
        for c in range(3):
            e_ref[c, x] = total[c]
            w = w1_ref[c, x]
            sums[0] = sums[0] + fold(w * w)
            sums[1] = sums[1] + fold(w * total[c])

    elastic(w1_ref, sh_ref, la_ref, in_ref, (xe, xo, ye, yo), (cxe, cxo, cye, cyo), emit)
    acc_ref[...] = jnp.zeros_like(acc_ref)

    def device(d, carry):
        fetch(d).wait()
        work = []
        for s in range(cap):
            n = d * cap + s
            work.append((target_ref[n], pair_part(got_ref[d, s], w_ref[d, 2 * s])))
            work.append((table_ref[0, n], pair_part(got_ref[d, cap + s], w_ref[d, 2 * s + 1])))
        for at, part in work:
            acc_ref[at] = acc_ref[at] + part
        return carry

    lax.fori_loop(0, bodies, device, 0)
    inner = jnp.zeros((4, points), F32)
    for k in range(blocks):
        acc = acc_ref[k]
        moved = move_ref[k]
        force = moved * acc[3:4] - acc
        force_ref[k] = force
        inner = inner + moved * force
    lines = [jnp.sum(value, axis=0, keepdims=True) for value in sums]
    lines[1] = lines[1] + jnp.sum(inner[0:3], axis=0, keepdims=True)
    line = jnp.concatenate([move_ref[blocks][0:2]] + lines, axis=0)
    for d in range(red_ref.shape[0]):
        red_ref[d] = line


def final_kernel(r_ref, w1_ref, w2_ref, red_ref, x_hbm, res_hbm, x_ref, res_ref, sem):
    line = jnp.sum(red_ref[...], axis=0)
    moment = [
        jnp.broadcast_to(jnp.sum(line[k : k + 1], axis=1, keepdims=True), (8, 128)) for k in range(4)
    ]
    m0, m1, m2, m3 = moment
    step = m0 / m1
    norm = (m0 - step * m1) + step * (step * m2 - m1)
    ratio = norm / m0
    grown = 1.0 + ratio
    curve = grown * (grown * m1 - 2.0 * step * m2) + step * step * m3
    next_step = norm / curve
    alpha = step + next_step * grown
    gamma = next_step * step
    cols, depth = r_ref.shape[2], r_ref.shape[3]
    alpha = jnp.broadcast_to(alpha[0:1, 0:1], (cols, depth))
    gamma = jnp.broadcast_to(gamma[0:1, 0:1], (cols, depth))
    copies = []
    for c in range(3):
        for x in range(r_ref.shape[1]):
            r, w1 = r_ref[c, x], w1_ref[c, x]
            x_ref[c, x] = alpha * r - gamma * w1
            res_ref[c, x] = r - alpha * w1 + gamma * w2_ref[c, x]
        copies.append(pltpu.make_async_copy(x_ref.at[c], x_hbm.at[c], sem.at[0, c]))
        copies.append(pltpu.make_async_copy(res_ref.at[c], res_hbm.at[c], sem.at[1, c]))
        for copy in copies[-2:]:
            copy.start()
    for copy in copies:
        copy.wait()


def exchange(xe, xo, ye, yo):
    def pairs(axis, start):
        count = lax.axis_size(axis)
        chosen = []
        for i in range(count):
            partner = i + 1 if (i - start) % 2 == 0 else i - 1
            chosen.append((i, partner if 0 <= partner < count else i))
        return chosen

    return (
        lax.ppermute(xe, "body", pairs("body", 0)),
        lax.ppermute(xo, "body", pairs("body", 1)),
        lax.ppermute(ye, "across", pairs("across", 0)),
        lax.ppermute(yo, "across", pairs("across", 1)),
    )


def on_device(
    cotangent, shear, lame, inertia, surface_points, point_counts, surface_maps, contact_pairs
):
    rows, cols, depth = shear.shape
    points = jnp.transpose(surface_points[0, 0], (1, 0, 2))
    counts = point_counts[0, 0]
    cell_maps = surface_maps[0, 0]
    pair_table = contact_pairs[0, 0][:, None, :]
    _, blocks, width = points.shape
    pairs = pair_table.shape[2]
    bodies, acrosses = lax.axis_size("body"), lax.axis_size("across")
    devices = bodies * acrosses
    cap = pairs // bodies
    slots = cap + blocks // 2
    chunks = blocks // 2
    cell_maps = cell_maps.reshape(chunks, 1, 2 * width)
    flat = rows * cols
    vector = sds((3, rows, cols, depth))

    def faces(count):
        return (
            sds((count, cols, depth)), sds((count, cols, depth)),
            sds((count, rows, depth)), sds((count, rows, depth)),
        )

    moves = sds((blocks, 4, width))
    both = pltpu.VMEM((3 * flat, 2 * depth), BF16)
    wide = 2 * blocks * width
    sides = (pltpu.VMEM((3 * flat, wide), BF16), pltpu.VMEM((depth, wide), BF16))
    total = pltpu.VMEM((blocks, 4, width), F32)
    kept = (bodies, 2 * cap, width, 2 * width)
    kept_mib = 10 + (8 * pairs * width * width >> 20) + (bodies >> 2)
    dma = pltpu.SemaphoreType.DMA
    cells = (sds((rows, cols, depth)),) * 3

    r, shear, lame, inertia, cell_maps, xe, xo, ye, yo, own, first_moves, message, table = call(
        open_kernel, "open", [HBM] * 8, [VMEM] * 12 + [SMEM],
        (vector,) + cells + (sds(cell_maps.shape, I32),) + faces(5)
        + (moves, moves, sds((bodies, slots, 8, width)), sds((2, pairs), I32)),
        scratch=(
            pltpu.VMEM(points.shape, F32), pltpu.SMEM(counts.shape, I32),
            pltpu.SMEM(pair_table.shape, I32), pltpu.SMEM((bodies,), I32),
            pltpu.VMEM((blocks, 8, width), F32), both, dma((10,)),
        ), cost=4.0,
    )(*in_hbm(cotangent, shear, lame, inertia, points, counts, pair_table, cell_maps))
    got = lax.all_to_all(message, "body", 0, 0, tiled=True)
    halo = exchange(xe, xo, ye, yo)
    grown = sds((blocks + 1, 4, width))
    elastic_one, next_moves = call(
        stencil_one_kernel, "stencil_one", [VMEM] * 9, [VMEM] * 2, (vector, grown),
        scratch=(both,), cost=5.0,
    )(r, shear, lame, inertia, *halo, cell_maps)
    force_one, second_moves, message, targets, weights = call(
        forces_one_kernel, "forces_one", [VMEM] * 2 + [SMEM] + [VMEM] * 2,
        [VMEM] * 3 + [SMEM, HBM],
        (moves, grown, sds((bodies, 2 * cap, 4, width)), sds((pairs,), I32), pltpu.HBM(kept, BF16)),
        scratch=(pltpu.VMEM(kept, BF16), total, dma((bodies,))), cost=6.0, mib=kept_mib,
    )(got, own, table, first_moves, next_moves)
    got = lax.all_to_all(message, "body", 0, 0, tiled=True)
    w1, xe, xo, ye, yo = call(
        scatter_one_kernel, "scatter_one", [VMEM] * 3, [VMEM] * 5, (vector,) + faces(3),
        scratch=sides, cost=3.0, mib=16,
    )(elastic_one, force_one, cell_maps)
    halo_two = exchange(xe, xo, ye, yo)
    elastic_two, force_two, partial = call(
        apply_two_kernel, "apply_two", [VMEM] * 13 + [SMEM] * 2 + [VMEM, HBM], [VMEM] * 3,
        (vector, moves, sds((devices, 4, 128))),
        scratch=(pltpu.VMEM(kept, BF16), total, dma((bodies,))), cost=2.0, mib=kept_mib,
    )(w1, shear, lame, inertia, *halo_two, *halo, got, targets, table, second_moves, *in_hbm(weights))
    sums = lax.all_to_all(partial, ("body", "across"), 0, 0, tiled=True)
    w2, r = call(
        scatter_two_kernel, "scatter_two", [VMEM] * 3 + [HBM], [VMEM] * 2, (vector, vector),
        scratch=sides + (dma(()),), cost=3.0, mib=16,
    )(elastic_two, force_two, cell_maps, *in_hbm(cotangent))
    out = pltpu.VMEM((3, rows, cols, depth), F32)
    return call(
        final_kernel, "final", [VMEM] * 4, [HBM] * 2, (vector, vector),
        scratch=(out, out, dma((2, 3))), cost=1.0,
    )(r, w1, w2, sums)


def solution(mesh):
    placed = (
        P(None, "body", "across", None),
        P("body", "across", None),
        P("body", "across", None),
        P("body", "across", None),
        P("body", "across", None, None, None),
        P("body", "across", None),
        P("body", "across", None, None),
        P("body", "across", None, None),
    )
    return jax.shard_map(
        on_device,
        mesh=mesh,
        in_specs=placed,
        out_specs=(P(None, "body", "across", None), P(None, "body", "across", None)),
        check_vma=False,
    )
```

```python
import jax
import jax.numpy as jnp
from jax import lax
from jax.experimental import pallas as pl
from jax.experimental.pallas import tpu as pltpu
from jax.sharding import PartitionSpec as P

F32 = jnp.float32
BF16 = jnp.bfloat16
I32 = jnp.int32

barrier_reach = 1.0
barrier_scale = 0.005
FAR = 1000.0

VMEM = pl.BlockSpec(memory_space=pltpu.VMEM)
SMEM = pl.BlockSpec(memory_space=pltpu.SMEM)
HBM = pl.BlockSpec(memory_space=pltpu.HBM)


def sds(shape, dtype=F32):
    return jax.ShapeDtypeStruct(shape, dtype)


def call(body, name, in_specs, out_specs, out_shape, scratch=(), cost=2.0, mib=8):
    estimate = pl.CostEstimate(flops=int(cost * 1e8), transcendentals=0, bytes_accessed=int(cost * 3e6))
    return pl.pallas_call(
        body,
        name=name,
        in_specs=in_specs,
        out_specs=out_specs,
        out_shape=out_shape,
        scratch_shapes=list(scratch),
        cost_estimate=estimate,
        compiler_params=pltpu.CompilerParams(vmem_limit_bytes=mib << 20),
    )


def in_hbm(*arrays):
    return tuple(pltpu.with_memory_space_constraint(array, pltpu.HBM) for array in arrays)


def split(values):
    high = values.astype(BF16)
    low = (values - high.astype(F32)).astype(BF16)
    return high, low


def even_faces(block, axis_parity, last):
    first = jnp.where(axis_parity == 0, last, 0)
    return first, last - first


def write_faces(sources, xe_ref, xo_ref, ye_ref, yo_ref):
    bpar = lax.rem(lax.axis_index("body"), 2)
    apar = lax.rem(lax.axis_index("across"), 2)
    for k, (ref, lead) in enumerate(sources):
        at = (lambda x: ref[lead, x]) if lead is not None else (lambda x: ref[x])
        rows = ref.shape[-3]
        cols = ref.shape[-2]
        xi = jnp.where(bpar == 0, rows - 1, 0)
        xe_ref[k] = at(xi)
        xo_ref[k] = at(rows - 1 - xi)
        for x in range(rows):
            slab = at(x)
            low = slab[0:1]
            high = slab[cols - 1 : cols]
            ye_ref[k, x : x + 1] = jnp.where(apar == 0, high, low)
            yo_ref[k, x : x + 1] = jnp.where(apar == 0, low, high)


def cell_parts(cells, depth):
    if depth & (depth - 1) == 0:
        shift = depth.bit_length() - 1
        return lax.shift_right_logical(cells, shift), jnp.bitwise_and(cells, depth - 1)
    row = cells // depth
    return row, cells - row * depth


def gather_into(load, rows, depth, map_ref, both_ref, write):
    for c in range(3):
        high, low = split(load(c))
        both_ref[c * rows : (c + 1) * rows, 0:depth] = high
        both_ref[c * rows : (c + 1) * rows, depth:] = low
    chunks, _, span = map_ref.shape
    depth_iota = lax.broadcasted_iota(I32, (depth, span), 0)
    row_iota = lax.broadcasted_iota(I32, (rows, span), 0)

    def chunk(j, carry):
        row, deep = cell_parts(map_ref[j], depth)
        onehot = jnp.where(depth_iota == deep, 1.0, 0.0).astype(BF16)
        onehot = jnp.concatenate([onehot, onehot], axis=0)
        picked = jnp.dot(both_ref[...], onehot, preferred_element_type=F32)
        here = row_iota == row
        for c in range(3):
            part = jnp.where(here, picked[c * rows : (c + 1) * rows], 0.0)
            write(j, c, jnp.sum(part, axis=0, keepdims=True))
        return carry

    lax.fori_loop(0, chunks, chunk, 0)


def open_kernel(
    r_hbm, sh_hbm, la_hbm, in_hbm, pt_hbm, cnt_hbm, pair_hbm, map_hbm,
    r_ref, sh_ref, la_ref, in_ref, map_ref,
    xe_ref, xo_ref, ye_ref, yo_ref, own_ref, move_ref, msg_ref, table_ref,
    pt_ref, cnt_ref, pair_ref, fill_ref, sent_ref, both_ref, sem,
):
    copies = [
        pltpu.make_async_copy(source, target, sem.at[k])
        for k, (source, target) in enumerate([
            (cnt_hbm, cnt_ref), (pair_hbm, pair_ref), (pt_hbm, pt_ref), (map_hbm, map_ref),
            (r_hbm.at[0], r_ref.at[0]), (r_hbm.at[1], r_ref.at[1]), (r_hbm.at[2], r_ref.at[2]),
            (sh_hbm, sh_ref), (la_hbm, la_ref), (in_hbm, in_ref),
        ])
    ]
    for copy in copies:
        copy.start()
    bodies, width = msg_ref.shape[0], msg_ref.shape[1]
    blocks = own_ref.shape[0]
    odd_total = blocks // 2
    cap = width - odd_total
    pairs = table_ref.shape[1]
    points = own_ref.shape[2]
    lane = lax.broadcasted_iota(I32, (1, points), 1)
    row = lax.broadcasted_iota(I32, (8, points), 0)
    edge = lax.broadcasted_iota(I32, (4, points), 0) == 3
    for copy in copies[:4]:
        copy.wait()
    for d in range(bodies):
        fill_ref[d] = 0

    def place(n, carry):
        dest = pair_ref[1, 0, n]
        rank = fill_ref[dest]
        fill_ref[dest] = rank + 1
        table_ref[0, dest * cap + rank] = pair_ref[0, 0, n]
        table_ref[1, dest * cap + rank] = pair_ref[2, 0, n]
        return carry

    lax.fori_loop(0, pairs, place, 0)
    blank = jnp.zeros((1, points), F32)
    for k in range(blocks):
        tile = jnp.concatenate([pt_ref[c, k : k + 1, :] for c in range(3)] + [blank], axis=0)
        own_ref[k] = target_rows(measured(jnp.where(lane < cnt_ref[k], tile, -FAR), edge))
        sent_ref[k, 4:8, :] = measured(jnp.where(lane < cnt_ref[k], tile, FAR), edge)
        sent_ref[k, 3:4, :] = blank
        move_ref[k, 3:4, :] = blank + 1.0
    for copy in copies[4:]:
        copy.wait()
    rows, depth = r_ref.shape[1] * r_ref.shape[2], r_ref.shape[3]

    def write(j, c, line):
        per = line.shape[1] // points
        for b in range(per):
            part = line[:, b * points : (b + 1) * points]
            move_ref[j * per + b, c : c + 1, :] = part
            sent_ref[j * per + b, c : c + 1, :] = part

    gather_into(lambda c: r_ref[c].reshape(rows, depth), rows, depth, map_ref, both_ref, write)

    def pack(d, carry):
        for s in range(cap):
            second = table_ref[1, d * cap + s].astype(F32)
            msg_ref[d, s] = jnp.where(row == 3, second, sent_ref[table_ref[0, d * cap + s]])
        for j in range(odd_total):
            msg_ref[d, cap + j] = sent_ref[2 * j + 1]
        return carry

    lax.fori_loop(0, bodies, pack, 0)
    sources = [(r_ref, 0), (r_ref, 1), (r_ref, 2), (sh_ref, None), (la_ref, None)]
    write_faces(sources, xe_ref, xo_ref, ye_ref, yo_ref)


def measured(tile, edge):
    square = jnp.where(edge, 0.0, tile * tile)
    return jnp.where(edge, jnp.sum(square, axis=0, keepdims=True), tile)


def three_parts(value):
    high = value.astype(BF16).astype(F32)
    rest = value - high
    middle = rest.astype(BF16).astype(F32)
    return high, middle, rest - middle


def source_rows(tile):
    row = lax.broadcasted_iota(I32, (8, tile.shape[1]), 0)
    high, middle, low = three_parts(jnp.concatenate([tile, tile], axis=0))
    first = jnp.where(row == 7, middle, high)
    second = jnp.where(row == 3, low, jnp.where(row < 3, middle, high))
    second = jnp.where(row == 7, 1.0, second)
    third = jnp.where(row < 3, low, middle)
    third = jnp.where((row == 3) | (row == 7), 1.0, third)
    return jnp.concatenate([first, second, third, jnp.zeros_like(first)], axis=0).astype(BF16)


def target_rows(tile):
    row = lax.broadcasted_iota(I32, (8, tile.shape[1]), 0)
    high, middle, low = three_parts(jnp.concatenate([tile, tile], axis=0))
    first = -2.0 * jnp.where(row < 4, high, middle)
    first = jnp.where((row == 3) | (row == 7), 1.0, first)
    second = -2.0 * jnp.where(row < 4, high, low)
    second = jnp.where(row == 3, 1.0, jnp.where(row == 7, high, second))
    third = -2.0 * jnp.where(row < 4, high, middle)
    third = jnp.where(row == 3, middle, jnp.where(row == 7, low, third))
    return jnp.concatenate([first, second, third, jnp.zeros_like(first)], axis=0).astype(BF16)


def weigh(tile, target):
    squared = lax.dot_general(
        source_rows(tile[4:8]), target, (((0,), (0,)), ((), ())), preferred_element_type=F32
    )
    q = 1.0 - 1.0 / squared
    weight = barrier_scale * (-2.0 * jnp.log(squared) - 4.0 * q + q * q)
    return jnp.where(squared < barrier_reach, weight, 0.0)


def pair_part(moves, weights):
    points = moves.shape[1]
    high = moves.astype(BF16).astype(F32)
    lhs = jnp.concatenate([high, moves - high], axis=0).astype(BF16)
    out = jnp.dot(lhs, weights, preferred_element_type=F32)
    return (out[0:4, :points] + out[4:8, :points]) + (out[0:4, points:] + out[4:8, points:])


def forces_one_kernel(
    got_ref, own_ref, table_ref, move_ref, next_ref,
    force_ref, sum_ref, msg_ref, target_ref, w_hbm, w_ref, acc_ref, sem,
):
    bodies, width = got_ref.shape[0], got_ref.shape[1]
    blocks, _, points = move_ref.shape
    cap = width - blocks // 2
    acc_ref[...] = jnp.zeros_like(acc_ref)

    edge = lax.broadcasted_iota(I32, (4, points), 0) == 3

    def keep(d):
        return pltpu.make_async_copy(w_ref.at[d], w_hbm.at[d], sem.at[d])

    def find(d, carry):
        for s in range(cap):
            target_ref[d * cap + s] = jnp.max(got_ref[d, s, 3:4, :]).astype(I32)
        return carry

    lax.fori_loop(0, bodies, find, 0, unroll=8)

    def device(d, carry):
        work = []
        for s in range(cap):
            n = d * cap + s
            work.append((got_ref[d, s], target_ref[n]))
            first = table_ref[0, n]
            odd = lax.shift_right_logical(table_ref[1, n], 1)
            work.append((got_ref[d, cap + odd], first))
        parts = []
        for k, (tile, at) in enumerate(work):
            high, low = split(weigh(tile, own_ref[at]))
            both = jnp.concatenate([high, low], axis=1)
            w_ref[d, k] = both
            parts.append(pair_part(jnp.where(edge, 1.0, tile[0:4]), both))
        for (_, at), part in zip(work, parts):
            acc_ref[at] = acc_ref[at] + part
        keep(d).start()
        return carry

    lax.fori_loop(0, bodies, device, 0)
    row = lax.broadcasted_iota(I32, (4, points), 0)
    inner = jnp.zeros((4, points), F32)
    for k in range(blocks):
        acc = acc_ref[k]
        force = move_ref[k] * acc[3:4] - acc
        force_ref[k] = force
        sum_ref[k] = jnp.where(row < 3, next_ref[k] + force, 1.0)
        inner = inner + move_ref[k] * force
    inner = jnp.sum(inner[0:3], axis=0, keepdims=True)
    sum_ref[blocks] = next_ref[blocks] + jnp.where(row == 1, inner, 0.0)

    def pack(d, carry):
        for s in range(cap):
            n = d * cap + s
            msg_ref[d, s] = sum_ref[table_ref[0, n]]
            msg_ref[d, cap + s] = sum_ref[target_ref[n]]
        return carry

    lax.fori_loop(0, bodies, pack, 0)

    def finish(d, carry):
        keep(d).wait()
        return carry

    lax.fori_loop(0, bodies, finish, 0)


def scatter_sum(base, rows, depth, map_ref, force_ref, left_ref, right_ref):
    span = map_ref.shape[2]
    per = force_ref.shape[0] // map_ref.shape[0]
    depth_iota = lax.broadcasted_iota(I32, (depth, span), 0)
    row_iota = lax.broadcasted_iota(I32, (rows, span), 0)
    chunks = map_ref.shape[0]
    for j in range(chunks):
        row, deep = cell_parts(map_ref[j], depth)
        onehot = jnp.where(depth_iota == deep, 1.0, 0.0).astype(BF16)
        right_ref[:, j * span : (j + 1) * span] = onehot
        right_ref[:, (chunks + j) * span : (chunks + j + 1) * span] = onehot
        here = row_iota == row
        for c in range(3):
            line = jnp.concatenate(
                [force_ref[j * per + b, c : c + 1, :] for b in range(per)], axis=1
            )
            high = line.astype(BF16).astype(F32)
            at = slice(c * rows, (c + 1) * rows)
            left_ref[at, j * span : (j + 1) * span] = jnp.where(here, high, 0.0).astype(BF16)
            left_ref[at, (chunks + j) * span : (chunks + j + 1) * span] = jnp.where(
                here, line - high, 0.0
            ).astype(BF16)
    spread = lax.dot_general(
        left_ref[...], right_ref[...], (((1,), (1,)), ((), ())), preferred_element_type=F32
    )
    return [base(c) + spread[c * rows : (c + 1) * rows] for c in range(3)]


def scatter_one_kernel(
    e_hbm, force_ref, map_ref, w1_ref, xe_ref, xo_ref, ye_ref, yo_ref, e_ref, left_ref, right_ref, sem
):
    copy = pltpu.make_async_copy(e_hbm, e_ref, sem)
    copy.start()
    shape = e_ref.shape[1:]
    rows, depth = shape[0] * shape[1], shape[2]

    def base(c):
        if c == 0:
            copy.wait()
        return e_ref[c].reshape(rows, depth)

    sums = scatter_sum(base, rows, depth, map_ref, force_ref, left_ref, right_ref)
    for c in range(3):
        w1_ref[c] = sums[c].reshape(shape)
    write_faces([(w1_ref, 0), (w1_ref, 1), (w1_ref, 2)], xe_ref, xo_ref, ye_ref, yo_ref)


def scatter_two_kernel(
    e_ref, force_ref, map_ref, r_hbm, w2_ref, r_ref, left_ref, right_ref, sem
):
    copy = pltpu.make_async_copy(r_hbm, r_ref, sem)
    copy.start()
    shape = e_ref.shape[1:]
    rows, depth = shape[0] * shape[1], shape[2]
    sums = scatter_sum(
        lambda c: e_ref[c].reshape(rows, depth), rows, depth, map_ref, force_ref, left_ref, right_ref
    )
    for c in range(3):
        w2_ref[c] = sums[c].reshape(shape)
    copy.wait()


def elastic(v_ref, sh_ref, la_ref, in_ref, vector_halo, stiff_halo, emit):
    rows, cols, depth = sh_ref.shape
    b, a = lax.axis_index("body"), lax.axis_index("across")
    bodies, acrosses = lax.axis_size("body"), lax.axis_size("across")
    bpar, apar = lax.rem(b, 2), lax.rem(a, 2)
    cut = bodies // 4
    x_low = jnp.where(b != 0, 1.0, 0.0).astype(F32)
    x_high = jnp.where(b != bodies - 1, 1.0, 0.0).astype(F32)
    keep_low = jnp.where(b != cut, 1.0, 0.0).astype(F32)
    keep_high = jnp.where(b + 1 != cut, 1.0, 0.0).astype(F32)
    y_low = jnp.where(a != 0, 1.0, 0.0).astype(F32)
    y_high = jnp.where(a != acrosses - 1, 1.0, 0.0).astype(F32)
    vxe, vxo, vye, vyo = vector_halo
    sxe, sxo, sye, syo = stiff_halo
    row = lax.broadcasted_iota(I32, (cols, depth), 0)
    lane = lax.broadcasted_iota(I32, (cols, depth), 1)
    z_mask = jnp.where(lane == depth - 1, 0.0, 1.0)
    start = lane == 0
    top = row == cols - 1
    bottom = row == 0

    def stiffness(shear, lame):
        return 0.5 * shear, shear + 0.5 * lame

    def pick(parity, even, odd):
        return jnp.where(parity == 0, even, odd)

    def x_halo(high):
        e, o = (sxe, sxo) if high else (sxo, sxe)
        there = x_high if high else x_low
        shear, lame = pick(bpar, e[3], o[3]), pick(bpar, e[4], o[4])
        e, o = (vxe, vxo) if high else (vxo, vxe)
        values = [there * pick(bpar, e[c], o[c]) for c in range(3)]
        return stiffness(there * shear, there * lame), values

    def y_halo(high, x):
        e, o = (sye, syo) if high else (syo, sye)
        there = y_high if high else y_low
        at = slice(x, x + 1)
        shear, lame = pick(apar, e[3, at], o[3, at]), pick(apar, e[4, at], o[4, at])
        e, o = (vye, vyo) if high else (vyo, vye)
        values = [there * pick(apar, e[c, at], o[c, at]) for c in range(3)]
        return stiffness(there * shear, there * lame), values

    def slab(x):
        return stiffness(sh_ref[x], la_ref[x]), [v_ref[c, x] for c in range(3)]

    def flux(near, far, along, mask):
        (off, diag), values = near
        (far_off, far_diag), far_values = far
        side, front = off + far_off, diag + far_diag
        if mask is not None:
            side, front = side * mask, front * mask
        return [
            (front if c == along else side) * (values[c] - far_values[c]) for c in range(3)
        ]

    before = flux(x_halo(False), slab(0), 0, keep_low)
    here = slab(0)
    for x in range(rows):
        after = slab(x + 1) if x + 1 < rows else x_halo(True)
        out = flux(here, after, 0, None if x + 1 < rows else keep_high)
        (off, diag), values = here
        inertia = in_ref[x]
        total = [inertia * values[c] + (out[c] - before[c]) for c in range(3)]
        before = out

        def up(value, edge):
            return jnp.where(top, edge, pltpu.roll(value, cols - 1, 0))

        (h_off, h_diag), h_values = y_halo(True, x)
        shifted = (up(off, h_off), up(diag, h_diag)), [up(values[c], h_values[c]) for c in range(3)]
        out = flux(here, shifted, 1, None)
        first = (off[0:1], diag[0:1]), [values[c][0:1] for c in range(3)]
        edge = flux(y_halo(False, x), first, 1, None)
        total = [
            total[c] + (out[c] - jnp.where(bottom, edge[c], pltpu.roll(out[c], 1, 0)))
            for c in range(3)
        ]

        def right(value):
            return z_mask * pltpu.roll(value, depth - 1, 1)

        shifted = (right(off), right(diag)), [right(values[c]) for c in range(3)]
        out = flux(here, shifted, 2, None)
        edge = [-(diag if c == 2 else off) * values[c] for c in range(3)]
        total = [
            total[c] + (out[c] - jnp.where(start, edge[c], pltpu.roll(out[c], 1, 1)))
            for c in range(3)
        ]
        emit(x, total)
        here = after


def stencil_one_kernel(
    r_ref, sh_ref, la_ref, in_ref, xe, xo, ye, yo, map_ref,
    e_hbm, next_ref, e_ref, both_ref, sem,
):
    sums = [jnp.zeros((8, 128), F32) for _ in range(2)]

    def emit(x, total):
        for c in range(3):
            e_ref[c, x] = total[c]
            r = r_ref[c, x]
            sums[0] = sums[0] + fold(r * r)
            sums[1] = sums[1] + fold(r * total[c])

    elastic(r_ref, sh_ref, la_ref, in_ref, (xe, xo, ye, yo), (xe, xo, ye, yo), emit)
    copy = pltpu.make_async_copy(e_ref, e_hbm, sem)
    copy.start()
    rows, depth = e_ref.shape[1] * e_ref.shape[2], e_ref.shape[3]
    points = next_ref.shape[2]

    def write(j, c, line):
        per = line.shape[1] // points
        for b in range(per):
            next_ref[j * per + b, c : c + 1, :] = line[:, b * points : (b + 1) * points]

    blocks = next_ref.shape[0] - 1
    for k in range(blocks):
        next_ref[k, 3:4, :] = jnp.zeros((1, points), F32)
    lines = [jnp.sum(value, axis=0, keepdims=True) for value in sums]
    next_ref[blocks] = jnp.concatenate(lines + [jnp.zeros((2, points), F32)], axis=0)
    gather_into(lambda c: e_ref[c].reshape(rows, depth), rows, depth, map_ref, both_ref, write)
    copy.wait()


def fold(value):
    cols, depth = value.shape
    total = None
    for k in range(depth // 128):
        part = value[:, k * 128 : (k + 1) * 128]
        part = jnp.sum(part.reshape(cols // 8, 8, 128), axis=0)
        total = part if total is None else total + part
    return total


def forces_two_kernel(
    got_ref, target_ref, table_ref, move_ref, w_hbm, force_ref, dots_ref, w_ref, acc_ref, sem
):
    bodies, width = got_ref.shape[0], got_ref.shape[1]
    cap = width // 2
    blocks, points = move_ref.shape[0] - 1, move_ref.shape[2]

    def fetch(d):
        return pltpu.make_async_copy(w_hbm.at[d], w_ref.at[d], sem.at[d])

    def begin(d, carry):
        fetch(d).start()
        return carry

    lax.fori_loop(0, bodies, begin, 0)
    acc_ref[...] = jnp.zeros_like(acc_ref)

    def device(d, carry):
        fetch(d).wait()
        work = []
        for s in range(cap):
            n = d * cap + s
            work.append((target_ref[n], pair_part(got_ref[d, s], w_ref[d, 2 * s])))
            work.append((table_ref[0, n], pair_part(got_ref[d, cap + s], w_ref[d, 2 * s + 1])))
        for at, part in work:
            acc_ref[at] = acc_ref[at] + part
        return carry

    lax.fori_loop(0, bodies, device, 0)
    inner = jnp.zeros((4, points), F32)
    for k in range(blocks):
        acc = acc_ref[k]
        moved = move_ref[k]
        force = moved * acc[3:4] - acc
        force_ref[k] = force
        inner = inner + moved * force
    inner = jnp.sum(inner[0:3], axis=0, keepdims=True)
    blank = jnp.zeros_like(inner)
    dots_ref[...] = jnp.concatenate([move_ref[blocks][0:2], blank, inner], axis=0)


def stencil_two_kernel(
    w1_ref, sh_ref, la_ref, in_ref, xe, xo, ye, yo, cxe, cxo, cye, cyo, dots_ref, e_ref, red_ref
):
    sums = [jnp.zeros((8, 128), F32) for _ in range(2)]

    def emit(x, total):
        for c in range(3):
            e_ref[c, x] = total[c]
            w = w1_ref[c, x]
            sums[0] = sums[0] + fold(w * w)
            sums[1] = sums[1] + fold(w * total[c])

    elastic(w1_ref, sh_ref, la_ref, in_ref, (xe, xo, ye, yo), (cxe, cxo, cye, cyo), emit)
    lines = [jnp.sum(value, axis=0, keepdims=True) for value in sums]
    blank = jnp.zeros_like(lines[0])
    line = dots_ref[...] + jnp.concatenate([blank, blank] + lines, axis=0)
    for d in range(red_ref.shape[0]):
        red_ref[d] = line


def final_kernel(r_ref, w1_ref, w2_ref, red_ref, x_hbm, res_hbm, x_ref, res_ref, sem):
    line = jnp.sum(red_ref[...], axis=0)
    moment = [
        jnp.broadcast_to(jnp.sum(line[k : k + 1], axis=1, keepdims=True), (8, 128)) for k in range(4)
    ]
    m0, m1, m2, m3 = moment
    step = m0 / m1
    norm = (m0 - step * m1) + step * (step * m2 - m1)
    ratio = norm / m0
    grown = 1.0 + ratio
    curve = grown * (grown * m1 - 2.0 * step * m2) + step * step * m3
    next_step = norm / curve
    alpha = step + next_step * grown
    gamma = next_step * step
    cols, depth = r_ref.shape[2], r_ref.shape[3]
    alpha = jnp.broadcast_to(alpha[0:1, 0:1], (cols, depth))
    gamma = jnp.broadcast_to(gamma[0:1, 0:1], (cols, depth))
    copies = []
    for c in range(3):
        for x in range(r_ref.shape[1]):
            r, w1 = r_ref[c, x], w1_ref[c, x]
            x_ref[c, x] = alpha * r - gamma * w1
            res_ref[c, x] = r - alpha * w1 + gamma * w2_ref[c, x]
        copies.append(pltpu.make_async_copy(x_ref.at[c], x_hbm.at[c], sem.at[0, c]))
        copies.append(pltpu.make_async_copy(res_ref.at[c], res_hbm.at[c], sem.at[1, c]))
        for copy in copies[-2:]:
            copy.start()
    for copy in copies:
        copy.wait()


def exchange(xe, xo, ye, yo):
    def pairs(axis, start):
        count = lax.axis_size(axis)
        chosen = []
        for i in range(count):
            partner = i + 1 if (i - start) % 2 == 0 else i - 1
            chosen.append((i, partner % count))
        return chosen

    got_xo = lax.ppermute(xo, "body", pairs("body", 1))
    got_xe = lax.ppermute(xe, "body", pairs("body", 0))
    got_yo = lax.ppermute(yo, "across", pairs("across", 1))
    got_ye = lax.ppermute(ye, "across", pairs("across", 0))
    return (
        got_xe, got_xo, got_ye, got_yo
    )


def on_device(
    cotangent, shear, lame, inertia, surface_points, point_counts, surface_maps, contact_pairs
):
    rows, cols, depth = shear.shape
    points = jnp.transpose(surface_points[0, 0], (1, 0, 2))
    counts = point_counts[0, 0]
    cell_maps = surface_maps[0, 0]
    pair_table = contact_pairs[0, 0][:, None, :]
    _, blocks, width = points.shape
    pairs = pair_table.shape[2]
    bodies, acrosses = lax.axis_size("body"), lax.axis_size("across")
    devices = bodies * acrosses
    cap = pairs // bodies
    slots = cap + blocks // 2
    chunks = blocks // 2
    cell_maps = cell_maps.reshape(chunks, 1, 2 * width)
    flat = rows * cols
    vector = sds((3, rows, cols, depth))

    def faces(count):
        return (
            sds((count, cols, depth)), sds((count, cols, depth)),
            sds((count, rows, depth)), sds((count, rows, depth)),
        )

    moves = sds((blocks, 4, width))
    both = pltpu.VMEM((3 * flat, 2 * depth), BF16)
    wide = 2 * blocks * width
    sides = (pltpu.VMEM((3 * flat, wide), BF16), pltpu.VMEM((depth, wide), BF16))
    total = pltpu.VMEM((blocks, 4, width), F32)
    kept = (bodies, 2 * cap, width, 2 * width)
    kept_mib = 10 + (8 * pairs * width * width >> 20) + (bodies >> 2)
    dma = pltpu.SemaphoreType.DMA
    cells = (sds((rows, cols, depth)),) * 3

    r, shear, lame, inertia, cell_maps, xe, xo, ye, yo, own, first_moves, message, table = call(
        open_kernel, "open", [HBM] * 8, [VMEM] * 12 + [SMEM],
        (vector,) + cells + (sds(cell_maps.shape, I32),) + faces(5)
        + (sds((blocks, 32, width), BF16), moves)
        + (sds((bodies, slots, 8, width)), sds((2, pairs), I32)),
        scratch=(
            pltpu.VMEM(points.shape, F32), pltpu.SMEM(counts.shape, I32),
            pltpu.SMEM(pair_table.shape, I32), pltpu.SMEM((bodies,), I32),
            pltpu.VMEM((blocks, 8, width), F32), both, dma((10,)),
        ), cost=4.0,
    )(*in_hbm(cotangent, shear, lame, inertia, points, counts, pair_table, cell_maps))
    got = lax.all_to_all(message, "body", 0, 0, tiled=True)
    halo = exchange(xe, xo, ye, yo)
    grown = sds((blocks + 1, 4, width))
    elastic_one, next_moves = call(
        stencil_one_kernel, "stencil_one", [VMEM] * 9, [HBM, VMEM],
        (pltpu.HBM((3, rows, cols, depth), F32), grown),
        scratch=(pltpu.VMEM((3, rows, cols, depth), F32), both, dma(())), cost=5.0,
    )(r, shear, lame, inertia, *halo, cell_maps)
    force_one, second_moves, message, targets, weights = call(
        forces_one_kernel, "forces_one", [VMEM] * 2 + [SMEM] + [VMEM] * 2,
        [VMEM] * 3 + [SMEM, HBM],
        (moves, grown, sds((bodies, 2 * cap, 4, width)), sds((pairs,), I32), pltpu.HBM(kept, BF16)),
        scratch=(pltpu.VMEM(kept, BF16), total, dma((bodies,))), cost=6.0, mib=kept_mib,
    )(got, own, table, first_moves, next_moves)
    got = lax.all_to_all(message, "body", 0, 0, tiled=True)
    w1, xe, xo, ye, yo = call(
        scatter_one_kernel, "scatter_one", [HBM] + [VMEM] * 2, [VMEM] * 5, (vector,) + faces(3),
        scratch=(pltpu.VMEM((3, rows, cols, depth), F32),) + sides + (dma(()),), cost=3.0, mib=16,
    )(*in_hbm(elastic_one), force_one, cell_maps)
    halo_two = exchange(xe, xo, ye, yo)
    force_two, dots = call(
        forces_two_kernel, "forces_two", [VMEM] + [SMEM] * 2 + [VMEM, HBM], [VMEM] * 2,
        (moves, sds((4, 128))),
        scratch=(pltpu.VMEM(kept, BF16), total, dma((bodies,))), cost=3.0, mib=kept_mib,
    )(got, targets, table, second_moves, *in_hbm(weights))
    elastic_two, partial = call(
        stencil_two_kernel, "stencil_two", [VMEM] * 13, [VMEM] * 2, (vector, sds((devices, 4, 128))),
        cost=1.5,
    )(w1, shear, lame, inertia, *halo_two, *halo, dots)
    sums = lax.all_to_all(partial, ("body", "across"), 0, 0, tiled=True)
    w2, r = call(
        scatter_two_kernel, "scatter_two", [VMEM] * 3 + [HBM], [VMEM] * 2, (vector, vector),
        scratch=sides + (dma(()),), cost=3.0, mib=16,
    )(elastic_two, force_two, cell_maps, *in_hbm(cotangent))
    out = pltpu.VMEM((3, rows, cols, depth), F32)
    return call(
        final_kernel, "final", [VMEM] * 4, [HBM] * 2, (vector, vector),
        scratch=(out, out, dma((2, 3))), cost=1.0,
    )(r, w1, w2, sums)


def solution(mesh):
    placed = (
        P(None, "body", "across", None),
        P("body", "across", None),
        P("body", "across", None),
        P("body", "across", None),
        P("body", "across", None, None, None),
        P("body", "across", None),
        P("body", "across", None, None),
        P("body", "across", None, None),
    )
    return jax.shard_map(
        on_device,
        mesh=mesh,
        in_specs=placed,
        out_specs=(P(None, "body", "across", None), P(None, "body", "across", None)),
        check_vma=False,
    )
```

```python
import jax
import jax.numpy as jnp
from jax import lax
from jax.experimental import pallas as pl
from jax.experimental.pallas import tpu as pltpu
from jax.sharding import PartitionSpec as P

F32 = jnp.float32
BF16 = jnp.bfloat16
I32 = jnp.int32

barrier_reach = 1.0
barrier_scale = 0.005
FAR = 1000.0

VMEM = pl.BlockSpec(memory_space=pltpu.VMEM)
SMEM = pl.BlockSpec(memory_space=pltpu.SMEM)
HBM = pl.BlockSpec(memory_space=pltpu.HBM)


def sds(shape, dtype=F32):
    return jax.ShapeDtypeStruct(shape, dtype)


def call(body, name, in_specs, out_specs, out_shape, scratch=(), cost=2.0, mib=8):
    estimate = pl.CostEstimate(flops=int(cost * 1e8), transcendentals=0, bytes_accessed=int(cost * 3e6))
    return pl.pallas_call(
        body,
        name=name,
        in_specs=in_specs,
        out_specs=out_specs,
        out_shape=out_shape,
        scratch_shapes=list(scratch),
        cost_estimate=estimate,
        compiler_params=pltpu.CompilerParams(vmem_limit_bytes=mib << 20),
    )


def in_hbm(*arrays):
    return tuple(pltpu.with_memory_space_constraint(array, pltpu.HBM) for array in arrays)


def split(values):
    high = values.astype(BF16)
    low = (values - high.astype(F32)).astype(BF16)
    return high, low


def even_faces(block, axis_parity, last):
    first = jnp.where(axis_parity == 0, last, 0)
    return first, last - first


def write_faces(sources, xe_ref, xo_ref, ye_ref, yo_ref):
    bpar = lax.rem(lax.axis_index("body"), 2)
    apar = lax.rem(lax.axis_index("across"), 2)
    for k, (ref, lead) in enumerate(sources):
        at = (lambda x: ref[lead, x]) if lead is not None else (lambda x: ref[x])
        rows = ref.shape[-3]
        cols = ref.shape[-2]
        xi = jnp.where(bpar == 0, rows - 1, 0)
        xe_ref[k] = at(xi)
        xo_ref[k] = at(rows - 1 - xi)
        for x in range(rows):
            slab = at(x)
            low = slab[0:1]
            high = slab[cols - 1 : cols]
            ye_ref[k, x : x + 1] = jnp.where(apar == 0, high, low)
            yo_ref[k, x : x + 1] = jnp.where(apar == 0, low, high)


def cell_parts(cells, depth):
    if depth & (depth - 1) == 0:
        shift = depth.bit_length() - 1
        return lax.shift_right_logical(cells, shift), jnp.bitwise_and(cells, depth - 1)
    row = cells // depth
    return row, cells - row * depth


def gather_into(load, rows, depth, map_ref, both_ref, write):
    for c in range(3):
        high, low = split(load(c))
        both_ref[c * rows : (c + 1) * rows, 0:depth] = high
        both_ref[c * rows : (c + 1) * rows, depth:] = low
    chunks, _, span = map_ref.shape
    depth_iota = lax.broadcasted_iota(I32, (depth, span), 0)
    row_iota = lax.broadcasted_iota(I32, (rows, span), 0)

    def chunk(j, carry):
        row, deep = cell_parts(map_ref[j], depth)
        onehot = jnp.where(depth_iota == deep, 1.0, 0.0).astype(BF16)
        onehot = jnp.concatenate([onehot, onehot], axis=0)
        picked = jnp.dot(both_ref[...], onehot, preferred_element_type=F32)
        here = row_iota == row
        for c in range(3):
            part = jnp.where(here, picked[c * rows : (c + 1) * rows], 0.0)
            write(j, c, jnp.sum(part, axis=0, keepdims=True))
        return carry

    lax.fori_loop(0, chunks, chunk, 0, unroll=8)


def open_kernel(
    r_hbm, sh_hbm, la_hbm, in_hbm, pt_hbm, cnt_hbm, pair_hbm, map_hbm,
    r_ref, sh_ref, la_ref, in_ref, map_ref,
    xe_ref, xo_ref, ye_ref, yo_ref, own_ref, move_ref, msg_ref, table_ref,
    pt_ref, cnt_ref, pair_ref, fill_ref, sent_ref, both_ref, sem,
):
    copies = [
        pltpu.make_async_copy(source, target, sem.at[k])
        for k, (source, target) in enumerate([
            (cnt_hbm, cnt_ref), (pair_hbm, pair_ref), (pt_hbm, pt_ref), (map_hbm, map_ref),
            (r_hbm.at[0], r_ref.at[0]), (r_hbm.at[1], r_ref.at[1]), (r_hbm.at[2], r_ref.at[2]),
            (sh_hbm, sh_ref), (la_hbm, la_ref), (in_hbm, in_ref),
        ])
    ]
    for copy in copies:
        copy.start()
    bodies, width = msg_ref.shape[0], msg_ref.shape[1]
    blocks = own_ref.shape[0]
    odd_total = blocks // 2
    cap = width - odd_total
    pairs = table_ref.shape[1]
    points = own_ref.shape[2]
    lane = lax.broadcasted_iota(I32, (1, points), 1)
    row = lax.broadcasted_iota(I32, (8, points), 0)
    edge = lax.broadcasted_iota(I32, (4, points), 0) == 3
    for copy in copies[:4]:
        copy.wait()
    for d in range(bodies):
        fill_ref[d] = 0

    def place(n, carry):
        dest = pair_ref[1, 0, n]
        rank = fill_ref[dest]
        fill_ref[dest] = rank + 1
        table_ref[0, dest * cap + rank] = pair_ref[0, 0, n]
        table_ref[1, dest * cap + rank] = pair_ref[2, 0, n]
        return carry

    lax.fori_loop(0, pairs, place, 0)
    blank = jnp.zeros((1, points), F32)
    for k in range(blocks):
        tile = jnp.concatenate([pt_ref[c, k : k + 1, :] for c in range(3)] + [blank], axis=0)
        own_ref[k] = target_rows(measured(jnp.where(lane < cnt_ref[k], tile, -FAR), edge))
        sent_ref[k, 4:8, :] = measured(jnp.where(lane < cnt_ref[k], tile, FAR), edge)
        sent_ref[k, 3:4, :] = blank
        move_ref[k, 3:4, :] = blank + 1.0
    for copy in copies[4:]:
        copy.wait()
    rows, depth = r_ref.shape[1] * r_ref.shape[2], r_ref.shape[3]

    def write(j, c, line):
        per = line.shape[1] // points
        for b in range(per):
            part = line[:, b * points : (b + 1) * points]
            move_ref[j * per + b, c : c + 1, :] = part
            sent_ref[j * per + b, c : c + 1, :] = part

    gather_into(lambda c: r_ref[c].reshape(rows, depth), rows, depth, map_ref, both_ref, write)

    def pack(d, carry):
        for s in range(cap):
            second = table_ref[1, d * cap + s].astype(F32)
            msg_ref[d, s] = jnp.where(row == 3, second, sent_ref[table_ref[0, d * cap + s]])
        for j in range(odd_total):
            msg_ref[d, cap + j] = sent_ref[2 * j + 1]
        return carry

    lax.fori_loop(0, bodies, pack, 0)
    sources = [(r_ref, 0), (r_ref, 1), (r_ref, 2), (sh_ref, None), (la_ref, None)]
    write_faces(sources, xe_ref, xo_ref, ye_ref, yo_ref)


def measured(tile, edge):
    square = jnp.where(edge, 0.0, tile * tile)
    return jnp.where(edge, jnp.sum(square, axis=0, keepdims=True), tile)


def three_parts(value):
    high = value.astype(BF16).astype(F32)
    rest = value - high
    middle = rest.astype(BF16).astype(F32)
    return high, middle, rest - middle


def source_rows(tile):
    row = lax.broadcasted_iota(I32, (8, tile.shape[1]), 0)
    high, middle, low = three_parts(jnp.concatenate([tile, tile], axis=0))
    first = jnp.where(row == 7, middle, high)
    second = jnp.where(row == 3, low, jnp.where(row < 3, middle, high))
    second = jnp.where(row == 7, 1.0, second)
    third = jnp.where(row < 3, low, middle)
    third = jnp.where((row == 3) | (row == 7), 1.0, third)
    return jnp.concatenate([first, second, third, jnp.zeros_like(first)], axis=0).astype(BF16)


def target_rows(tile):
    row = lax.broadcasted_iota(I32, (8, tile.shape[1]), 0)
    high, middle, low = three_parts(jnp.concatenate([tile, tile], axis=0))
    first = -2.0 * jnp.where(row < 4, high, middle)
    first = jnp.where((row == 3) | (row == 7), 1.0, first)
    second = -2.0 * jnp.where(row < 4, high, low)
    second = jnp.where(row == 3, 1.0, jnp.where(row == 7, high, second))
    third = -2.0 * jnp.where(row < 4, high, middle)
    third = jnp.where(row == 3, middle, jnp.where(row == 7, low, third))
    return jnp.concatenate([first, second, third, jnp.zeros_like(first)], axis=0).astype(BF16)


def weigh(tile, target):
    squared = lax.dot_general(
        source_rows(tile[4:8]), target, (((0,), (0,)), ((), ())), preferred_element_type=F32
    )
    q = 1.0 - 1.0 / squared
    weight = barrier_scale * (-2.0 * jnp.log(squared) - 4.0 * q + q * q)
    return jnp.where(squared < barrier_reach, weight, 0.0)


def pair_part(moves, weights):
    points = moves.shape[1]
    high = moves.astype(BF16).astype(F32)
    lhs = jnp.concatenate([high, moves - high], axis=0).astype(BF16)
    out = jnp.dot(lhs, weights, preferred_element_type=F32)
    return (out[0:4, :points] + out[4:8, :points]) + (out[0:4, points:] + out[4:8, points:])


def forces_one_kernel(
    got_ref, own_ref, table_ref, move_ref, next_ref,
    force_ref, sum_ref, msg_ref, target_ref, w_hbm, w_ref, acc_ref, sem,
):
    bodies, width = got_ref.shape[0], got_ref.shape[1]
    blocks, _, points = move_ref.shape
    cap = width - blocks // 2
    acc_ref[...] = jnp.zeros_like(acc_ref)

    edge = lax.broadcasted_iota(I32, (4, points), 0) == 3

    def keep(d):
        return pltpu.make_async_copy(w_ref.at[d], w_hbm.at[d], sem.at[d])

    def find(d, carry):
        for s in range(cap):
            target_ref[d * cap + s] = jnp.max(got_ref[d, s, 3:4, :]).astype(I32)
        return carry

    lax.fori_loop(0, bodies, find, 0, unroll=8)

    def device(d, carry):
        work = []
        for s in range(cap):
            n = d * cap + s
            work.append((got_ref[d, s], target_ref[n]))
            first = table_ref[0, n]
            odd = lax.shift_right_logical(table_ref[1, n], 1)
            work.append((got_ref[d, cap + odd], first))
        parts = []
        for k, (tile, at) in enumerate(work):
            high, low = split(weigh(tile, own_ref[at]))
            both = jnp.concatenate([high, low], axis=1)
            w_ref[d, k] = both
            parts.append(pair_part(jnp.where(edge, 1.0, tile[0:4]), both))
        for (_, at), part in zip(work, parts):
            acc_ref[at] = acc_ref[at] + part
        keep(d).start()
        return carry

    lax.fori_loop(0, bodies, device, 0, unroll=4)
    row = lax.broadcasted_iota(I32, (4, points), 0)
    inner = jnp.zeros((4, points), F32)
    for k in range(blocks):
        acc = acc_ref[k]
        force = move_ref[k] * acc[3:4] - acc
        force_ref[k] = force
        sum_ref[k] = jnp.where(row < 3, next_ref[k] + force, 1.0)
        inner = inner + move_ref[k] * force
    inner = jnp.sum(inner[0:3], axis=0, keepdims=True)
    sum_ref[blocks] = next_ref[blocks] + jnp.where(row == 1, inner, 0.0)

    def pack(d, carry):
        for s in range(cap):
            n = d * cap + s
            msg_ref[d, s] = sum_ref[table_ref[0, n]]
            msg_ref[d, cap + s] = sum_ref[target_ref[n]]
        return carry

    lax.fori_loop(0, bodies, pack, 0)

    def finish(d, carry):
        keep(d).wait()
        return carry

    lax.fori_loop(0, bodies, finish, 0)


def scatter_parts(rows, depth, map_ref, force_ref, left_ref, right_ref):
    span = map_ref.shape[2]
    per = force_ref.shape[0] // map_ref.shape[0]
    depth_iota = lax.broadcasted_iota(I32, (depth, span), 0)
    row_iota = lax.broadcasted_iota(I32, (rows, span), 0)
    chunks = map_ref.shape[0]
    for j in range(chunks):
        row, deep = cell_parts(map_ref[j], depth)
        onehot = jnp.where(depth_iota == deep, 1.0, 0.0).astype(BF16)
        right_ref[:, j * span : (j + 1) * span] = onehot
        right_ref[:, (chunks + j) * span : (chunks + j + 1) * span] = onehot
        here = row_iota == row
        for c in range(3):
            line = jnp.concatenate(
                [force_ref[j * per + b, c : c + 1, :] for b in range(per)], axis=1
            )
            high = line.astype(BF16).astype(F32)
            at = slice(c * rows, (c + 1) * rows)
            left_ref[at, j * span : (j + 1) * span] = jnp.where(here, high, 0.0).astype(BF16)
            left_ref[at, (chunks + j) * span : (chunks + j + 1) * span] = jnp.where(
                here, line - high, 0.0
            ).astype(BF16)
    def spread(c):
        return lax.dot_general(
            left_ref[c * rows : (c + 1) * rows], right_ref[...], (((1,), (1,)), ((), ())),
            preferred_element_type=F32,
        )

    return spread


def scatter_one_kernel(
    e0_ref, e1_ref, e2_ref, force_ref, map_ref,
    w1_ref, xe_ref, xo_ref, ye_ref, yo_ref, left_ref, right_ref,
):
    shape = e0_ref.shape
    spread = scatter_parts(shape[0] * shape[1], shape[2], map_ref, force_ref, left_ref, right_ref)
    for c, e_ref in enumerate((e0_ref, e1_ref, e2_ref)):
        w1_ref[c] = e_ref[...] + spread(c).reshape(shape)
    write_faces([(w1_ref, 0), (w1_ref, 1), (w1_ref, 2)], xe_ref, xo_ref, ye_ref, yo_ref)


def scatter_two_kernel(
    e_ref, force_ref, map_ref, r_hbm, w2_ref, r_ref, left_ref, right_ref, sem
):
    copy = pltpu.make_async_copy(r_hbm, r_ref, sem)
    copy.start()
    shape = e_ref.shape[1:]
    spread = scatter_parts(shape[0] * shape[1], shape[2], map_ref, force_ref, left_ref, right_ref)
    for c in range(3):
        w2_ref[c] = e_ref[c] + spread(c).reshape(shape)
    copy.wait()


def elastic(v_ref, sh_ref, la_ref, in_ref, vector_halo, stiff_halo, emit):
    rows, cols, depth = sh_ref.shape
    b, a = lax.axis_index("body"), lax.axis_index("across")
    bodies, acrosses = lax.axis_size("body"), lax.axis_size("across")
    bpar, apar = lax.rem(b, 2), lax.rem(a, 2)
    cut = bodies // 4
    x_low = jnp.where(b != 0, 1.0, 0.0).astype(F32)
    x_high = jnp.where(b != bodies - 1, 1.0, 0.0).astype(F32)
    keep_low = jnp.where(b != cut, 1.0, 0.0).astype(F32)
    keep_high = jnp.where(b + 1 != cut, 1.0, 0.0).astype(F32)
    y_low = jnp.where(a != 0, 1.0, 0.0).astype(F32)
    y_high = jnp.where(a != acrosses - 1, 1.0, 0.0).astype(F32)
    vxe, vxo, vye, vyo = vector_halo
    sxe, sxo, sye, syo = stiff_halo
    row = lax.broadcasted_iota(I32, (cols, depth), 0)
    lane = lax.broadcasted_iota(I32, (cols, depth), 1)
    z_mask = jnp.where(lane == depth - 1, 0.0, 1.0)
    start = lane == 0
    top = row == cols - 1
    bottom = row == 0

    def stiffness(shear, lame):
        return 0.5 * shear, shear + 0.5 * lame

    def pick(parity, even, odd):
        return jnp.where(parity == 0, even, odd)

    def x_halo(high):
        e, o = (sxe, sxo) if high else (sxo, sxe)
        there = x_high if high else x_low
        shear, lame = pick(bpar, e[3], o[3]), pick(bpar, e[4], o[4])
        e, o = (vxe, vxo) if high else (vxo, vxe)
        values = [there * pick(bpar, e[c], o[c]) for c in range(3)]
        return stiffness(there * shear, there * lame), values

    def y_halo(high, x):
        e, o = (sye, syo) if high else (syo, sye)
        there = y_high if high else y_low
        at = slice(x, x + 1)
        shear, lame = pick(apar, e[3, at], o[3, at]), pick(apar, e[4, at], o[4, at])
        e, o = (vye, vyo) if high else (vyo, vye)
        values = [there * pick(apar, e[c, at], o[c, at]) for c in range(3)]
        return stiffness(there * shear, there * lame), values

    def slab(x):
        return stiffness(sh_ref[x], la_ref[x]), [v_ref[c, x] for c in range(3)]

    def flux(near, far, along, mask):
        (off, diag), values = near
        (far_off, far_diag), far_values = far
        side, front = off + far_off, diag + far_diag
        if mask is not None:
            side, front = side * mask, front * mask
        return [
            (front if c == along else side) * (values[c] - far_values[c]) for c in range(3)
        ]

    before = flux(x_halo(False), slab(0), 0, keep_low)
    here = slab(0)
    for x in range(rows):
        after = slab(x + 1) if x + 1 < rows else x_halo(True)
        out = flux(here, after, 0, None if x + 1 < rows else keep_high)
        (off, diag), values = here
        inertia = in_ref[x]
        total = [inertia * values[c] + (out[c] - before[c]) for c in range(3)]
        before = out

        def up(value, edge):
            return jnp.where(top, edge, pltpu.roll(value, cols - 1, 0))

        (h_off, h_diag), h_values = y_halo(True, x)
        shifted = (up(off, h_off), up(diag, h_diag)), [up(values[c], h_values[c]) for c in range(3)]
        out = flux(here, shifted, 1, None)
        first = (off[0:1], diag[0:1]), [values[c][0:1] for c in range(3)]
        edge = flux(y_halo(False, x), first, 1, None)
        total = [
            total[c] + (out[c] - jnp.where(bottom, edge[c], pltpu.roll(out[c], 1, 0)))
            for c in range(3)
        ]

        def right(value):
            return z_mask * pltpu.roll(value, depth - 1, 1)

        shifted = (right(off), right(diag)), [right(values[c]) for c in range(3)]
        out = flux(here, shifted, 2, None)
        edge = [-(diag if c == 2 else off) * values[c] for c in range(3)]
        total = [
            total[c] + (out[c] - jnp.where(start, edge[c], pltpu.roll(out[c], 1, 1)))
            for c in range(3)
        ]
        emit(x, total)
        here = after


def stencil_one_kernel(
    r_ref, sh_ref, la_ref, in_ref, xe, xo, ye, yo, map_ref,
    e0_ref, e1_ref, e2_ref, next_ref, both_ref,
):
    e_refs = (e0_ref, e1_ref, e2_ref)
    sums = [jnp.zeros((8, 128), F32) for _ in range(2)]

    def emit(x, total):
        for c in range(3):
            e_refs[c][x] = total[c]
            r = r_ref[c, x]
            sums[0] = sums[0] + fold(r * r)
            sums[1] = sums[1] + fold(r * total[c])

    elastic(r_ref, sh_ref, la_ref, in_ref, (xe, xo, ye, yo), (xe, xo, ye, yo), emit)
    rows, depth = e0_ref.shape[0] * e0_ref.shape[1], e0_ref.shape[2]
    points = next_ref.shape[2]

    def write(j, c, line):
        per = line.shape[1] // points
        for b in range(per):
            next_ref[j * per + b, c : c + 1, :] = line[:, b * points : (b + 1) * points]

    blocks = next_ref.shape[0] - 1
    for k in range(blocks):
        next_ref[k, 3:4, :] = jnp.zeros((1, points), F32)
    lines = [jnp.sum(value, axis=0, keepdims=True) for value in sums]
    next_ref[blocks] = jnp.concatenate(lines + [jnp.zeros((2, points), F32)], axis=0)
    gather_into(lambda c: e_refs[c][...].reshape(rows, depth), rows, depth, map_ref, both_ref, write)


def fold(value):
    cols, depth = value.shape
    total = None
    for k in range(depth // 128):
        part = value[:, k * 128 : (k + 1) * 128]
        part = jnp.sum(part.reshape(cols // 8, 8, 128), axis=0)
        total = part if total is None else total + part
    return total


def forces_two_kernel(
    got_ref, target_ref, table_ref, move_ref, w_hbm, sh_hbm, la_hbm, in_hbm_ref,
    force_ref, dots_ref, sh_ref, la_ref, in_ref, w_ref, acc_ref, sem, cell_sem,
):
    bodies, width = got_ref.shape[0], got_ref.shape[1]
    cap = width // 2
    blocks, points = move_ref.shape[0] - 1, move_ref.shape[2]

    def fetch(d):
        return pltpu.make_async_copy(w_hbm.at[d], w_ref.at[d], sem.at[d])

    def begin(d, carry):
        fetch(d).start()
        return carry

    lax.fori_loop(0, bodies, begin, 0)
    cells = [
        pltpu.make_async_copy(source, target, cell_sem.at[k])
        for k, (source, target) in enumerate(
            [(sh_hbm, sh_ref), (la_hbm, la_ref), (in_hbm_ref, in_ref)]
        )
    ]
    for copy in cells:
        copy.start()
    acc_ref[...] = jnp.zeros_like(acc_ref)

    def device(d, carry):
        fetch(d).wait()
        work = []
        for s in range(cap):
            n = d * cap + s
            work.append((target_ref[n], pair_part(got_ref[d, s], w_ref[d, 2 * s])))
            work.append((table_ref[0, n], pair_part(got_ref[d, cap + s], w_ref[d, 2 * s + 1])))
        for at, part in work:
            acc_ref[at] = acc_ref[at] + part
        return carry

    lax.fori_loop(0, bodies, device, 0)
    inner = jnp.zeros((4, points), F32)
    for k in range(blocks):
        acc = acc_ref[k]
        moved = move_ref[k]
        force = moved * acc[3:4] - acc
        force_ref[k] = force
        inner = inner + moved * force
    inner = jnp.sum(inner[0:3], axis=0, keepdims=True)
    blank = jnp.zeros_like(inner)
    dots_ref[...] = jnp.concatenate([move_ref[blocks][0:2], blank, inner], axis=0)
    for copy in cells:
        copy.wait()


def stencil_two_kernel(
    w1_ref, sh_ref, la_ref, in_ref, xe, xo, ye, yo, cxe, cxo, cye, cyo, dots_ref, e_ref, red_ref
):
    sums = [jnp.zeros((8, 128), F32) for _ in range(2)]

    def emit(x, total):
        for c in range(3):
            e_ref[c, x] = total[c]
            w = w1_ref[c, x]
            sums[0] = sums[0] + fold(w * w)
            sums[1] = sums[1] + fold(w * total[c])

    elastic(w1_ref, sh_ref, la_ref, in_ref, (xe, xo, ye, yo), (cxe, cxo, cye, cyo), emit)
    lines = [jnp.sum(value, axis=0, keepdims=True) for value in sums]
    blank = jnp.zeros_like(lines[0])
    line = dots_ref[...] + jnp.concatenate([blank, blank] + lines, axis=0)
    for d in range(red_ref.shape[0]):
        red_ref[d] = line


def final_kernel(r_ref, w1_ref, w2_ref, red_ref, x_hbm, res_hbm, x_ref, res_ref, sem):
    line = jnp.sum(red_ref[...], axis=0)
    moment = [
        jnp.broadcast_to(jnp.sum(line[k : k + 1], axis=1, keepdims=True), (8, 128)) for k in range(4)
    ]
    m0, m1, m2, m3 = moment
    step = m0 / m1
    norm = (m0 - step * m1) + step * (step * m2 - m1)
    ratio = norm / m0
    grown = 1.0 + ratio
    curve = grown * (grown * m1 - 2.0 * step * m2) + step * step * m3
    next_step = norm / curve
    alpha = step + next_step * grown
    gamma = next_step * step
    cols, depth = r_ref.shape[2], r_ref.shape[3]
    alpha = jnp.broadcast_to(alpha[0:1, 0:1], (cols, depth))
    gamma = jnp.broadcast_to(gamma[0:1, 0:1], (cols, depth))
    copies = []
    for c in range(3):
        for x in range(r_ref.shape[1]):
            r, w1 = r_ref[c, x], w1_ref[c, x]
            x_ref[c, x] = alpha * r - gamma * w1
            res_ref[c, x] = r - alpha * w1 + gamma * w2_ref[c, x]
        copies.append(pltpu.make_async_copy(x_ref.at[c], x_hbm.at[c], sem.at[0, c]))
        copies.append(pltpu.make_async_copy(res_ref.at[c], res_hbm.at[c], sem.at[1, c]))
        for copy in copies[-2:]:
            copy.start()
    for copy in copies:
        copy.wait()


def exchange(xe, xo, ye, yo):
    def pairs(axis, start):
        count = lax.axis_size(axis)
        chosen = []
        for i in range(count):
            partner = i + 1 if (i - start) % 2 == 0 else i - 1
            chosen.append((i, partner % count))
        return chosen

    got_xo = lax.ppermute(xo, "body", pairs("body", 1))
    got_xe = lax.ppermute(xe, "body", pairs("body", 0))
    got_yo = lax.ppermute(yo, "across", pairs("across", 1))
    got_ye = lax.ppermute(ye, "across", pairs("across", 0))
    return (
        got_xe, got_xo, got_ye, got_yo
    )


def on_device(
    cotangent, shear, lame, inertia, surface_points, point_counts, surface_maps, contact_pairs
):
    rows, cols, depth = shear.shape
    points = jnp.transpose(surface_points[0, 0], (1, 0, 2))
    counts = point_counts[0, 0]
    cell_maps = surface_maps[0, 0]
    pair_table = contact_pairs[0, 0][:, None, :]
    _, blocks, width = points.shape
    pairs = pair_table.shape[2]
    bodies, acrosses = lax.axis_size("body"), lax.axis_size("across")
    devices = bodies * acrosses
    cap = pairs // bodies
    slots = cap + blocks // 2
    chunks = blocks // 2
    cell_maps = cell_maps.reshape(chunks, 1, 2 * width)
    flat = rows * cols
    vector = sds((3, rows, cols, depth))

    def faces(count):
        return (
            sds((count, cols, depth)), sds((count, cols, depth)),
            sds((count, rows, depth)), sds((count, rows, depth)),
        )

    moves = sds((blocks, 4, width))
    both = pltpu.VMEM((3 * flat, 2 * depth), BF16)
    wide = 2 * blocks * width
    sides = (pltpu.VMEM((3 * flat, wide), BF16), pltpu.VMEM((depth, wide), BF16))
    total = pltpu.VMEM((blocks, 4, width), F32)
    kept = (bodies, 2 * cap, width, 2 * width)
    kept_mib = 10 + (8 * pairs * width * width >> 20) + (bodies >> 2)
    dma = pltpu.SemaphoreType.DMA
    cells = (sds((rows, cols, depth)),) * 3

    given = (shear, lame, inertia)
    r, shear, lame, inertia, cell_maps, xe, xo, ye, yo, own, first_moves, message, table = call(
        open_kernel, "open", [HBM] * 8, [VMEM] * 12 + [SMEM],
        (vector,) + cells + (sds(cell_maps.shape, I32),) + faces(5)
        + (sds((blocks, 32, width), BF16), moves)
        + (sds((bodies, slots, 8, width)), sds((2, pairs), I32)),
        scratch=(
            pltpu.VMEM(points.shape, F32), pltpu.SMEM(counts.shape, I32),
            pltpu.SMEM(pair_table.shape, I32), pltpu.SMEM((bodies,), I32),
            pltpu.VMEM((blocks, 8, width), F32), both, dma((10,)),
        ), cost=4.0,
    )(*in_hbm(cotangent, shear, lame, inertia, points, counts, pair_table, cell_maps))
    got = lax.all_to_all(message, "body", 0, 0, tiled=True)
    halo = exchange(xe, xo, ye, yo)
    grown = sds((blocks + 1, 4, width))
    *elastic_one, next_moves = call(
        stencil_one_kernel, "stencil_one", [VMEM] * 9, [VMEM] * 4, cells + (grown,),
        scratch=(both,), cost=5.0,
    )(r, shear, lame, inertia, *halo, cell_maps)
    force_one, second_moves, message, targets, weights = call(
        forces_one_kernel, "forces_one", [VMEM] * 2 + [SMEM] + [VMEM] * 2,
        [VMEM] * 3 + [SMEM, HBM],
        (moves, grown, sds((bodies, 2 * cap, 4, width)), sds((pairs,), I32), pltpu.HBM(kept, BF16)),
        scratch=(pltpu.VMEM(kept, BF16), total, dma((bodies,))), cost=6.0, mib=kept_mib,
    )(got, own, table, first_moves, next_moves)
    got = lax.all_to_all(message, "body", 0, 0, tiled=True)
    w1, xe, xo, ye, yo = call(
        scatter_one_kernel, "scatter_one", [VMEM] * 5, [VMEM] * 5, (vector,) + faces(3),
        scratch=sides, cost=3.0, mib=16,
    )(*elastic_one, force_one, cell_maps)
    halo_two = exchange(xe, xo, ye, yo)
    force_two, dots, shear, lame, inertia = call(
        forces_two_kernel, "forces_two", [VMEM] + [SMEM] * 2 + [VMEM] + [HBM] * 4, [VMEM] * 5,
        (moves, sds((4, 128))) + cells,
        scratch=(pltpu.VMEM(kept, BF16), total, dma((bodies,)), dma((3,))), cost=3.0, mib=kept_mib,
    )(got, targets, table, second_moves, *in_hbm(weights, *given))
    elastic_two, partial = call(
        stencil_two_kernel, "stencil_two", [VMEM] * 13, [VMEM] * 2, (vector, sds((devices, 4, 128))),
        cost=1.5,
    )(w1, shear, lame, inertia, *halo_two, *halo, dots)
    sums = lax.all_to_all(partial, ("body", "across"), 0, 0, tiled=True)
    w2, r = call(
        scatter_two_kernel, "scatter_two", [VMEM] * 3 + [HBM], [VMEM] * 2, (vector, vector),
        scratch=sides + (dma(()),), cost=3.0, mib=16,
    )(elastic_two, force_two, cell_maps, *in_hbm(cotangent))
    out = pltpu.VMEM((3, rows, cols, depth), F32)
    return call(
        final_kernel, "final", [VMEM] * 4, [HBM] * 2, (vector, vector),
        scratch=(out, out, dma((2, 3))), cost=1.0,
    )(r, w1, w2, sums)


def solution(mesh):
    placed = (
        P(None, "body", "across", None),
        P("body", "across", None),
        P("body", "across", None),
        P("body", "across", None),
        P("body", "across", None, None, None),
        P("body", "across", None),
        P("body", "across", None, None),
        P("body", "across", None, None),
    )
    return jax.shard_map(
        on_device,
        mesh=mesh,
        in_specs=placed,
        out_specs=(P(None, "body", "across", None), P(None, "body", "across", None)),
        check_vma=False,
    )
```

```python
import jax
import jax.numpy as jnp
from jax import lax
from jax.experimental import pallas as pl
from jax.experimental.pallas import tpu as pltpu
from jax.sharding import PartitionSpec as P

F32 = jnp.float32
BF16 = jnp.bfloat16
I32 = jnp.int32

barrier_reach = 1.0
barrier_scale = 0.005
FAR = 1000.0

VMEM = pl.BlockSpec(memory_space=pltpu.VMEM)
SMEM = pl.BlockSpec(memory_space=pltpu.SMEM)
HBM = pl.BlockSpec(memory_space=pltpu.HBM)


def sds(shape, dtype=F32):
    return jax.ShapeDtypeStruct(shape, dtype)


def call(body, name, in_specs, out_specs, out_shape, scratch=(), cost=2.0, mib=8):
    estimate = pl.CostEstimate(flops=int(cost * 1e8), transcendentals=0, bytes_accessed=int(cost * 3e6))
    return pl.pallas_call(
        body,
        name=name,
        in_specs=in_specs,
        out_specs=out_specs,
        out_shape=out_shape,
        scratch_shapes=list(scratch),
        cost_estimate=estimate,
        compiler_params=pltpu.CompilerParams(vmem_limit_bytes=mib << 20),
    )


def in_hbm(*arrays):
    return tuple(pltpu.with_memory_space_constraint(array, pltpu.HBM) for array in arrays)


def split(values):
    high = values.astype(BF16)
    low = (values - high.astype(F32)).astype(BF16)
    return high, low


def even_faces(block, axis_parity, last):
    first = jnp.where(axis_parity == 0, last, 0)
    return first, last - first


def write_faces(sources, xe_ref, xo_ref, ye_ref, yo_ref):
    bpar = lax.rem(lax.axis_index("body"), 2)
    apar = lax.rem(lax.axis_index("across"), 2)
    for k, (ref, lead) in enumerate(sources):
        at = (lambda x: ref[lead, x]) if lead is not None else (lambda x: ref[x])
        rows = ref.shape[-3]
        cols = ref.shape[-2]
        xi = jnp.where(bpar == 0, rows - 1, 0)
        xe_ref[k] = at(xi)
        xo_ref[k] = at(rows - 1 - xi)
        for x in range(rows):
            slab = at(x)
            low = slab[0:1]
            high = slab[cols - 1 : cols]
            ye_ref[k, x : x + 1] = jnp.where(apar == 0, high, low)
            yo_ref[k, x : x + 1] = jnp.where(apar == 0, low, high)


def cell_parts(cells, depth):
    if depth & (depth - 1) == 0:
        shift = depth.bit_length() - 1
        return lax.shift_right_logical(cells, shift), jnp.bitwise_and(cells, depth - 1)
    row = cells // depth
    return row, cells - row * depth


def gather_into(load, rows, depth, map_ref, both_ref, write):
    for c in range(3):
        high, low = split(load(c))
        both_ref[c * rows : (c + 1) * rows, 0:depth] = high
        both_ref[c * rows : (c + 1) * rows, depth:] = low
    chunks, _, span = map_ref.shape
    depth_iota = lax.broadcasted_iota(I32, (depth, span), 0)
    row_iota = lax.broadcasted_iota(I32, (rows, span), 0)

    def chunk(j, carry):
        row, deep = cell_parts(map_ref[j], depth)
        onehot = jnp.where(depth_iota == deep, 1.0, 0.0).astype(BF16)
        onehot = jnp.concatenate([onehot, onehot], axis=0)
        picked = jnp.dot(both_ref[...], onehot, preferred_element_type=F32)
        here = row_iota == row
        for c in range(3):
            part = jnp.where(here, picked[c * rows : (c + 1) * rows], 0.0)
            write(j, c, jnp.sum(part, axis=0, keepdims=True))
        return carry

    lax.fori_loop(0, chunks, chunk, 0, unroll=8)


def open_kernel(
    r_hbm, sh_hbm, la_hbm, in_hbm, pt_hbm, cnt_hbm, pair_hbm, map_hbm,
    r_ref, sh_ref, la_ref, in_ref, map_ref,
    xe_ref, xo_ref, ye_ref, yo_ref, own_ref, move_ref, msg_ref, table_ref,
    pt_ref, cnt_ref, pair_ref, fill_ref, sent_ref, both_ref, sem,
):
    copies = [
        pltpu.make_async_copy(source, target, sem.at[k])
        for k, (source, target) in enumerate([
            (cnt_hbm, cnt_ref), (pair_hbm, pair_ref), (pt_hbm, pt_ref), (map_hbm, map_ref),
            (r_hbm.at[0], r_ref.at[0]), (r_hbm.at[1], r_ref.at[1]), (r_hbm.at[2], r_ref.at[2]),
            (sh_hbm, sh_ref), (la_hbm, la_ref), (in_hbm, in_ref),
        ])
    ]
    for copy in copies:
        copy.start()
    bodies = msg_ref.shape[0]
    blocks = own_ref.shape[0]
    odd_total = blocks // 2
    pairs = table_ref.shape[1]
    cap = pairs // bodies
    slots = cap + odd_total
    points = own_ref.shape[2]
    lane = lax.broadcasted_iota(I32, (1, points), 1)
    edge = lax.broadcasted_iota(I32, (4, points), 0) == 3
    for copy in copies[:4]:
        copy.wait()
    for d in range(bodies):
        fill_ref[d] = 0

    def place(n, carry):
        dest = pair_ref[1, 0, n]
        rank = fill_ref[dest]
        fill_ref[dest] = rank + 1
        table_ref[0, dest * cap + rank] = pair_ref[0, 0, n]
        table_ref[1, dest * cap + rank] = pair_ref[2, 0, n]
        return carry

    lax.fori_loop(0, pairs, place, 0)
    blank = jnp.zeros((1, points), F32)
    for k in range(blocks):
        tile = jnp.concatenate([pt_ref[c, k : k + 1, :] for c in range(3)] + [blank], axis=0)
        own_ref[k] = target_rows(measured(jnp.where(lane < cnt_ref[k], tile, -FAR), edge))
        tile = jnp.where(lane < cnt_ref[k], tile, FAR)
        sent_ref[k, 1, 1:2, :] = tile[0:1]
        sent_ref[k, 2] = tile[1:3]
        move_ref[k, 3:4, :] = blank + 1.0
    for copy in copies[4:]:
        copy.wait()
    rows, depth = r_ref.shape[1] * r_ref.shape[2], r_ref.shape[3]

    def write(j, c, line):
        per = line.shape[1] // points
        for b in range(per):
            part = line[:, b * points : (b + 1) * points]
            move_ref[j * per + b, c : c + 1, :] = part
            sent_ref[j * per + b, c // 2, c % 2 : c % 2 + 1, :] = part

    gather_into(lambda c: r_ref[c].reshape(rows, depth), rows, depth, map_ref, both_ref, write)

    def pack(d, carry):
        for s in range(cap):
            second = table_ref[1, d * cap + s].astype(F32)
            msg_ref[d, 3 * s : 3 * s + 3] = sent_ref[table_ref[0, d * cap + s]]
            msg_ref[d, 3 * slots + s // 2, s % 2 : s % 2 + 1, :] = jnp.full((1, points), second)
        for j in range(odd_total):
            msg_ref[d, 3 * (cap + j) : 3 * (cap + j) + 3] = sent_ref[2 * j + 1]
        return carry

    lax.fori_loop(0, bodies, pack, 0)
    sources = [(r_ref, 0), (r_ref, 1), (r_ref, 2), (sh_ref, None), (la_ref, None)]
    write_faces(sources, xe_ref, xo_ref, ye_ref, yo_ref)


def measured(tile, edge):
    square = jnp.where(edge, 0.0, tile * tile)
    return jnp.where(edge, jnp.sum(square, axis=0, keepdims=True), tile)


def three_parts(value):
    high = value.astype(BF16).astype(F32)
    rest = value - high
    middle = rest.astype(BF16).astype(F32)
    return high, middle, rest - middle


def source_rows(tile):
    row = lax.broadcasted_iota(I32, (8, tile.shape[1]), 0)
    high, middle, low = three_parts(jnp.concatenate([tile, tile], axis=0))
    first = jnp.where(row == 7, middle, high)
    second = jnp.where(row == 3, low, jnp.where(row < 3, middle, high))
    second = jnp.where(row == 7, 1.0, second)
    third = jnp.where(row < 3, low, middle)
    third = jnp.where((row == 3) | (row == 7), 1.0, third)
    return jnp.concatenate([first, second, third, jnp.zeros_like(first)], axis=0).astype(BF16)


def target_rows(tile):
    row = lax.broadcasted_iota(I32, (8, tile.shape[1]), 0)
    high, middle, low = three_parts(jnp.concatenate([tile, tile], axis=0))
    first = -2.0 * jnp.where(row < 4, high, middle)
    first = jnp.where((row == 3) | (row == 7), 1.0, first)
    second = -2.0 * jnp.where(row < 4, high, low)
    second = jnp.where(row == 3, 1.0, jnp.where(row == 7, high, second))
    third = -2.0 * jnp.where(row < 4, high, middle)
    third = jnp.where(row == 3, middle, jnp.where(row == 7, low, third))
    return jnp.concatenate([first, second, third, jnp.zeros_like(first)], axis=0).astype(BF16)


def weigh(tile, target):
    squared = lax.dot_general(
        source_rows(tile), target, (((0,), (0,)), ((), ())), preferred_element_type=F32
    )
    q = 1.0 - 1.0 / squared
    weight = barrier_scale * (-2.0 * jnp.log(squared) - 4.0 * q + q * q)
    return jnp.where(squared < barrier_reach, weight, 0.0)


def pair_part(moves, weights):
    points = moves.shape[1]
    high = moves.astype(BF16).astype(F32)
    lhs = jnp.concatenate([high, moves - high], axis=0).astype(BF16)
    out = jnp.dot(lhs, weights, preferred_element_type=F32)
    return (out[0:4, :points] + out[4:8, :points]) + (out[0:4, points:] + out[4:8, points:])


def forces_one_kernel(
    got_ref, own_ref, table_ref, move_ref, next_ref,
    force_ref, sum_ref, msg_ref, target_ref, w_hbm, w_ref, acc_ref, sem,
):
    bodies = got_ref.shape[0]
    blocks, _, points = move_ref.shape
    cap = table_ref.shape[1] // bodies
    slots = cap + blocks // 2
    one = jnp.ones((1, points), F32)

    def received(d, slot):
        parts = got_ref[d, pl.ds(3 * slot, 3)]
        moves = jnp.concatenate([parts[0], parts[1, 0:1], one], axis=0)
        tile = jnp.concatenate([parts[1, 1:2], parts[2], one], axis=0)
        return moves, measured(tile, edge)

    acc_ref[...] = jnp.zeros_like(acc_ref)

    edge = lax.broadcasted_iota(I32, (4, points), 0) == 3

    def keep(d):
        return pltpu.make_async_copy(w_ref.at[d], w_hbm.at[d], sem.at[d])

    def find(d, carry):
        for s in range(cap):
            target_ref[d * cap + s] = jnp.max(
                got_ref[d, 3 * slots + s // 2, s % 2 : s % 2 + 1, :]
            ).astype(I32)
        return carry

    lax.fori_loop(0, bodies, find, 0, unroll=8)

    def device(d, carry):
        work = []
        for s in range(cap):
            n = d * cap + s
            work.append((received(d, s), target_ref[n]))
            first = table_ref[0, n]
            odd = lax.shift_right_logical(table_ref[1, n], 1)
            work.append((received(d, cap + odd), first))
        parts = []
        for k, ((moves, tile), at) in enumerate(work):
            high, low = split(weigh(tile, own_ref[at]))
            both = jnp.concatenate([high, low], axis=1)
            w_ref[d, k] = both
            parts.append(pair_part(moves, both))
        for (_, at), part in zip(work, parts):
            acc_ref[at] = acc_ref[at] + part
        keep(d).start()
        return carry

    lax.fori_loop(0, bodies, device, 0, unroll=4)
    row = lax.broadcasted_iota(I32, (4, points), 0)
    inner = jnp.zeros((4, points), F32)
    for k in range(blocks):
        acc = acc_ref[k]
        force = move_ref[k] * acc[3:4] - acc
        force_ref[k] = force
        sum_ref[k] = jnp.where(row < 3, next_ref[k] + force, 1.0)
        inner = inner + move_ref[k] * force
    inner = jnp.sum(inner[0:3], axis=0, keepdims=True)
    sum_ref[blocks] = next_ref[blocks] + jnp.where(row == 1, inner, 0.0)

    def pack(d, carry):
        for s in range(cap):
            n = d * cap + s
            msg_ref[d, s] = sum_ref[table_ref[0, n]]
            msg_ref[d, cap + s] = sum_ref[target_ref[n]]
        return carry

    lax.fori_loop(0, bodies, pack, 0)

    def finish(d, carry):
        keep(d).wait()
        return carry

    lax.fori_loop(0, bodies, finish, 0)


def scatter_parts(rows, depth, map_ref, force_ref, left_ref, right_ref):
    span = map_ref.shape[2]
    per = force_ref.shape[0] // map_ref.shape[0]
    depth_iota = lax.broadcasted_iota(I32, (depth, span), 0)
    row_iota = lax.broadcasted_iota(I32, (rows, span), 0)
    chunks = map_ref.shape[0]
    for j in range(chunks):
        row, deep = cell_parts(map_ref[j], depth)
        onehot = jnp.where(depth_iota == deep, 1.0, 0.0).astype(BF16)
        right_ref[:, j * span : (j + 1) * span] = onehot
        right_ref[:, (chunks + j) * span : (chunks + j + 1) * span] = onehot
        here = row_iota == row
        for c in range(3):
            line = jnp.concatenate(
                [force_ref[j * per + b, c : c + 1, :] for b in range(per)], axis=1
            )
            high = line.astype(BF16).astype(F32)
            at = slice(c * rows, (c + 1) * rows)
            left_ref[at, j * span : (j + 1) * span] = jnp.where(here, high, 0.0).astype(BF16)
            left_ref[at, (chunks + j) * span : (chunks + j + 1) * span] = jnp.where(
                here, line - high, 0.0
            ).astype(BF16)
    def spread(c):
        return lax.dot_general(
            left_ref[c * rows : (c + 1) * rows], right_ref[...], (((1,), (1,)), ((), ())),
            preferred_element_type=F32,
        )

    return spread


def scatter_one_kernel(
    e0_ref, e1_ref, e2_ref, force_ref, map_ref,
    w1_ref, xe_ref, xo_ref, ye_ref, yo_ref, left_ref, right_ref,
):
    shape = e0_ref.shape
    spread = scatter_parts(shape[0] * shape[1], shape[2], map_ref, force_ref, left_ref, right_ref)
    for c, e_ref in enumerate((e0_ref, e1_ref, e2_ref)):
        w1_ref[c] = e_ref[...] + spread(c).reshape(shape)
    write_faces([(w1_ref, 0), (w1_ref, 1), (w1_ref, 2)], xe_ref, xo_ref, ye_ref, yo_ref)


def scatter_two_kernel(
    e_ref, force_ref, map_ref, r_hbm, w2_ref, r_ref, left_ref, right_ref, sem
):
    copy = pltpu.make_async_copy(r_hbm, r_ref, sem)
    copy.start()
    shape = e_ref.shape[1:]
    spread = scatter_parts(shape[0] * shape[1], shape[2], map_ref, force_ref, left_ref, right_ref)
    for c in range(3):
        w2_ref[c] = e_ref[c] + spread(c).reshape(shape)
    copy.wait()


def elastic(v_ref, sh_ref, la_ref, in_ref, vector_halo, stiff_halo, emit):
    rows, cols, depth = sh_ref.shape
    b, a = lax.axis_index("body"), lax.axis_index("across")
    bodies, acrosses = lax.axis_size("body"), lax.axis_size("across")
    bpar, apar = lax.rem(b, 2), lax.rem(a, 2)
    cut = bodies // 4
    x_low = jnp.where(b != 0, 1.0, 0.0).astype(F32)
    x_high = jnp.where(b != bodies - 1, 1.0, 0.0).astype(F32)
    keep_low = jnp.where(b != cut, 1.0, 0.0).astype(F32)
    keep_high = jnp.where(b + 1 != cut, 1.0, 0.0).astype(F32)
    y_low = jnp.where(a != 0, 1.0, 0.0).astype(F32)
    y_high = jnp.where(a != acrosses - 1, 1.0, 0.0).astype(F32)
    vxe, vxo, vye, vyo = vector_halo
    sxe, sxo, sye, syo = stiff_halo
    row = lax.broadcasted_iota(I32, (cols, depth), 0)
    lane = lax.broadcasted_iota(I32, (cols, depth), 1)
    z_mask = jnp.where(lane == depth - 1, 0.0, 1.0)
    start = lane == 0
    top = row == cols - 1
    bottom = row == 0

    def stiffness(shear, lame):
        return 0.5 * shear, shear + 0.5 * lame

    def pick(parity, even, odd):
        return jnp.where(parity == 0, even, odd)

    def x_halo(high):
        e, o = (sxe, sxo) if high else (sxo, sxe)
        there = x_high if high else x_low
        shear, lame = pick(bpar, e[3], o[3]), pick(bpar, e[4], o[4])
        e, o = (vxe, vxo) if high else (vxo, vxe)
        values = [there * pick(bpar, e[c], o[c]) for c in range(3)]
        return stiffness(there * shear, there * lame), values

    def y_halo(high, x):
        e, o = (sye, syo) if high else (syo, sye)
        there = y_high if high else y_low
        at = slice(x, x + 1)
        shear, lame = pick(apar, e[3, at], o[3, at]), pick(apar, e[4, at], o[4, at])
        e, o = (vye, vyo) if high else (vyo, vye)
        values = [there * pick(apar, e[c, at], o[c, at]) for c in range(3)]
        return stiffness(there * shear, there * lame), values

    def slab(x):
        return stiffness(sh_ref[x], la_ref[x]), [v_ref[c, x] for c in range(3)]

    def flux(near, far, along, mask):
        (off, diag), values = near
        (far_off, far_diag), far_values = far
        side, front = off + far_off, diag + far_diag
        if mask is not None:
            side, front = side * mask, front * mask
        return [
            (front if c == along else side) * (values[c] - far_values[c]) for c in range(3)
        ]

    before = flux(x_halo(False), slab(0), 0, keep_low)
    here = slab(0)
    for x in range(rows):
        after = slab(x + 1) if x + 1 < rows else x_halo(True)
        out = flux(here, after, 0, None if x + 1 < rows else keep_high)
        (off, diag), values = here
        inertia = in_ref[x]
        total = [inertia * values[c] + (out[c] - before[c]) for c in range(3)]
        before = out

        def up(value, edge):
            return jnp.where(top, edge, pltpu.roll(value, cols - 1, 0))

        (h_off, h_diag), h_values = y_halo(True, x)
        shifted = (up(off, h_off), up(diag, h_diag)), [up(values[c], h_values[c]) for c in range(3)]
        out = flux(here, shifted, 1, None)
        first = (off[0:1], diag[0:1]), [values[c][0:1] for c in range(3)]
        edge = flux(y_halo(False, x), first, 1, None)
        total = [
            total[c] + (out[c] - jnp.where(bottom, edge[c], pltpu.roll(out[c], 1, 0)))
            for c in range(3)
        ]

        def right(value):
            return z_mask * pltpu.roll(value, depth - 1, 1)

        shifted = (right(off), right(diag)), [right(values[c]) for c in range(3)]
        out = flux(here, shifted, 2, None)
        edge = [-(diag if c == 2 else off) * values[c] for c in range(3)]
        total = [
            total[c] + (out[c] - jnp.where(start, edge[c], pltpu.roll(out[c], 1, 1)))
            for c in range(3)
        ]
        emit(x, total)
        here = after


def stencil_one_kernel(
    r_ref, sh_ref, la_ref, in_ref, xe, xo, ye, yo, map_ref,
    e0_ref, e1_ref, e2_ref, next_ref, both_ref,
):
    e_refs = (e0_ref, e1_ref, e2_ref)
    sums = [jnp.zeros((8, 128), F32) for _ in range(2)]

    def emit(x, total):
        for c in range(3):
            e_refs[c][x] = total[c]
            r = r_ref[c, x]
            sums[0] = sums[0] + fold(r * r)
            sums[1] = sums[1] + fold(r * total[c])

    elastic(r_ref, sh_ref, la_ref, in_ref, (xe, xo, ye, yo), (xe, xo, ye, yo), emit)
    rows, depth = e0_ref.shape[0] * e0_ref.shape[1], e0_ref.shape[2]
    points = next_ref.shape[2]

    def write(j, c, line):
        per = line.shape[1] // points
        for b in range(per):
            next_ref[j * per + b, c : c + 1, :] = line[:, b * points : (b + 1) * points]

    blocks = next_ref.shape[0] - 1
    for k in range(blocks):
        next_ref[k, 3:4, :] = jnp.zeros((1, points), F32)
    lines = [jnp.sum(value, axis=0, keepdims=True) for value in sums]
    next_ref[blocks] = jnp.concatenate(lines + [jnp.zeros((2, points), F32)], axis=0)
    gather_into(lambda c: e_refs[c][...].reshape(rows, depth), rows, depth, map_ref, both_ref, write)


def fold(value):
    cols, depth = value.shape
    total = None
    for k in range(depth // 128):
        part = value[:, k * 128 : (k + 1) * 128]
        part = jnp.sum(part.reshape(cols // 8, 8, 128), axis=0)
        total = part if total is None else total + part
    return total


def forces_two_kernel(
    got_ref, target_ref, table_ref, move_ref, w_hbm, sh_hbm, la_hbm, in_hbm_ref,
    force_ref, dots_ref, sh_ref, la_ref, in_ref, w_ref, acc_ref, sem, cell_sem,
):
    bodies, width = got_ref.shape[0], got_ref.shape[1]
    cap = width // 2
    blocks, points = move_ref.shape[0] - 1, move_ref.shape[2]

    def fetch(d):
        return pltpu.make_async_copy(w_hbm.at[d], w_ref.at[d], sem.at[d])

    def begin(d, carry):
        fetch(d).start()
        return carry

    lax.fori_loop(0, bodies, begin, 0)
    cells = [
        pltpu.make_async_copy(source, target, cell_sem.at[k])
        for k, (source, target) in enumerate(
            [(sh_hbm, sh_ref), (la_hbm, la_ref), (in_hbm_ref, in_ref)]
        )
    ]
    for copy in cells:
        copy.start()
    acc_ref[...] = jnp.zeros_like(acc_ref)

    def device(d, carry):
        fetch(d).wait()
        work = []
        for s in range(cap):
            n = d * cap + s
            work.append((target_ref[n], pair_part(got_ref[d, s], w_ref[d, 2 * s])))
            work.append((table_ref[0, n], pair_part(got_ref[d, cap + s], w_ref[d, 2 * s + 1])))
        for at, part in work:
            acc_ref[at] = acc_ref[at] + part
        return carry

    lax.fori_loop(0, bodies, device, 0)
    inner = jnp.zeros((4, points), F32)
    for k in range(blocks):
        acc = acc_ref[k]
        moved = move_ref[k]
        force = moved * acc[3:4] - acc
        force_ref[k] = force
        inner = inner + moved * force
    inner = jnp.sum(inner[0:3], axis=0, keepdims=True)
    blank = jnp.zeros_like(inner)
    dots_ref[...] = jnp.concatenate([move_ref[blocks][0:2], blank, inner], axis=0)
    for copy in cells:
        copy.wait()


def stencil_two_kernel(
    w1_ref, sh_ref, la_ref, in_ref, xe, xo, ye, yo, cxe, cxo, cye, cyo, dots_ref, e_ref, red_ref
):
    sums = [jnp.zeros((8, 128), F32) for _ in range(2)]

    def emit(x, total):
        for c in range(3):
            e_ref[c, x] = total[c]
            w = w1_ref[c, x]
            sums[0] = sums[0] + fold(w * w)
            sums[1] = sums[1] + fold(w * total[c])

    elastic(w1_ref, sh_ref, la_ref, in_ref, (xe, xo, ye, yo), (cxe, cxo, cye, cyo), emit)
    lines = [jnp.sum(value, axis=0, keepdims=True) for value in sums]
    blank = jnp.zeros_like(lines[0])
    line = dots_ref[...] + jnp.concatenate([blank, blank] + lines, axis=0)
    for d in range(red_ref.shape[0]):
        red_ref[d] = line


def final_kernel(r_ref, w1_ref, w2_ref, red_ref, x_hbm, res_hbm, x_ref, res_ref, sem):
    line = jnp.sum(red_ref[...], axis=0)
    moment = [
        jnp.broadcast_to(jnp.sum(line[k : k + 1], axis=1, keepdims=True), (8, 128)) for k in range(4)
    ]
    m0, m1, m2, m3 = moment
    step = m0 / m1
    norm = (m0 - step * m1) + step * (step * m2 - m1)
    ratio = norm / m0
    grown = 1.0 + ratio
    curve = grown * (grown * m1 - 2.0 * step * m2) + step * step * m3
    next_step = norm / curve
    alpha = step + next_step * grown
    gamma = next_step * step
    cols, depth = r_ref.shape[2], r_ref.shape[3]
    alpha = jnp.broadcast_to(alpha[0:1, 0:1], (cols, depth))
    gamma = jnp.broadcast_to(gamma[0:1, 0:1], (cols, depth))
    copies = []
    for c in range(3):
        for x in range(r_ref.shape[1]):
            r, w1 = r_ref[c, x], w1_ref[c, x]
            x_ref[c, x] = alpha * r - gamma * w1
            res_ref[c, x] = r - alpha * w1 + gamma * w2_ref[c, x]
        copies.append(pltpu.make_async_copy(x_ref.at[c], x_hbm.at[c], sem.at[0, c]))
        copies.append(pltpu.make_async_copy(res_ref.at[c], res_hbm.at[c], sem.at[1, c]))
        for copy in copies[-2:]:
            copy.start()
    for copy in copies:
        copy.wait()


def exchange(xe, xo, ye, yo):
    def pairs(axis, start):
        count = lax.axis_size(axis)
        chosen = []
        for i in range(count):
            partner = i + 1 if (i - start) % 2 == 0 else i - 1
            chosen.append((i, partner % count))
        return chosen

    got_xo = lax.ppermute(xo, "body", pairs("body", 1))
    got_xe = lax.ppermute(xe, "body", pairs("body", 0))
    got_yo = lax.ppermute(yo, "across", pairs("across", 1))
    got_ye = lax.ppermute(ye, "across", pairs("across", 0))
    return (
        got_xe, got_xo, got_ye, got_yo
    )


def on_device(
    cotangent, shear, lame, inertia, surface_points, point_counts, surface_maps, contact_pairs
):
    rows, cols, depth = shear.shape
    points = jnp.transpose(surface_points[0, 0], (1, 0, 2))
    counts = point_counts[0, 0]
    cell_maps = surface_maps[0, 0]
    pair_table = contact_pairs[0, 0][:, None, :]
    _, blocks, width = points.shape
    pairs = pair_table.shape[2]
    bodies, acrosses = lax.axis_size("body"), lax.axis_size("across")
    devices = bodies * acrosses
    cap = pairs // bodies
    slots = cap + blocks // 2
    chunks = blocks // 2
    cell_maps = cell_maps.reshape(chunks, 1, 2 * width)
    flat = rows * cols
    vector = sds((3, rows, cols, depth))

    def faces(count):
        return (
            sds((count, cols, depth)), sds((count, cols, depth)),
            sds((count, rows, depth)), sds((count, rows, depth)),
        )

    moves = sds((blocks, 4, width))
    both = pltpu.VMEM((3 * flat, 2 * depth), BF16)
    wide = 2 * blocks * width
    sides = (pltpu.VMEM((3 * flat, wide), BF16), pltpu.VMEM((depth, wide), BF16))
    total = pltpu.VMEM((blocks, 4, width), F32)
    kept = (bodies, 2 * cap, width, 2 * width)
    kept_mib = 10 + (8 * pairs * width * width >> 20) + (bodies >> 2)
    dma = pltpu.SemaphoreType.DMA
    cells = (sds((rows, cols, depth)),) * 3

    given = (shear, lame, inertia)
    r, shear, lame, inertia, cell_maps, xe, xo, ye, yo, own, first_moves, message, table = call(
        open_kernel, "open", [HBM] * 8, [VMEM] * 12 + [SMEM],
        (vector,) + cells + (sds(cell_maps.shape, I32),) + faces(5)
        + (sds((blocks, 32, width), BF16), moves)
        + (sds((bodies, 3 * slots + (cap + 1) // 2, 2, width)), sds((2, pairs), I32)),
        scratch=(
            pltpu.VMEM(points.shape, F32), pltpu.SMEM(counts.shape, I32),
            pltpu.SMEM(pair_table.shape, I32), pltpu.SMEM((bodies,), I32),
            pltpu.VMEM((blocks, 3, 2, width), F32), both, dma((10,)),
        ), cost=4.0,
    )(*in_hbm(cotangent, shear, lame, inertia, points, counts, pair_table, cell_maps))
    got = lax.all_to_all(message, "body", 0, 0, tiled=True)
    halo = exchange(xe, xo, ye, yo)
    grown = sds((blocks + 1, 4, width))
    *elastic_one, next_moves = call(
        stencil_one_kernel, "stencil_one", [VMEM] * 9, [VMEM] * 4, cells + (grown,),
        scratch=(both,), cost=5.0,
    )(r, shear, lame, inertia, *halo, cell_maps)
    force_one, second_moves, message, targets, weights = call(
        forces_one_kernel, "forces_one", [VMEM] * 2 + [SMEM] + [VMEM] * 2,
        [VMEM] * 3 + [SMEM, HBM],
        (moves, grown, sds((bodies, 2 * cap, 4, width)), sds((pairs,), I32), pltpu.HBM(kept, BF16)),
        scratch=(pltpu.VMEM(kept, BF16), total, dma((bodies,))), cost=6.0, mib=kept_mib,
    )(got, own, table, first_moves, next_moves)
    got = lax.all_to_all(message, "body", 0, 0, tiled=True)
    w1, xe, xo, ye, yo = call(
        scatter_one_kernel, "scatter_one", [VMEM] * 5, [VMEM] * 5, (vector,) + faces(3),
        scratch=sides, cost=3.0, mib=16,
    )(*elastic_one, force_one, cell_maps)
    halo_two = exchange(xe, xo, ye, yo)
    force_two, dots, shear, lame, inertia = call(
        forces_two_kernel, "forces_two", [VMEM] + [SMEM] * 2 + [VMEM] + [HBM] * 4, [VMEM] * 5,
        (moves, sds((4, 128))) + cells,
        scratch=(pltpu.VMEM(kept, BF16), total, dma((bodies,)), dma((3,))), cost=3.0, mib=kept_mib,
    )(got, targets, table, second_moves, *in_hbm(weights, *given))
    elastic_two, partial = call(
        stencil_two_kernel, "stencil_two", [VMEM] * 13, [VMEM] * 2, (vector, sds((devices, 4, 128))),
        cost=1.5,
    )(w1, shear, lame, inertia, *halo_two, *halo, dots)
    sums = lax.all_to_all(partial, ("body", "across"), 0, 0, tiled=True)
    w2, r = call(
        scatter_two_kernel, "scatter_two", [VMEM] * 3 + [HBM], [VMEM] * 2, (vector, vector),
        scratch=sides + (dma(()),), cost=3.0, mib=16,
    )(elastic_two, force_two, cell_maps, *in_hbm(cotangent))
    out = pltpu.VMEM((3, rows, cols, depth), F32)
    return call(
        final_kernel, "final", [VMEM] * 4, [HBM] * 2, (vector, vector),
        scratch=(out, out, dma((2, 3))), cost=1.0,
    )(r, w1, w2, sums)


def solution(mesh):
    placed = (
        P(None, "body", "across", None),
        P("body", "across", None),
        P("body", "across", None),
        P("body", "across", None),
        P("body", "across", None, None, None),
        P("body", "across", None),
        P("body", "across", None, None),
        P("body", "across", None, None),
    )
    return jax.shard_map(
        on_device,
        mesh=mesh,
        in_specs=placed,
        out_specs=(P(None, "body", "across", None), P(None, "body", "across", None)),
        check_vma=False,
    )
```

```python
import jax
import jax.numpy as jnp
from jax import lax
from jax.experimental import pallas as pl
from jax.experimental.pallas import tpu as pltpu
from jax.sharding import PartitionSpec as P

F32 = jnp.float32
BF16 = jnp.bfloat16
I32 = jnp.int32

barrier_reach = 1.0
barrier_scale = 0.005
FAR = 1000.0

VMEM = pl.BlockSpec(memory_space=pltpu.VMEM)
SMEM = pl.BlockSpec(memory_space=pltpu.SMEM)
HBM = pl.BlockSpec(memory_space=pltpu.HBM)


def sds(shape, dtype=F32):
    return jax.ShapeDtypeStruct(shape, dtype)


def call(body, name, in_specs, out_specs, out_shape, scratch=(), cost=2.0, mib=8):
    estimate = pl.CostEstimate(flops=int(cost * 1e8), transcendentals=0, bytes_accessed=int(cost * 3e6))
    return pl.pallas_call(
        body,
        name=name,
        in_specs=in_specs,
        out_specs=out_specs,
        out_shape=out_shape,
        scratch_shapes=list(scratch),
        cost_estimate=estimate,
        compiler_params=pltpu.CompilerParams(vmem_limit_bytes=mib << 20),
    )


def in_hbm(*arrays):
    return tuple(pltpu.with_memory_space_constraint(array, pltpu.HBM) for array in arrays)


def split(values):
    high = values.astype(BF16)
    low = (values - high.astype(F32)).astype(BF16)
    return high, low


def even_faces(block, axis_parity, last):
    first = jnp.where(axis_parity == 0, last, 0)
    return first, last - first


def write_faces(sources, xe_ref, xo_ref, ye_ref, yo_ref):
    bpar = lax.rem(lax.axis_index("body"), 2)
    apar = lax.rem(lax.axis_index("across"), 2)
    for k, (ref, lead) in enumerate(sources):
        at = (lambda x: ref[lead, x]) if lead is not None else (lambda x: ref[x])
        rows = ref.shape[-3]
        cols = ref.shape[-2]
        xi = jnp.where(bpar == 0, rows - 1, 0)
        xe_ref[k] = at(xi)
        xo_ref[k] = at(rows - 1 - xi)
        for x in range(rows):
            slab = at(x)
            low = slab[0:1]
            high = slab[cols - 1 : cols]
            ye_ref[k, x : x + 1] = jnp.where(apar == 0, high, low)
            yo_ref[k, x : x + 1] = jnp.where(apar == 0, low, high)


def cell_parts(cells, depth):
    if depth & (depth - 1) == 0:
        shift = depth.bit_length() - 1
        return lax.shift_right_logical(cells, shift), jnp.bitwise_and(cells, depth - 1)
    row = cells // depth
    return row, cells - row * depth


def gather_into(load, rows, depth, map_ref, both_ref, write, place=None):
    for c in range(3):
        high, low = split(load(c))
        both_ref[c * rows : (c + 1) * rows, 0:depth] = high
        both_ref[c * rows : (c + 1) * rows, depth:] = low
    chunks, _, span = map_ref.shape
    depth_iota = lax.broadcasted_iota(I32, (depth, span), 0)
    row_iota = lax.broadcasted_iota(I32, (rows, span), 0)

    def chunk(j, carry):
        row, deep = cell_parts(map_ref[j], depth)
        onehot = jnp.where(depth_iota == deep, 1.0, 0.0).astype(BF16)
        onehot = jnp.concatenate([onehot, onehot], axis=0)
        row = row if place is None else place(row)
        picked = jnp.dot(both_ref[...], onehot, preferred_element_type=F32)
        here = row_iota == row
        for c in range(3):
            part = jnp.where(here, picked[c * rows : (c + 1) * rows], 0.0)
            write(j, c, jnp.sum(part, axis=0, keepdims=True))
        return carry

    lax.fori_loop(0, chunks, chunk, 0, unroll=8)


def open_kernel(
    r_hbm, sh_hbm, la_hbm, in_hbm, pt_hbm, cnt_hbm, pair_hbm, map_hbm,
    r_ref, sh_ref, la_ref, in_ref, map_ref,
    xe_ref, xo_ref, ye_ref, yo_ref, own_ref, move_ref, msg_ref, table_ref,
    pt_ref, cnt_ref, pair_ref, fill_ref, sent_ref, both_ref, sem,
):
    copies = [
        pltpu.make_async_copy(source, target, sem.at[k])
        for k, (source, target) in enumerate([
            (cnt_hbm, cnt_ref), (pair_hbm, pair_ref), (pt_hbm, pt_ref), (map_hbm, map_ref),
            (r_hbm.at[0], r_ref.at[0]), (r_hbm.at[1], r_ref.at[1]), (r_hbm.at[2], r_ref.at[2]),
            (sh_hbm, sh_ref), (la_hbm, la_ref), (in_hbm, in_ref),
        ])
    ]
    for copy in copies:
        copy.start()
    bodies = msg_ref.shape[0]
    blocks = own_ref.shape[0]
    odd_total = blocks // 2
    pairs = table_ref.shape[1]
    cap = pairs // bodies
    slots = cap + odd_total
    points = own_ref.shape[2]
    lane = lax.broadcasted_iota(I32, (1, points), 1)
    edge = lax.broadcasted_iota(I32, (4, points), 0) == 3
    for copy in copies[:4]:
        copy.wait()
    for d in range(bodies):
        fill_ref[d] = 0

    def place(n, carry):
        dest = pair_ref[1, 0, n]
        rank = fill_ref[dest]
        fill_ref[dest] = rank + 1
        table_ref[0, dest * cap + rank] = pair_ref[0, 0, n]
        table_ref[1, dest * cap + rank] = pair_ref[2, 0, n]
        return carry

    lax.fori_loop(0, pairs, place, 0)
    blank = jnp.zeros((1, points), F32)
    for k in range(blocks):
        tile = jnp.concatenate([pt_ref[c, k : k + 1, :] for c in range(3)] + [blank], axis=0)
        own_ref[k] = target_rows(measured(jnp.where(lane < cnt_ref[k], tile, -FAR), edge))
        tile = jnp.where(lane < cnt_ref[k], tile, FAR)
        sent_ref[k, 1, 1:2, :] = tile[0:1]
        sent_ref[k, 2] = tile[1:3]
        move_ref[k, 3:4, :] = blank + 1.0
    for copy in copies[4:]:
        copy.wait()
    rows, depth = r_ref.shape[1] * r_ref.shape[2], r_ref.shape[3]

    def write(j, c, line):
        per = line.shape[1] // points
        for b in range(per):
            part = line[:, b * points : (b + 1) * points]
            move_ref[j * per + b, c : c + 1, :] = part
            sent_ref[j * per + b, c // 2, c % 2 : c % 2 + 1, :] = part

    gather_into(lambda c: r_ref[c].reshape(rows, depth), rows, depth, map_ref, both_ref, write)

    def pack(d, carry):
        for s in range(cap):
            second = table_ref[1, d * cap + s].astype(F32)
            msg_ref[d, 3 * s : 3 * s + 3] = sent_ref[table_ref[0, d * cap + s]]
            msg_ref[d, 3 * slots + s // 2, s % 2 : s % 2 + 1, :] = jnp.full((1, points), second)
        for j in range(odd_total):
            msg_ref[d, 3 * (cap + j) : 3 * (cap + j) + 3] = sent_ref[2 * j + 1]
        return carry

    lax.fori_loop(0, bodies, pack, 0)
    sources = [(r_ref, 0), (r_ref, 1), (r_ref, 2), (sh_ref, None), (la_ref, None)]
    write_faces(sources, xe_ref, xo_ref, ye_ref, yo_ref)


def measured(tile, edge):
    square = jnp.where(edge, 0.0, tile * tile)
    return jnp.where(edge, jnp.sum(square, axis=0, keepdims=True), tile)


def three_parts(value):
    high = value.astype(BF16).astype(F32)
    rest = value - high
    middle = rest.astype(BF16).astype(F32)
    return high, middle, rest - middle


def source_rows(tile):
    row = lax.broadcasted_iota(I32, (8, tile.shape[1]), 0)
    high, middle, low = three_parts(jnp.concatenate([tile, tile], axis=0))
    first = jnp.where(row == 7, middle, high)
    second = jnp.where(row == 3, low, jnp.where(row < 3, middle, high))
    second = jnp.where(row == 7, 1.0, second)
    third = jnp.where(row < 3, low, middle)
    third = jnp.where((row == 3) | (row == 7), 1.0, third)
    return jnp.concatenate([first, second, third, jnp.zeros_like(first)], axis=0).astype(BF16)


def target_rows(tile):
    row = lax.broadcasted_iota(I32, (8, tile.shape[1]), 0)
    high, middle, low = three_parts(jnp.concatenate([tile, tile], axis=0))
    first = -2.0 * jnp.where(row < 4, high, middle)
    first = jnp.where((row == 3) | (row == 7), 1.0, first)
    second = -2.0 * jnp.where(row < 4, high, low)
    second = jnp.where(row == 3, 1.0, jnp.where(row == 7, high, second))
    third = -2.0 * jnp.where(row < 4, high, middle)
    third = jnp.where(row == 3, middle, jnp.where(row == 7, low, third))
    return jnp.concatenate([first, second, third, jnp.zeros_like(first)], axis=0).astype(BF16)


def weigh(tile, target):
    squared = lax.dot_general(
        source_rows(tile), target, (((0,), (0,)), ((), ())), preferred_element_type=F32
    )
    q = 1.0 - 1.0 / squared
    weight = barrier_scale * (-2.0 * jnp.log(squared) - 4.0 * q + q * q)
    return jnp.where(squared < barrier_reach, weight, 0.0)


def pair_part(moves, weights):
    points = moves.shape[1]
    high = moves.astype(BF16).astype(F32)
    lhs = jnp.concatenate([high, moves - high], axis=0).astype(BF16)
    out = jnp.dot(lhs, weights, preferred_element_type=F32)
    return (out[0:4, :points] + out[4:8, :points]) + (out[0:4, points:] + out[4:8, points:])


def forces_one_kernel(
    got_ref, own_ref, table_ref, move_ref, next_ref,
    force_ref, sum_ref, msg_ref, target_ref, w_hbm, w_ref, acc_ref, sem,
):
    bodies = got_ref.shape[0]
    blocks, _, points = move_ref.shape
    cap = table_ref.shape[1] // bodies
    slots = cap + blocks // 2
    one = jnp.ones((1, points), F32)

    def received(d, slot):
        parts = got_ref[d, pl.ds(3 * slot, 3)]
        moves = jnp.concatenate([parts[0], parts[1, 0:1], one], axis=0)
        tile = jnp.concatenate([parts[1, 1:2], parts[2], one], axis=0)
        return moves, measured(tile, edge)

    acc_ref[...] = jnp.zeros_like(acc_ref)

    edge = lax.broadcasted_iota(I32, (4, points), 0) == 3

    def keep(d):
        return pltpu.make_async_copy(w_ref.at[d], w_hbm.at[d], sem.at[d])

    def find(d, carry):
        for s in range(cap):
            target_ref[d * cap + s] = jnp.max(
                got_ref[d, 3 * slots + s // 2, s % 2 : s % 2 + 1, :]
            ).astype(I32)
        return carry

    lax.fori_loop(0, bodies, find, 0, unroll=8)

    def device(d, carry):
        work = []
        for s in range(cap):
            n = d * cap + s
            work.append((received(d, s), target_ref[n]))
            first = table_ref[0, n]
            odd = lax.shift_right_logical(table_ref[1, n], 1)
            work.append((received(d, cap + odd), first))
        parts = []
        for k, ((moves, tile), at) in enumerate(work):
            high, low = split(weigh(tile, own_ref[at]))
            both = jnp.concatenate([high, low], axis=1)
            w_ref[d, k] = both
            parts.append(pair_part(moves, both))
        for (_, at), part in zip(work, parts):
            acc_ref[at] = acc_ref[at] + part
        keep(d).start()
        return carry

    lax.fori_loop(0, bodies, device, 0, unroll=4)
    row = lax.broadcasted_iota(I32, (4, points), 0)
    inner = jnp.zeros((4, points), F32)
    for k in range(blocks):
        acc = acc_ref[k]
        force = move_ref[k] * acc[3:4] - acc
        force_ref[k] = force
        sum_ref[k] = jnp.where(row < 3, next_ref[k] + force, 1.0)
        inner = inner + move_ref[k] * force
    inner = jnp.sum(inner[0:3], axis=0, keepdims=True)
    sum_ref[blocks] = next_ref[blocks] + jnp.where(row == 1, inner, 0.0)

    def pack(d, carry):
        for s in range(cap):
            n = d * cap + s
            msg_ref[d, s] = sum_ref[table_ref[0, n]]
            msg_ref[d, cap + s] = sum_ref[target_ref[n]]
        return carry

    lax.fori_loop(0, bodies, pack, 0)

    def finish(d, carry):
        keep(d).wait()
        return carry

    lax.fori_loop(0, bodies, finish, 0)


def scatter_parts(rows, depth, map_ref, force_ref, left_ref, right_ref):
    span = map_ref.shape[2]
    per = force_ref.shape[0] // map_ref.shape[0]
    depth_iota = lax.broadcasted_iota(I32, (depth, span), 0)
    row_iota = lax.broadcasted_iota(I32, (rows, span), 0)
    chunks = map_ref.shape[0]
    for j in range(chunks):
        row, deep = cell_parts(map_ref[j], depth)
        onehot = jnp.where(depth_iota == deep, 1.0, 0.0).astype(BF16)
        right_ref[:, j * span : (j + 1) * span] = onehot
        right_ref[:, (chunks + j) * span : (chunks + j + 1) * span] = onehot
        here = row_iota == row
        for c in range(3):
            line = jnp.concatenate(
                [force_ref[j * per + b, c : c + 1, :] for b in range(per)], axis=1
            )
            high = line.astype(BF16).astype(F32)
            at = slice(c * rows, (c + 1) * rows)
            left_ref[at, j * span : (j + 1) * span] = jnp.where(here, high, 0.0).astype(BF16)
            left_ref[at, (chunks + j) * span : (chunks + j + 1) * span] = jnp.where(
                here, line - high, 0.0
            ).astype(BF16)
    def spread(c):
        return lax.dot_general(
            left_ref[c * rows : (c + 1) * rows], right_ref[...], (((1,), (1,)), ((), ())),
            preferred_element_type=F32,
        )

    return spread


def scatter_one_kernel(
    e0_ref, e1_ref, e2_ref, face_ref, force_ref, map_ref,
    w1_ref, xe_ref, xo_ref, ye_ref, yo_ref, left_ref, right_ref,
):
    shape = e0_ref.shape
    spread = scatter_parts(shape[0] * shape[1], shape[2], map_ref, force_ref, left_ref, right_ref)
    for c, e_ref in enumerate((e0_ref, e1_ref, e2_ref)):
        w1_ref[c] = e_ref[...] + spread(c).reshape(shape)
    rows, cols, _ = shape
    for c in range(3):
        w1_ref[c, 0] = w1_ref[c, 0] + face_ref[c, 0:cols]
        w1_ref[c, rows - 1] = w1_ref[c, rows - 1] + face_ref[c, cols : 2 * cols]
        for x in range(1, rows - 1):
            for y, at in ((0, 2 * cols + x), (cols - 1, 2 * cols + rows + x)):
                w1_ref[c, x, y : y + 1] = w1_ref[c, x, y : y + 1] + face_ref[c, at : at + 1]
    write_faces([(w1_ref, 0), (w1_ref, 1), (w1_ref, 2)], xe_ref, xo_ref, ye_ref, yo_ref)


def scatter_two_kernel(
    e_ref, force_ref, map_ref, r_hbm, w2_ref, r_ref, left_ref, right_ref, sem
):
    copy = pltpu.make_async_copy(r_hbm, r_ref, sem)
    copy.start()
    shape = e_ref.shape[1:]
    spread = scatter_parts(shape[0] * shape[1], shape[2], map_ref, force_ref, left_ref, right_ref)
    for c in range(3):
        w2_ref[c] = e_ref[c] + spread(c).reshape(shape)
    copy.wait()


def elastic(v_ref, sh_ref, la_ref, in_ref, vector_halo, stiff_halo, emit, at_shear=3):
    rows, cols, depth = sh_ref.shape
    b, a = lax.axis_index("body"), lax.axis_index("across")
    bodies, acrosses = lax.axis_size("body"), lax.axis_size("across")
    bpar, apar = lax.rem(b, 2), lax.rem(a, 2)
    cut = bodies // 4
    x_low = jnp.where(b != 0, 1.0, 0.0).astype(F32)
    x_high = jnp.where(b != bodies - 1, 1.0, 0.0).astype(F32)
    keep_low = jnp.where(b != cut, 1.0, 0.0).astype(F32)
    keep_high = jnp.where(b + 1 != cut, 1.0, 0.0).astype(F32)
    y_low = jnp.where(a != 0, 1.0, 0.0).astype(F32)
    y_high = jnp.where(a != acrosses - 1, 1.0, 0.0).astype(F32)
    inner = vector_halo is None
    vxe, vxo, vye, vyo = (None,) * 4 if inner else vector_halo
    sxe, sxo, sye, syo = (None,) * 4 if inner else stiff_halo
    row = lax.broadcasted_iota(I32, (cols, depth), 0)
    lane = lax.broadcasted_iota(I32, (cols, depth), 1)
    z_mask = jnp.where(lane == depth - 1, 0.0, 1.0)
    start = lane == 0
    top = row == cols - 1
    bottom = row == 0

    def stiffness(shear, lame):
        return 0.5 * shear, shear + 0.5 * lame

    def pick(parity, even, odd):
        return jnp.where(parity == 0, even, odd)

    def x_halo(high):
        e, o = (sxe, sxo) if high else (sxo, sxe)
        there = x_high if high else x_low
        shear, lame = pick(bpar, e[at_shear], o[at_shear]), pick(bpar, e[at_shear + 1], o[at_shear + 1])
        e, o = (vxe, vxo) if high else (vxo, vxe)
        values = [there * pick(bpar, e[c], o[c]) for c in range(3)]
        return stiffness(there * shear, there * lame), values

    def y_halo(high, x):
        e, o = (sye, syo) if high else (syo, sye)
        there = y_high if high else y_low
        at = slice(x, x + 1)
        shear, lame = pick(apar, e[at_shear, at], o[at_shear, at]), pick(apar, e[at_shear + 1, at], o[at_shear + 1, at])
        e, o = (vye, vyo) if high else (vyo, vye)
        values = [there * pick(apar, e[c, at], o[c, at]) for c in range(3)]
        return stiffness(there * shear, there * lame), values

    def slab(x):
        return stiffness(sh_ref[x], la_ref[x]), [v_ref[c, x] for c in range(3)]

    def flux(near, far, along, mask):
        (off, diag), values = near
        (far_off, far_diag), far_values = far
        side, front = off + far_off, diag + far_diag
        if mask is not None:
            side, front = side * mask, front * mask
        return [
            (front if c == along else side) * (values[c] - far_values[c]) for c in range(3)
        ]

    if in_ref is None:

        def edge_rows(ref, y, lead=None):
            at = (lambda x: ref[x, y : y + 1]) if lead is None else (lambda x: ref[lead, x, y : y + 1])
            return jnp.concatenate([at(x) for x in range(rows)], axis=0)

        def near(y):
            stiff = stiffness(edge_rows(sh_ref, y), edge_rows(la_ref, y))
            return stiff, [edge_rows(v_ref, y, c) for c in range(3)]

        def far(high):
            there = y_high if high else y_low
            e, o = (sye, syo) if high else (syo, sye)
            shear, lame = pick(apar, e[at_shear], o[at_shear]), pick(apar, e[at_shear + 1], o[at_shear + 1])
            e, o = (vye, vyo) if high else (vyo, vye)
            return stiffness(there * shear, there * lame), [there * pick(apar, e[c], o[c]) for c in range(3)]

        x_first = [-value for value in flux(x_halo(False), slab(0), 0, keep_low)]
        x_last = flux(slab(rows - 1), x_halo(True), 0, keep_high)
        y_first, y_last = flux(near(0), far(False), 1, None), flux(near(cols - 1), far(True), 1, None)

        def joined(value, c, x):
            value = value + jnp.where(bottom, y_first[c][x : x + 1], 0.0)
            return value + jnp.where(top, y_last[c][x : x + 1], 0.0)

        x_first = [joined(x_first[c], c, 0) for c in range(3)]
        x_last = [joined(x_last[c], c, rows - 1) for c in range(3)]
        return x_first, x_last, y_first, y_last

    before = None if inner else flux(x_halo(False), slab(0), 0, keep_low)
    here = slab(0)
    for x in range(rows):
        out = after = None
        if x + 1 < rows or not inner:
            after = slab(x + 1) if x + 1 < rows else x_halo(True)
            out = flux(here, after, 0, None if x + 1 < rows else keep_high)
        (off, diag), values = here
        inertia = in_ref[x]
        total = [inertia * values[c] for c in range(3)]
        if out is not None:
            total = [total[c] + out[c] for c in range(3)]
        if before is not None:
            total = [total[c] - before[c] for c in range(3)]
        before = out

        def up(value, edge):
            return jnp.where(top, edge, pltpu.roll(value, cols - 1, 0))

        if inner:

            def down(value):
                return pltpu.roll(value, cols - 1, 0)

            shifted = (down(off), down(diag)), [down(values[c]) for c in range(3)]
            out = [jnp.where(top, 0.0, value) for value in flux(here, shifted, 1, None)]
            total = [total[c] + (out[c] - pltpu.roll(out[c], 1, 0)) for c in range(3)]
        else:
            (h_off, h_diag), h_values = y_halo(True, x)
            shifted = (up(off, h_off), up(diag, h_diag)), [
                up(values[c], h_values[c]) for c in range(3)
            ]
            out = flux(here, shifted, 1, None)
            first = (off[0:1], diag[0:1]), [values[c][0:1] for c in range(3)]
            edge = flux(y_halo(False, x), first, 1, None)
            total = [
                total[c] + (out[c] - jnp.where(bottom, edge[c], pltpu.roll(out[c], 1, 0)))
                for c in range(3)
            ]

        def right(value):
            return z_mask * pltpu.roll(value, depth - 1, 1)

        shifted = (right(off), right(diag)), [right(values[c]) for c in range(3)]
        out = flux(here, shifted, 2, None)
        edge = [-(diag if c == 2 else off) * values[c] for c in range(3)]
        total = [
            total[c] + (out[c] - jnp.where(start, edge[c], pltpu.roll(out[c], 1, 1)))
            for c in range(3)
        ]
        emit(x, total)
        here = after


def stencil_one_kernel(
    r_ref, sh_ref, la_ref, in_ref, map_ref,
    e0_ref, e1_ref, e2_ref, next_ref, both_ref,
):
    e_refs = (e0_ref, e1_ref, e2_ref)
    sums = [jnp.zeros((8, 128), F32) for _ in range(2)]

    def emit(x, total):
        for c in range(3):
            e_refs[c][x] = total[c]
            r = r_ref[c, x]
            sums[0] = sums[0] + fold(r * r)
            sums[1] = sums[1] + fold(r * total[c])

    elastic(r_ref, sh_ref, la_ref, in_ref, None, None, emit)
    rows, depth = e0_ref.shape[0] * e0_ref.shape[1], e0_ref.shape[2]
    points = next_ref.shape[2]

    def write(j, c, line):
        per = line.shape[1] // points
        for b in range(per):
            next_ref[j * per + b, c : c + 1, :] = line[:, b * points : (b + 1) * points]

    blocks = next_ref.shape[0] - 1
    for k in range(blocks):
        next_ref[k, 3:4, :] = jnp.zeros((1, points), F32)
    lines = [jnp.sum(value, axis=0, keepdims=True) for value in sums]
    next_ref[blocks] = jnp.concatenate(lines + [jnp.zeros((2, points), F32)], axis=0)
    gather_into(lambda c: e_refs[c][...].reshape(rows, depth), rows, depth, map_ref, both_ref, write)


def faces_one_kernel(
    r_ref, sh_ref, la_ref, xe, xo, ye, yo, map_ref, inner_ref,
    face_ref, next_ref, sxe, sxo, sye, syo, both_ref,
):
    _, rows, cols, depth = r_ref.shape
    halo = (xe, xo, ye, yo)
    for source, target in zip(halo, (sxe, sxo, sye, syo)):
        for k in range(2):
            target[k] = source[3 + k]
    x_first, x_last, y_first, y_last = elastic(r_ref, sh_ref, la_ref, None, halo, halo, None)
    blocks, points = next_ref.shape[0] - 1, next_ref.shape[2]
    between = lax.broadcasted_iota(I32, (rows, depth), 0)
    between = (between > 0) & (between < rows - 1)
    product = jnp.zeros((1, 128), F32)
    for c in range(3):
        face_ref[c, 0:cols] = x_first[c]
        face_ref[c, cols : 2 * cols] = x_last[c]
        face_ref[c, 2 * cols : 2 * cols + rows] = y_first[c]
        face_ref[c, 2 * cols + rows :] = y_last[c]
        ends = r_ref[c, 0] * x_first[c] + r_ref[c, rows - 1] * x_last[c]
        low = jnp.concatenate([r_ref[c, x, 0:1] for x in range(rows)], axis=0)
        high = jnp.concatenate([r_ref[c, x, cols - 1 : cols] for x in range(rows)], axis=0)
        sides = jnp.where(between, low * y_first[c] + high * y_last[c], 0.0)
        for value in (ends, sides):
            line = jnp.sum(value, axis=0, keepdims=True)
            for k in range(depth // 128):
                product = product + line[:, k * 128 : (k + 1) * 128]

    def place(row):
        x, y = cell_parts(row, cols)
        at = jnp.where(y == cols - 1, 2 * cols + rows + x, -1)
        at = jnp.where(y == 0, 2 * cols + x, at)
        at = jnp.where(x == rows - 1, cols + y, at)
        return jnp.where(x == 0, y, at)

    def write(j, c, line):
        per = line.shape[1] // points
        for b in range(per):
            k = j * per + b
            next_ref[k, c : c + 1, :] = inner_ref[k, c : c + 1, :] + line[:, b * points : (b + 1) * points]

    for k in range(blocks):
        next_ref[k, 3:4, :] = jnp.zeros((1, points), F32)
    line = lax.broadcasted_iota(I32, (4, points), 0)
    next_ref[blocks] = inner_ref[blocks] + jnp.where(line == 1, product, 0.0)
    gather_into(
        lambda c: face_ref[c], face_ref.shape[1], depth, map_ref, both_ref, write, place
    )


def fold(value):
    cols, depth = value.shape
    total = None
    for k in range(depth // 128):
        part = value[:, k * 128 : (k + 1) * 128]
        part = jnp.sum(part.reshape(cols // 8, 8, 128), axis=0)
        total = part if total is None else total + part
    return total


def forces_two_kernel(
    got_ref, target_ref, table_ref, move_ref, w_hbm, sh_hbm, la_hbm, in_hbm_ref,
    force_ref, dots_ref, sh_ref, la_ref, in_ref, w_ref, acc_ref, sem, cell_sem,
):
    bodies, width = got_ref.shape[0], got_ref.shape[1]
    cap = width // 2
    blocks, points = move_ref.shape[0] - 1, move_ref.shape[2]

    def fetch(d):
        return pltpu.make_async_copy(w_hbm.at[d], w_ref.at[d], sem.at[d])

    def begin(d, carry):
        fetch(d).start()
        return carry

    lax.fori_loop(0, bodies, begin, 0)
    cells = [
        pltpu.make_async_copy(source, target, cell_sem.at[k])
        for k, (source, target) in enumerate(
            [(sh_hbm, sh_ref), (la_hbm, la_ref), (in_hbm_ref, in_ref)]
        )
    ]
    for copy in cells:
        copy.start()
    acc_ref[...] = jnp.zeros_like(acc_ref)

    def device(d, carry):
        fetch(d).wait()
        work = []
        for s in range(cap):
            n = d * cap + s
            work.append((target_ref[n], pair_part(got_ref[d, s], w_ref[d, 2 * s])))
            work.append((table_ref[0, n], pair_part(got_ref[d, cap + s], w_ref[d, 2 * s + 1])))
        for at, part in work:
            acc_ref[at] = acc_ref[at] + part
        return carry

    lax.fori_loop(0, bodies, device, 0)
    inner = jnp.zeros((4, points), F32)
    for k in range(blocks):
        acc = acc_ref[k]
        moved = move_ref[k]
        force = moved * acc[3:4] - acc
        force_ref[k] = force
        inner = inner + moved * force
    inner = jnp.sum(inner[0:3], axis=0, keepdims=True)
    blank = jnp.zeros_like(inner)
    dots_ref[...] = jnp.concatenate([move_ref[blocks][0:2], blank, inner], axis=0)
    for copy in cells:
        copy.wait()


def stencil_two_kernel(
    w1_ref, sh_ref, la_ref, in_ref, xe, xo, ye, yo, cxe, cxo, cye, cyo, dots_ref, e_ref, red_ref
):
    sums = [jnp.zeros((8, 128), F32) for _ in range(2)]

    def emit(x, total):
        for c in range(3):
            e_ref[c, x] = total[c]
            w = w1_ref[c, x]
            sums[0] = sums[0] + fold(w * w)
            sums[1] = sums[1] + fold(w * total[c])

    elastic(w1_ref, sh_ref, la_ref, in_ref, (xe, xo, ye, yo), (cxe, cxo, cye, cyo), emit, 0)
    lines = [jnp.sum(value, axis=0, keepdims=True) for value in sums]
    blank = jnp.zeros_like(lines[0])
    line = dots_ref[...] + jnp.concatenate([blank, blank] + lines, axis=0)
    for d in range(red_ref.shape[0]):
        red_ref[d] = line


def final_kernel(r_ref, w1_ref, w2_ref, red_ref, x_hbm, res_hbm, x_ref, res_ref, sem):
    line = jnp.sum(red_ref[...], axis=0)
    moment = [
        jnp.broadcast_to(jnp.sum(line[k : k + 1], axis=1, keepdims=True), (8, 128)) for k in range(4)
    ]
    m0, m1, m2, m3 = moment
    step = m0 / m1
    norm = (m0 - step * m1) + step * (step * m2 - m1)
    ratio = norm / m0
    grown = 1.0 + ratio
    curve = grown * (grown * m1 - 2.0 * step * m2) + step * step * m3
    next_step = norm / curve
    alpha = step + next_step * grown
    gamma = next_step * step
    cols, depth = r_ref.shape[2], r_ref.shape[3]
    alpha = jnp.broadcast_to(alpha[0:1, 0:1], (cols, depth))
    gamma = jnp.broadcast_to(gamma[0:1, 0:1], (cols, depth))
    copies = []
    for c in range(3):
        for x in range(r_ref.shape[1]):
            r, w1 = r_ref[c, x], w1_ref[c, x]
            x_ref[c, x] = alpha * r - gamma * w1
            res_ref[c, x] = r - alpha * w1 + gamma * w2_ref[c, x]
        copies.append(pltpu.make_async_copy(x_ref.at[c], x_hbm.at[c], sem.at[0, c]))
        copies.append(pltpu.make_async_copy(res_ref.at[c], res_hbm.at[c], sem.at[1, c]))
        for copy in copies[-2:]:
            copy.start()
    for copy in copies:
        copy.wait()


def exchange(xe, xo, ye, yo):
    def pairs(axis, start):
        count = lax.axis_size(axis)
        chosen = []
        for i in range(count):
            partner = i + 1 if (i - start) % 2 == 0 else i - 1
            chosen.append((i, partner % count))
        return chosen

    got_xo = lax.ppermute(xo, "body", pairs("body", 1))
    got_xe = lax.ppermute(xe, "body", pairs("body", 0))
    got_yo = lax.ppermute(yo, "across", pairs("across", 1))
    got_ye = lax.ppermute(ye, "across", pairs("across", 0))
    return (
        got_xe, got_xo, got_ye, got_yo
    )


def on_device(
    cotangent, shear, lame, inertia, surface_points, point_counts, surface_maps, contact_pairs
):
    rows, cols, depth = shear.shape
    points = jnp.transpose(surface_points[0, 0], (1, 0, 2))
    counts = point_counts[0, 0]
    cell_maps = surface_maps[0, 0]
    pair_table = contact_pairs[0, 0][:, None, :]
    _, blocks, width = points.shape
    pairs = pair_table.shape[2]
    bodies, acrosses = lax.axis_size("body"), lax.axis_size("across")
    devices = bodies * acrosses
    cap = pairs // bodies
    slots = cap + blocks // 2
    chunks = blocks // 2
    cell_maps = cell_maps.reshape(chunks, 1, 2 * width)
    flat = rows * cols
    vector = sds((3, rows, cols, depth))

    def faces(count):
        return (
            sds((count, cols, depth)), sds((count, cols, depth)),
            sds((count, rows, depth)), sds((count, rows, depth)),
        )

    moves = sds((blocks, 4, width))
    both = pltpu.VMEM((3 * flat, 2 * depth), BF16)
    wide = 2 * blocks * width
    sides = (pltpu.VMEM((3 * flat, wide), BF16), pltpu.VMEM((depth, wide), BF16))
    total = pltpu.VMEM((blocks, 4, width), F32)
    kept = (bodies, 2 * cap, width, 2 * width)
    kept_mib = 10 + (8 * pairs * width * width >> 20) + (bodies >> 2)
    dma = pltpu.SemaphoreType.DMA
    cells = (sds((rows, cols, depth)),) * 3

    given = (shear, lame, inertia)
    r, shear, lame, inertia, cell_maps, xe, xo, ye, yo, own, first_moves, message, table = call(
        open_kernel, "open", [HBM] * 8, [VMEM] * 12 + [SMEM],
        (vector,) + cells + (sds(cell_maps.shape, I32),) + faces(5)
        + (sds((blocks, 32, width), BF16), moves)
        + (sds((bodies, 3 * slots + (cap + 1) // 2, 2, width)), sds((2, pairs), I32)),
        scratch=(
            pltpu.VMEM(points.shape, F32), pltpu.SMEM(counts.shape, I32),
            pltpu.SMEM(pair_table.shape, I32), pltpu.SMEM((bodies,), I32),
            pltpu.VMEM((blocks, 3, 2, width), F32), both, dma((10,)),
        ), cost=4.0,
    )(*in_hbm(cotangent, shear, lame, inertia, points, counts, pair_table, cell_maps))
    got = lax.all_to_all(message, "body", 0, 0, tiled=True)
    halo = exchange(xe, xo, ye, yo)
    grown = sds((blocks + 1, 4, width))
    *elastic_one, inner_moves = call(
        stencil_one_kernel, "stencil_one", [VMEM] * 5, [VMEM] * 4, cells + (grown,),
        scratch=(both,), cost=5.0,
    )(r, shear, lame, inertia, cell_maps)
    rim = 2 * (rows + cols)
    face_one, next_moves, *stiff = call(
        faces_one_kernel, "faces_one", [VMEM] * 9, [VMEM] * 6,
        (sds((3, rim, depth)), grown) + faces(2),
        scratch=(pltpu.VMEM((3 * rim, 2 * depth), BF16),), cost=1.0,
    )(r, shear, lame, *halo, cell_maps, inner_moves)
    force_one, second_moves, message, targets, weights = call(
        forces_one_kernel, "forces_one", [VMEM] * 2 + [SMEM] + [VMEM] * 2,
        [VMEM] * 3 + [SMEM, HBM],
        (moves, grown, sds((bodies, 2 * cap, 4, width)), sds((pairs,), I32), pltpu.HBM(kept, BF16)),
        scratch=(pltpu.VMEM(kept, BF16), total, dma((bodies,))), cost=6.0, mib=kept_mib,
    )(got, own, table, first_moves, next_moves)
    got = lax.all_to_all(message, "body", 0, 0, tiled=True)
    w1, xe, xo, ye, yo = call(
        scatter_one_kernel, "scatter_one", [VMEM] * 6, [VMEM] * 5, (vector,) + faces(3),
        scratch=sides, cost=3.0, mib=16,
    )(*elastic_one, face_one, force_one, cell_maps)
    halo_two = exchange(xe, xo, ye, yo)
    force_two, dots, shear, lame, inertia = call(
        forces_two_kernel, "forces_two", [VMEM] + [SMEM] * 2 + [VMEM] + [HBM] * 4, [VMEM] * 5,
        (moves, sds((4, 128))) + cells,
        scratch=(pltpu.VMEM(kept, BF16), total, dma((bodies,)), dma((3,))), cost=3.0, mib=kept_mib,
    )(got, targets, table, second_moves, *in_hbm(weights, *given))
    elastic_two, partial = call(
        stencil_two_kernel, "stencil_two", [VMEM] * 13, [VMEM] * 2, (vector, sds((devices, 4, 128))),
        cost=1.5,
    )(w1, shear, lame, inertia, *halo_two, *stiff, dots)
    sums = lax.all_to_all(partial, ("body", "across"), 0, 0, tiled=True)
    w2, r = call(
        scatter_two_kernel, "scatter_two", [VMEM] * 3 + [HBM], [VMEM] * 2, (vector, vector),
        scratch=sides + (dma(()),), cost=3.0, mib=16,
    )(elastic_two, force_two, cell_maps, *in_hbm(cotangent))
    out = pltpu.VMEM((3, rows, cols, depth), F32)
    return call(
        final_kernel, "final", [VMEM] * 4, [HBM] * 2, (vector, vector),
        scratch=(out, out, dma((2, 3))), cost=1.0,
    )(r, w1, w2, sums)


def solution(mesh):
    placed = (
        P(None, "body", "across", None),
        P("body", "across", None),
        P("body", "across", None),
        P("body", "across", None),
        P("body", "across", None, None, None),
        P("body", "across", None),
        P("body", "across", None, None),
        P("body", "across", None, None),
    )
    return jax.shard_map(
        on_device,
        mesh=mesh,
        in_specs=placed,
        out_specs=(P(None, "body", "across", None), P(None, "body", "across", None)),
        check_vma=False,
    )
```

```python
import jax
import jax.numpy as jnp
from jax import lax
from jax.experimental import pallas as pl
from jax.experimental.pallas import tpu as pltpu
from jax.sharding import PartitionSpec as P

F32 = jnp.float32
BF16 = jnp.bfloat16
I32 = jnp.int32

barrier_reach = 1.0
barrier_scale = 0.005
FAR = 1000.0

VMEM = pl.BlockSpec(memory_space=pltpu.VMEM)
SMEM = pl.BlockSpec(memory_space=pltpu.SMEM)
HBM = pl.BlockSpec(memory_space=pltpu.HBM)


def sds(shape, dtype=F32):
    return jax.ShapeDtypeStruct(shape, dtype)


def call(body, name, in_specs, out_specs, out_shape, scratch=(), cost=2.0, mib=8):
    estimate = pl.CostEstimate(flops=int(cost * 1e8), transcendentals=0, bytes_accessed=int(cost * 3e6))
    return pl.pallas_call(
        body,
        name=name,
        in_specs=in_specs,
        out_specs=out_specs,
        out_shape=out_shape,
        scratch_shapes=list(scratch),
        cost_estimate=estimate,
        compiler_params=pltpu.CompilerParams(vmem_limit_bytes=mib << 20),
    )


def in_hbm(*arrays):
    return tuple(pltpu.with_memory_space_constraint(array, pltpu.HBM) for array in arrays)


def split(values):
    high = values.astype(BF16)
    low = (values - high.astype(F32)).astype(BF16)
    return high, low


def even_faces(block, axis_parity, last):
    first = jnp.where(axis_parity == 0, last, 0)
    return first, last - first


def write_faces(sources, xe_ref, xo_ref, ye_ref, yo_ref):
    bpar = lax.rem(lax.axis_index("body"), 2)
    apar = lax.rem(lax.axis_index("across"), 2)
    for k, (ref, lead) in enumerate(sources):
        at = (lambda x: ref[lead, x]) if lead is not None else (lambda x: ref[x])
        rows = ref.shape[-3]
        cols = ref.shape[-2]
        xi = jnp.where(bpar == 0, rows - 1, 0)
        xe_ref[k] = at(xi)
        xo_ref[k] = at(rows - 1 - xi)
        for x in range(rows):
            slab = at(x)
            low = slab[0:1]
            high = slab[cols - 1 : cols]
            ye_ref[k, x : x + 1] = jnp.where(apar == 0, high, low)
            yo_ref[k, x : x + 1] = jnp.where(apar == 0, low, high)


def cell_parts(cells, depth):
    if depth & (depth - 1) == 0:
        shift = depth.bit_length() - 1
        return lax.shift_right_logical(cells, shift), jnp.bitwise_and(cells, depth - 1)
    row = cells // depth
    return row, cells - row * depth


def gather_into(load, rows, depth, map_ref, both_ref, write, place=None):
    for c in range(3):
        high, low = split(load(c))
        both_ref[c * rows : (c + 1) * rows, 0:depth] = high
        both_ref[c * rows : (c + 1) * rows, depth:] = low
    chunks, _, span = map_ref.shape
    depth_iota = lax.broadcasted_iota(I32, (depth, span), 0)
    row_iota = lax.broadcasted_iota(I32, (rows, span), 0)

    def chunk(j, carry):
        row, deep = cell_parts(map_ref[j], depth)
        onehot = jnp.where(depth_iota == deep, 1.0, 0.0).astype(BF16)
        onehot = jnp.concatenate([onehot, onehot], axis=0)
        row = row if place is None else place(row)
        picked = jnp.dot(both_ref[...], onehot, preferred_element_type=F32)
        here = row_iota == row
        for c in range(3):
            part = jnp.where(here, picked[c * rows : (c + 1) * rows], 0.0)
            write(j, c, jnp.sum(part, axis=0, keepdims=True))
        return carry

    lax.fori_loop(0, chunks, chunk, 0, unroll=8)


def open_kernel(
    r_hbm, sh_hbm, la_hbm, in_hbm, pt_hbm, cnt_hbm, pair_hbm, map_hbm,
    r_ref, sh_ref, la_ref, in_ref, map_ref,
    xe_ref, xo_ref, ye_ref, yo_ref, own_ref, move_ref, msg_ref, table_ref,
    pt_ref, cnt_ref, pair_ref, fill_ref, sent_ref, both_ref, sem,
):
    copies = [
        pltpu.make_async_copy(source, target, sem.at[k])
        for k, (source, target) in enumerate([
            (cnt_hbm, cnt_ref), (pair_hbm, pair_ref), (pt_hbm, pt_ref), (map_hbm, map_ref),
            (r_hbm.at[0], r_ref.at[0]), (r_hbm.at[1], r_ref.at[1]), (r_hbm.at[2], r_ref.at[2]),
            (sh_hbm, sh_ref), (la_hbm, la_ref), (in_hbm, in_ref),
        ])
    ]
    for copy in copies:
        copy.start()
    bodies = msg_ref.shape[0]
    blocks = own_ref.shape[0]
    odd_total = blocks // 2
    pairs = table_ref.shape[1]
    cap = pairs // bodies
    slots = cap + odd_total
    points = own_ref.shape[2]
    lane = lax.broadcasted_iota(I32, (1, points), 1)
    edge = lax.broadcasted_iota(I32, (4, points), 0) == 3
    for copy in copies[:4]:
        copy.wait()
    for d in range(bodies):
        fill_ref[d] = 0

    def place(n, carry):
        dest = pair_ref[1, 0, n]
        rank = fill_ref[dest]
        fill_ref[dest] = rank + 1
        table_ref[0, dest * cap + rank] = pair_ref[0, 0, n]
        table_ref[1, dest * cap + rank] = pair_ref[2, 0, n]
        return carry

    lax.fori_loop(0, pairs, place, 0)
    blank = jnp.zeros((1, points), F32)
    for k in range(blocks):
        tile = jnp.concatenate([pt_ref[c, k : k + 1, :] for c in range(3)] + [blank], axis=0)
        own_ref[k] = measured(jnp.where(lane < cnt_ref[k], tile, -FAR), edge)
        tile = jnp.where(lane < cnt_ref[k], tile, FAR)
        sent_ref[k, 1, 1:2, :] = tile[0:1]
        sent_ref[k, 2] = tile[1:3]
        move_ref[k, 3:4, :] = blank + 1.0
    for copy in copies[4:]:
        copy.wait()
    rows, depth = r_ref.shape[1] * r_ref.shape[2], r_ref.shape[3]

    def write(j, c, line):
        per = line.shape[1] // points
        for b in range(per):
            part = line[:, b * points : (b + 1) * points]
            move_ref[j * per + b, c : c + 1, :] = part
            sent_ref[j * per + b, c // 2, c % 2 : c % 2 + 1, :] = part

    gather_into(lambda c: r_ref[c].reshape(rows, depth), rows, depth, map_ref, both_ref, write)

    def pack(d, carry):
        for s in range(cap):
            second = table_ref[1, d * cap + s].astype(F32)
            msg_ref[d, 3 * s : 3 * s + 3] = sent_ref[table_ref[0, d * cap + s]]
            msg_ref[d, 3 * slots + s // 2, s % 2 : s % 2 + 1, :] = jnp.full((1, points), second)
        for j in range(odd_total):
            msg_ref[d, 3 * (cap + j) : 3 * (cap + j) + 3] = sent_ref[2 * j + 1]
        return carry

    lax.fori_loop(0, bodies, pack, 0)
    sources = [(r_ref, 0), (r_ref, 1), (r_ref, 2), (sh_ref, None), (la_ref, None)]
    write_faces(sources, xe_ref, xo_ref, ye_ref, yo_ref)


def measured(tile, edge):
    square = jnp.where(edge, 0.0, tile * tile)
    return jnp.where(edge, jnp.sum(square, axis=0, keepdims=True), tile)


def three_parts(value):
    high = value.astype(BF16).astype(F32)
    rest = value - high
    middle = rest.astype(BF16).astype(F32)
    return high, middle, rest - middle


def source_rows(tile):
    row = lax.broadcasted_iota(I32, (8, tile.shape[1]), 0)
    high, middle, low = three_parts(jnp.concatenate([tile, tile], axis=0))
    first = jnp.where(row == 7, middle, high)
    second = jnp.where(row == 3, low, jnp.where(row < 3, middle, high))
    second = jnp.where(row == 7, 1.0, second)
    third = jnp.where(row < 3, low, middle)
    third = jnp.where((row == 3) | (row == 7), 1.0, third)
    return jnp.concatenate([first, second, third, jnp.zeros_like(first)], axis=0).astype(BF16)


def target_rows(tile):
    row = lax.broadcasted_iota(I32, (8, tile.shape[1]), 0)
    high, middle, low = three_parts(jnp.concatenate([tile, tile], axis=0))
    first = -2.0 * jnp.where(row < 4, high, middle)
    first = jnp.where((row == 3) | (row == 7), 1.0, first)
    second = -2.0 * jnp.where(row < 4, high, low)
    second = jnp.where(row == 3, 1.0, jnp.where(row == 7, high, second))
    third = -2.0 * jnp.where(row < 4, high, middle)
    third = jnp.where(row == 3, middle, jnp.where(row == 7, low, third))
    return jnp.concatenate([first, second, third, jnp.zeros_like(first)], axis=0).astype(BF16)


def weigh(tile, target):
    squared = lax.dot_general(
        source_rows(tile), target, (((0,), (0,)), ((), ())), preferred_element_type=F32
    )
    q = 1.0 - 1.0 / squared
    weight = barrier_scale * (-2.0 * jnp.log(squared) - 4.0 * q + q * q)
    return jnp.where(squared < barrier_reach, weight, 0.0)


def pair_part(moves, weights):
    points = moves.shape[1]
    high = moves.astype(BF16).astype(F32)
    lhs = jnp.concatenate([high, moves - high], axis=0).astype(BF16)
    out = jnp.dot(lhs, weights, preferred_element_type=F32)
    return (out[0:4, :points] + out[4:8, :points]) + (out[0:4, points:] + out[4:8, points:])


def forces_one_kernel(
    got_ref, own_ref, table_ref, move_ref, next_ref,
    force_ref, sum_ref, msg_ref, target_ref, w_hbm, w_ref, acc_ref, right_ref, sem,
):
    bodies = got_ref.shape[0]
    blocks, _, points = move_ref.shape
    cap = table_ref.shape[1] // bodies
    slots = cap + blocks // 2
    one = jnp.ones((1, points), F32)

    def received(d, slot):
        parts = got_ref[d, pl.ds(3 * slot, 3)]
        moves = jnp.concatenate([parts[0], parts[1, 0:1], one], axis=0)
        tile = jnp.concatenate([parts[1, 1:2], parts[2], one], axis=0)
        return moves, measured(tile, edge)

    for k in range(blocks):
        right_ref[k] = target_rows(own_ref[k])
    acc_ref[...] = jnp.zeros_like(acc_ref)

    edge = lax.broadcasted_iota(I32, (4, points), 0) == 3

    def keep(d):
        return pltpu.make_async_copy(w_ref.at[d], w_hbm.at[d], sem.at[d])

    def find(d, carry):
        for s in range(cap):
            target_ref[d * cap + s] = jnp.max(
                got_ref[d, 3 * slots + s // 2, s % 2 : s % 2 + 1, :]
            ).astype(I32)
        return carry

    lax.fori_loop(0, bodies, find, 0, unroll=8)

    def device(d, carry):
        work = []
        for s in range(cap):
            n = d * cap + s
            work.append((received(d, s), target_ref[n]))
            first = table_ref[0, n]
            odd = lax.shift_right_logical(table_ref[1, n], 1)
            work.append((received(d, cap + odd), first))
        parts = []
        for k, ((moves, tile), at) in enumerate(work):
            high, low = split(weigh(tile, right_ref[at]))
            both = jnp.concatenate([high, low], axis=1)
            w_ref[d, k] = both
            parts.append(pair_part(moves, both))
        for (_, at), part in zip(work, parts):
            acc_ref[at] = acc_ref[at] + part
        keep(d).start()
        return carry

    lax.fori_loop(0, bodies, device, 0, unroll=4)
    row = lax.broadcasted_iota(I32, (4, points), 0)
    inner = jnp.zeros((4, points), F32)
    for k in range(blocks):
        acc = acc_ref[k]
        force = move_ref[k] * acc[3:4] - acc
        force_ref[k] = force
        sum_ref[k] = jnp.where(row < 3, next_ref[k] + force, 1.0)
        inner = inner + move_ref[k] * force
    inner = jnp.sum(inner[0:3], axis=0, keepdims=True)
    sum_ref[blocks] = next_ref[blocks] + jnp.where(row == 1, inner, 0.0)

    def pack(d, carry):
        for s in range(cap):
            n = d * cap + s
            msg_ref[d, s] = sum_ref[table_ref[0, n]]
            msg_ref[d, cap + s] = sum_ref[target_ref[n]]
        return carry

    lax.fori_loop(0, bodies, pack, 0)

    def finish(d, carry):
        keep(d).wait()
        return carry

    lax.fori_loop(0, bodies, finish, 0)


def scatter_parts(rows, depth, map_ref, force_ref, left_ref, right_ref):
    span = map_ref.shape[2]
    per = force_ref.shape[0] // map_ref.shape[0]
    depth_iota = lax.broadcasted_iota(I32, (depth, span), 0)
    row_iota = lax.broadcasted_iota(I32, (rows, span), 0)
    chunks = map_ref.shape[0]
    for j in range(chunks):
        row, deep = cell_parts(map_ref[j], depth)
        onehot = jnp.where(depth_iota == deep, 1.0, 0.0).astype(BF16)
        right_ref[:, j * span : (j + 1) * span] = onehot
        right_ref[:, (chunks + j) * span : (chunks + j + 1) * span] = onehot
        here = row_iota == row
        for c in range(3):
            line = jnp.concatenate(
                [force_ref[j * per + b, c : c + 1, :] for b in range(per)], axis=1
            )
            high = line.astype(BF16).astype(F32)
            at = slice(c * rows, (c + 1) * rows)
            left_ref[at, j * span : (j + 1) * span] = jnp.where(here, high, 0.0).astype(BF16)
            left_ref[at, (chunks + j) * span : (chunks + j + 1) * span] = jnp.where(
                here, line - high, 0.0
            ).astype(BF16)
    def spread(c):
        return lax.dot_general(
            left_ref[c * rows : (c + 1) * rows], right_ref[...], (((1,), (1,)), ((), ())),
            preferred_element_type=F32,
        )

    return spread


def scatter_one_kernel(
    e0_ref, e1_ref, e2_ref, face_ref, force_ref, map_ref, sh_hbm, la_hbm, in_hbm_ref,
    w1_ref, xe_ref, xo_ref, ye_ref, yo_ref, sh_ref, la_ref, in_ref, left_ref, right_ref, sem,
):
    cells = [
        pltpu.make_async_copy(source, target, sem.at[k])
        for k, (source, target) in enumerate(
            [(sh_hbm, sh_ref), (la_hbm, la_ref), (in_hbm_ref, in_ref)]
        )
    ]
    for copy in cells:
        copy.start()
    shape = e0_ref.shape
    spread = scatter_parts(shape[0] * shape[1], shape[2], map_ref, force_ref, left_ref, right_ref)
    for c, e_ref in enumerate((e0_ref, e1_ref, e2_ref)):
        w1_ref[c] = e_ref[...] + spread(c).reshape(shape)
    add_faces(w1_ref, face_ref)
    write_faces([(w1_ref, 0), (w1_ref, 1), (w1_ref, 2)], xe_ref, xo_ref, ye_ref, yo_ref)
    for copy in cells:
        copy.wait()


def scatter_two_kernel(
    e_ref, face_ref, force_ref, map_ref, r_hbm,
    w2_ref, r0_ref, r1_ref, r2_ref, left_ref, right_ref, sem,
):
    copies = [
        pltpu.make_async_copy(r_hbm.at[c], target, sem.at[c])
        for c, target in enumerate((r0_ref, r1_ref, r2_ref))
    ]
    for copy in copies:
        copy.start()
    shape = e_ref.shape[1:]
    spread = scatter_parts(shape[0] * shape[1], shape[2], map_ref, force_ref, left_ref, right_ref)
    for c in range(3):
        w2_ref[c] = e_ref[c] + spread(c).reshape(shape)
    add_faces(w2_ref, face_ref)
    for copy in copies:
        copy.wait()


def elastic(v_ref, sh_ref, la_ref, in_ref, vector_halo, stiff_halo, emit, at_shear=3):
    rows, cols, depth = sh_ref.shape
    b, a = lax.axis_index("body"), lax.axis_index("across")
    bodies, acrosses = lax.axis_size("body"), lax.axis_size("across")
    bpar, apar = lax.rem(b, 2), lax.rem(a, 2)
    cut = bodies // 4
    x_low = jnp.where(b != 0, 1.0, 0.0).astype(F32)
    x_high = jnp.where(b != bodies - 1, 1.0, 0.0).astype(F32)
    keep_low = jnp.where(b != cut, 1.0, 0.0).astype(F32)
    keep_high = jnp.where(b + 1 != cut, 1.0, 0.0).astype(F32)
    y_low = jnp.where(a != 0, 1.0, 0.0).astype(F32)
    y_high = jnp.where(a != acrosses - 1, 1.0, 0.0).astype(F32)
    inner = vector_halo is None
    vxe, vxo, vye, vyo = (None,) * 4 if inner else vector_halo
    sxe, sxo, sye, syo = (None,) * 4 if inner else stiff_halo
    row = lax.broadcasted_iota(I32, (cols, depth), 0)
    lane = lax.broadcasted_iota(I32, (cols, depth), 1)
    z_mask = jnp.where(lane == depth - 1, 0.0, 1.0)
    start = lane == 0
    top = row == cols - 1
    bottom = row == 0

    def stiffness(shear, lame):
        return 0.5 * shear, shear + 0.5 * lame

    def pick(parity, even, odd):
        return jnp.where(parity == 0, even, odd)

    def x_halo(high):
        e, o = (sxe, sxo) if high else (sxo, sxe)
        there = x_high if high else x_low
        shear, lame = pick(bpar, e[at_shear], o[at_shear]), pick(bpar, e[at_shear + 1], o[at_shear + 1])
        e, o = (vxe, vxo) if high else (vxo, vxe)
        values = [there * pick(bpar, e[c], o[c]) for c in range(3)]
        return stiffness(there * shear, there * lame), values

    def y_halo(high, x):
        e, o = (sye, syo) if high else (syo, sye)
        there = y_high if high else y_low
        at = slice(x, x + 1)
        shear, lame = pick(apar, e[at_shear, at], o[at_shear, at]), pick(apar, e[at_shear + 1, at], o[at_shear + 1, at])
        e, o = (vye, vyo) if high else (vyo, vye)
        values = [there * pick(apar, e[c, at], o[c, at]) for c in range(3)]
        return stiffness(there * shear, there * lame), values

    def slab(x):
        return stiffness(sh_ref[x], la_ref[x]), [v_ref[c, x] for c in range(3)]

    def flux(near, far, along, mask):
        (off, diag), values = near
        (far_off, far_diag), far_values = far
        side, front = off + far_off, diag + far_diag
        if mask is not None:
            side, front = side * mask, front * mask
        return [
            (front if c == along else side) * (values[c] - far_values[c]) for c in range(3)
        ]

    if in_ref is None:

        def edge_rows(ref, y, lead=None):
            at = (lambda x: ref[x, y : y + 1]) if lead is None else (lambda x: ref[lead, x, y : y + 1])
            return jnp.concatenate([at(x) for x in range(rows)], axis=0)

        def near(y):
            stiff = stiffness(edge_rows(sh_ref, y), edge_rows(la_ref, y))
            return stiff, [edge_rows(v_ref, y, c) for c in range(3)]

        def far(high):
            there = y_high if high else y_low
            e, o = (sye, syo) if high else (syo, sye)
            shear, lame = pick(apar, e[at_shear], o[at_shear]), pick(apar, e[at_shear + 1], o[at_shear + 1])
            e, o = (vye, vyo) if high else (vyo, vye)
            return stiffness(there * shear, there * lame), [there * pick(apar, e[c], o[c]) for c in range(3)]

        x_first = [-value for value in flux(x_halo(False), slab(0), 0, keep_low)]
        x_last = flux(slab(rows - 1), x_halo(True), 0, keep_high)
        y_first, y_last = flux(near(0), far(False), 1, None), flux(near(cols - 1), far(True), 1, None)

        def joined(value, c, x):
            value = value + jnp.where(bottom, y_first[c][x : x + 1], 0.0)
            return value + jnp.where(top, y_last[c][x : x + 1], 0.0)

        x_first = [joined(x_first[c], c, 0) for c in range(3)]
        x_last = [joined(x_last[c], c, rows - 1) for c in range(3)]
        return x_first, x_last, y_first, y_last

    before = None if inner else flux(x_halo(False), slab(0), 0, keep_low)
    here = slab(0)
    for x in range(rows):
        out = after = None
        if x + 1 < rows or not inner:
            after = slab(x + 1) if x + 1 < rows else x_halo(True)
            out = flux(here, after, 0, None if x + 1 < rows else keep_high)
        (off, diag), values = here
        inertia = in_ref[x]
        total = [inertia * values[c] for c in range(3)]
        if out is not None:
            total = [total[c] + out[c] for c in range(3)]
        if before is not None:
            total = [total[c] - before[c] for c in range(3)]
        before = out

        def up(value, edge):
            return jnp.where(top, edge, pltpu.roll(value, cols - 1, 0))

        if inner:

            def down(value):
                return pltpu.roll(value, cols - 1, 0)

            shifted = (down(off), down(diag)), [down(values[c]) for c in range(3)]
            out = [jnp.where(top, 0.0, value) for value in flux(here, shifted, 1, None)]
            total = [total[c] + (out[c] - pltpu.roll(out[c], 1, 0)) for c in range(3)]
        else:
            (h_off, h_diag), h_values = y_halo(True, x)
            shifted = (up(off, h_off), up(diag, h_diag)), [
                up(values[c], h_values[c]) for c in range(3)
            ]
            out = flux(here, shifted, 1, None)
            first = (off[0:1], diag[0:1]), [values[c][0:1] for c in range(3)]
            edge = flux(y_halo(False, x), first, 1, None)
            total = [
                total[c] + (out[c] - jnp.where(bottom, edge[c], pltpu.roll(out[c], 1, 0)))
                for c in range(3)
            ]

        def right(value):
            return z_mask * pltpu.roll(value, depth - 1, 1)

        shifted = (right(off), right(diag)), [right(values[c]) for c in range(3)]
        out = flux(here, shifted, 2, None)
        edge = [-(diag if c == 2 else off) * values[c] for c in range(3)]
        total = [
            total[c] + (out[c] - jnp.where(start, edge[c], pltpu.roll(out[c], 1, 1)))
            for c in range(3)
        ]
        emit(x, total)
        here = after


def stencil_one_kernel(
    r_ref, sh_ref, la_ref, in_ref, map_ref,
    e0_ref, e1_ref, e2_ref, next_ref, both_ref,
):
    e_refs = (e0_ref, e1_ref, e2_ref)
    sums = [jnp.zeros((8, 128), F32) for _ in range(2)]

    def emit(x, total):
        for c in range(3):
            e_refs[c][x] = total[c]
            r = r_ref[c, x]
            sums[0] = sums[0] + fold(r * r)
            sums[1] = sums[1] + fold(r * total[c])

    elastic(r_ref, sh_ref, la_ref, in_ref, None, None, emit)
    rows, depth = e0_ref.shape[0] * e0_ref.shape[1], e0_ref.shape[2]
    points = next_ref.shape[2]

    def write(j, c, line):
        per = line.shape[1] // points
        for b in range(per):
            next_ref[j * per + b, c : c + 1, :] = line[:, b * points : (b + 1) * points]

    blocks = next_ref.shape[0] - 1
    for k in range(blocks):
        next_ref[k, 3:4, :] = jnp.zeros((1, points), F32)
    lines = [jnp.sum(value, axis=0, keepdims=True) for value in sums]
    next_ref[blocks] = jnp.concatenate(lines + [jnp.zeros((2, points), F32)], axis=0)
    gather_into(lambda c: e_refs[c][...].reshape(rows, depth), rows, depth, map_ref, both_ref, write)


def store_faces(v_ref, parts, face_ref):
    _, rows, cols, depth = v_ref.shape
    x_first, x_last, y_first, y_last = parts
    between = lax.broadcasted_iota(I32, (rows, depth), 0)
    between = (between > 0) & (between < rows - 1)
    product = jnp.zeros((1, 128), F32)
    for c in range(3):
        face_ref[c, 0:cols] = x_first[c]
        face_ref[c, cols : 2 * cols] = x_last[c]
        face_ref[c, 2 * cols : 2 * cols + rows] = y_first[c]
        face_ref[c, 2 * cols + rows :] = y_last[c]
        ends = v_ref[c, 0] * x_first[c] + v_ref[c, rows - 1] * x_last[c]
        low = jnp.concatenate([v_ref[c, x, 0:1] for x in range(rows)], axis=0)
        high = jnp.concatenate([v_ref[c, x, cols - 1 : cols] for x in range(rows)], axis=0)
        sides = jnp.where(between, low * y_first[c] + high * y_last[c], 0.0)
        for value in (ends, sides):
            line = jnp.sum(value, axis=0, keepdims=True)
            for k in range(depth // 128):
                product = product + line[:, k * 128 : (k + 1) * 128]
    return product


def add_faces(out_ref, face_ref):
    _, rows, cols, _ = out_ref.shape
    for c in range(3):
        out_ref[c, 0] = out_ref[c, 0] + face_ref[c, 0:cols]
        out_ref[c, rows - 1] = out_ref[c, rows - 1] + face_ref[c, cols : 2 * cols]
        for x in range(1, rows - 1):
            for y, at in ((0, 2 * cols + x), (cols - 1, 2 * cols + rows + x)):
                out_ref[c, x, y : y + 1] = out_ref[c, x, y : y + 1] + face_ref[c, at : at + 1]


def faces_one_kernel(
    r_ref, sh_ref, la_ref, xe, xo, ye, yo, map_ref, inner_ref,
    face_ref, next_ref, sxe, sxo, sye, syo, both_ref,
):
    _, rows, cols, depth = r_ref.shape
    halo = (xe, xo, ye, yo)
    for source, target in zip(halo, (sxe, sxo, sye, syo)):
        for k in range(2):
            target[k] = source[3 + k]
    parts = elastic(r_ref, sh_ref, la_ref, None, halo, halo, None)
    blocks, points = next_ref.shape[0] - 1, next_ref.shape[2]
    product = store_faces(r_ref, parts, face_ref)

    def place(row):
        x, y = cell_parts(row, cols)
        at = jnp.where(y == cols - 1, 2 * cols + rows + x, -1)
        at = jnp.where(y == 0, 2 * cols + x, at)
        at = jnp.where(x == rows - 1, cols + y, at)
        return jnp.where(x == 0, y, at)

    def write(j, c, line):
        per = line.shape[1] // points
        for b in range(per):
            k = j * per + b
            next_ref[k, c : c + 1, :] = inner_ref[k, c : c + 1, :] + line[:, b * points : (b + 1) * points]

    for k in range(blocks):
        next_ref[k, 3:4, :] = jnp.zeros((1, points), F32)
    line = lax.broadcasted_iota(I32, (4, points), 0)
    next_ref[blocks] = inner_ref[blocks] + jnp.where(line == 1, product, 0.0)
    gather_into(
        lambda c: face_ref[c], face_ref.shape[1], depth, map_ref, both_ref, write, place
    )


def fold(value):
    cols, depth = value.shape
    total = None
    for k in range(depth // 128):
        part = value[:, k * 128 : (k + 1) * 128]
        part = jnp.sum(part.reshape(cols // 8, 8, 128), axis=0)
        total = part if total is None else total + part
    return total


def apply_two_kernel(
    w1_ref, sh_ref, la_ref, in_ref, got_ref, target_ref, table_ref, move_ref, w_hbm,
    e_ref, force_ref, dots_ref, w_ref, acc_ref, sem,
):
    bodies, width = got_ref.shape[0], got_ref.shape[1]
    cap = width // 2
    blocks, points = move_ref.shape[0] - 1, move_ref.shape[2]

    def fetch(d):
        return pltpu.make_async_copy(w_hbm.at[d], w_ref.at[d], sem.at[d])

    def begin(d, carry):
        fetch(d).start()
        return carry

    lax.fori_loop(0, bodies, begin, 0)
    sums = [jnp.zeros((8, 128), F32) for _ in range(2)]

    def emit(x, total):
        for c in range(3):
            e_ref[c, x] = total[c]
            w = w1_ref[c, x]
            sums[0] = sums[0] + fold(w * w)
            sums[1] = sums[1] + fold(w * total[c])

    elastic(w1_ref, sh_ref, la_ref, in_ref, None, None, emit)
    acc_ref[...] = jnp.zeros_like(acc_ref)

    def device(d, carry):
        fetch(d).wait()
        work = []
        for s in range(cap):
            n = d * cap + s
            work.append((target_ref[n], pair_part(got_ref[d, s], w_ref[d, 2 * s])))
            work.append((table_ref[0, n], pair_part(got_ref[d, cap + s], w_ref[d, 2 * s + 1])))
        for at, part in work:
            acc_ref[at] = acc_ref[at] + part
        return carry

    lax.fori_loop(0, bodies, device, 0)
    inner = jnp.zeros((4, points), F32)
    for k in range(blocks):
        acc = acc_ref[k]
        moved = move_ref[k]
        force = moved * acc[3:4] - acc
        force_ref[k] = force
        inner = inner + moved * force
    lines = [jnp.sum(value, axis=0, keepdims=True) for value in sums]
    lines[1] = lines[1] + jnp.sum(inner[0:3], axis=0, keepdims=True)
    dots_ref[...] = jnp.concatenate([move_ref[blocks][0:2]] + lines, axis=0)


def faces_two_kernel(
    w1_ref, sh_ref, la_ref, xe, xo, ye, yo, cxe, cxo, cye, cyo, dots_ref, face_ref, red_ref
):
    parts = elastic(
        w1_ref, sh_ref, la_ref, None, (xe, xo, ye, yo), (cxe, cxo, cye, cyo), None, 0
    )
    product = store_faces(w1_ref, parts, face_ref)
    line = dots_ref[...]
    line = line + jnp.where(lax.broadcasted_iota(I32, line.shape, 0) == 3, product, 0.0)
    for d in range(red_ref.shape[0]):
        red_ref[d] = line


def final_kernel(
    r0_ref, r1_ref, r2_ref, w1_ref, w2_ref, red_ref, x_hbm, res_hbm, x_ref, res_ref, sem
):
    r_refs = (r0_ref, r1_ref, r2_ref)
    line = jnp.sum(red_ref[...], axis=0)
    moment = [
        jnp.broadcast_to(jnp.sum(line[k : k + 1], axis=1, keepdims=True), (8, 128)) for k in range(4)
    ]
    m0, m1, m2, m3 = moment
    step = m0 / m1
    norm = (m0 - step * m1) + step * (step * m2 - m1)
    ratio = norm / m0
    grown = 1.0 + ratio
    curve = grown * (grown * m1 - 2.0 * step * m2) + step * step * m3
    next_step = norm / curve
    alpha = step + next_step * grown
    gamma = next_step * step
    _, rows, cols, depth = w1_ref.shape
    alpha = jnp.broadcast_to(alpha[0:1, 0:1], (cols, depth))
    gamma = jnp.broadcast_to(gamma[0:1, 0:1], (cols, depth))
    copies = []
    for c in range(3):
        for x in range(rows):
            r, w1 = r_refs[c][x], w1_ref[c, x]
            x_ref[c, x] = alpha * r - gamma * w1
            res_ref[c, x] = r - alpha * w1 + gamma * w2_ref[c, x]
        copies.append(pltpu.make_async_copy(x_ref.at[c], x_hbm.at[c], sem.at[0, c]))
        copies.append(pltpu.make_async_copy(res_ref.at[c], res_hbm.at[c], sem.at[1, c]))
        for copy in copies[-2:]:
            copy.start()
    for copy in copies:
        copy.wait()


def exchange(xe, xo, ye, yo):
    def pairs(axis, start):
        count = lax.axis_size(axis)
        chosen = []
        for i in range(count):
            partner = i + 1 if (i - start) % 2 == 0 else i - 1
            chosen.append((i, partner % count))
        return chosen

    got_xo = lax.ppermute(xo, "body", pairs("body", 1))
    got_xe = lax.ppermute(xe, "body", pairs("body", 0))
    got_yo = lax.ppermute(yo, "across", pairs("across", 1))
    got_ye = lax.ppermute(ye, "across", pairs("across", 0))
    return (
        got_xe, got_xo, got_ye, got_yo
    )


def on_device(
    cotangent, shear, lame, inertia, surface_points, point_counts, surface_maps, contact_pairs
):
    rows, cols, depth = shear.shape
    points = jnp.transpose(surface_points[0, 0], (1, 0, 2))
    counts = point_counts[0, 0]
    cell_maps = surface_maps[0, 0]
    pair_table = contact_pairs[0, 0][:, None, :]
    _, blocks, width = points.shape
    pairs = pair_table.shape[2]
    bodies, acrosses = lax.axis_size("body"), lax.axis_size("across")
    devices = bodies * acrosses
    cap = pairs // bodies
    slots = cap + blocks // 2
    chunks = blocks // 2
    cell_maps = cell_maps.reshape(chunks, 1, 2 * width)
    flat = rows * cols
    vector = sds((3, rows, cols, depth))

    def faces(count):
        return (
            sds((count, cols, depth)), sds((count, cols, depth)),
            sds((count, rows, depth)), sds((count, rows, depth)),
        )

    moves = sds((blocks, 4, width))
    both = pltpu.VMEM((3 * flat, 2 * depth), BF16)
    wide = 2 * blocks * width
    sides = (pltpu.VMEM((3 * flat, wide), BF16), pltpu.VMEM((depth, wide), BF16))
    total = pltpu.VMEM((blocks, 4, width), F32)
    kept = (bodies, 2 * cap, width, 2 * width)
    kept_mib = 10 + (8 * pairs * width * width >> 20) + (bodies >> 2)
    dma = pltpu.SemaphoreType.DMA
    cells = (sds((rows, cols, depth)),) * 3

    given = (shear, lame, inertia)
    r, shear, lame, inertia, cell_maps, xe, xo, ye, yo, own, first_moves, message, table = call(
        open_kernel, "open", [HBM] * 8, [VMEM] * 12 + [SMEM],
        (vector,) + cells + (sds(cell_maps.shape, I32),) + faces(5)
        + (moves, moves)
        + (sds((bodies, 3 * slots + (cap + 1) // 2, 2, width)), sds((2, pairs), I32)),
        scratch=(
            pltpu.VMEM(points.shape, F32), pltpu.SMEM(counts.shape, I32),
            pltpu.SMEM(pair_table.shape, I32), pltpu.SMEM((bodies,), I32),
            pltpu.VMEM((blocks, 3, 2, width), F32), both, dma((10,)),
        ), cost=4.0,
    )(*in_hbm(cotangent, shear, lame, inertia, points, counts, pair_table, cell_maps))
    got = lax.all_to_all(message, "body", 0, 0, tiled=True)
    halo = exchange(xe, xo, ye, yo)
    grown = sds((blocks + 1, 4, width))
    *elastic_one, inner_moves = call(
        stencil_one_kernel, "stencil_one", [VMEM] * 5, [VMEM] * 4, cells + (grown,),
        scratch=(both,), cost=5.0,
    )(r, shear, lame, inertia, cell_maps)
    rim = 2 * (rows + cols)
    face_one, next_moves, *stiff = call(
        faces_one_kernel, "faces_one", [VMEM] * 9, [VMEM] * 6,
        (sds((3, rim, depth)), grown) + faces(2),
        scratch=(pltpu.VMEM((3 * rim, 2 * depth), BF16),), cost=1.0,
    )(r, shear, lame, *halo, cell_maps, inner_moves)
    force_one, second_moves, message, targets, weights = call(
        forces_one_kernel, "forces_one", [VMEM] * 2 + [SMEM] + [VMEM] * 2,
        [VMEM] * 3 + [SMEM, HBM],
        (moves, grown, sds((bodies, 2 * cap, 4, width)), sds((pairs,), I32), pltpu.HBM(kept, BF16)),
        scratch=(
            pltpu.VMEM(kept, BF16), total, pltpu.VMEM((blocks, 32, width), BF16), dma((bodies,))
        ), cost=6.0, mib=kept_mib,
    )(got, own, table, first_moves, next_moves)
    got = lax.all_to_all(message, "body", 0, 0, tiled=True)
    w1, xe, xo, ye, yo, shear, lame, inertia = call(
        scatter_one_kernel, "scatter_one", [VMEM] * 6 + [HBM] * 3, [VMEM] * 8,
        (vector,) + faces(3) + cells, scratch=sides + (dma((3,)),), cost=3.0, mib=16,
    )(*elastic_one, face_one, force_one, cell_maps, *in_hbm(*given))
    halo_two = exchange(xe, xo, ye, yo)
    elastic_two, force_two, dots = call(
        apply_two_kernel, "apply_two", [VMEM] * 5 + [SMEM] * 2 + [VMEM, HBM], [VMEM] * 3,
        (vector, moves, sds((4, 128))),
        scratch=(pltpu.VMEM(kept, BF16), total, dma((bodies,))), cost=3.0, mib=kept_mib,
    )(w1, shear, lame, inertia, got, targets, table, second_moves, *in_hbm(weights))
    face_two, partial = call(
        faces_two_kernel, "faces_two", [VMEM] * 12, [VMEM] * 2,
        (sds((3, rim, depth)), sds((devices, 4, 128))), cost=1.0,
    )(w1, shear, lame, *halo_two, *stiff, dots)
    sums = lax.all_to_all(partial, ("body", "across"), 0, 0, tiled=True)
    w2, *parts = call(
        scatter_two_kernel, "scatter_two", [VMEM] * 4 + [HBM], [VMEM] * 4, (vector,) + cells,
        scratch=sides + (dma((3,)),), cost=3.0, mib=16,
    )(elastic_two, face_two, force_two, cell_maps, *in_hbm(cotangent))
    out = pltpu.VMEM((3, rows, cols, depth), F32)
    return call(
        final_kernel, "final", [VMEM] * 6, [HBM] * 2, (vector, vector),
        scratch=(out, out, dma((2, 3))), cost=1.0,
    )(*parts, w1, w2, sums)


def solution(mesh):
    placed = (
        P(None, "body", "across", None),
        P("body", "across", None),
        P("body", "across", None),
        P("body", "across", None),
        P("body", "across", None, None, None),
        P("body", "across", None),
        P("body", "across", None, None),
        P("body", "across", None, None),
    )
    return jax.shard_map(
        on_device,
        mesh=mesh,
        in_specs=placed,
        out_specs=(P(None, "body", "across", None), P(None, "body", "across", None)),
        check_vma=False,
    )
```

```python
import jax
import jax.numpy as jnp
from jax import lax
from jax.experimental import pallas as pl
from jax.experimental.pallas import tpu as pltpu
from jax.sharding import PartitionSpec as P

F32 = jnp.float32
BF16 = jnp.bfloat16
I32 = jnp.int32

barrier_reach = 1.0
barrier_scale = 0.005
FAR = 1000.0

VMEM = pl.BlockSpec(memory_space=pltpu.VMEM)
SMEM = pl.BlockSpec(memory_space=pltpu.SMEM)
HBM = pl.BlockSpec(memory_space=pltpu.HBM)


def sds(shape, dtype=F32):
    return jax.ShapeDtypeStruct(shape, dtype)


def call(body, name, in_specs, out_specs, out_shape, scratch=(), cost=2.0, mib=8):
    estimate = pl.CostEstimate(flops=int(cost * 1e8), transcendentals=0, bytes_accessed=int(cost * 3e6))
    return pl.pallas_call(
        body,
        name=name,
        in_specs=in_specs,
        out_specs=out_specs,
        out_shape=out_shape,
        scratch_shapes=list(scratch),
        cost_estimate=estimate,
        compiler_params=pltpu.CompilerParams(vmem_limit_bytes=mib << 20),
    )


def in_hbm(*arrays):
    return tuple(pltpu.with_memory_space_constraint(array, pltpu.HBM) for array in arrays)


def split(values):
    high = values.astype(BF16)
    low = (values - high.astype(F32)).astype(BF16)
    return high, low


def even_faces(block, axis_parity, last):
    first = jnp.where(axis_parity == 0, last, 0)
    return first, last - first


def write_faces(sources, xe_ref, xo_ref, ye_ref, yo_ref):
    bpar = lax.rem(lax.axis_index("body"), 2)
    apar = lax.rem(lax.axis_index("across"), 2)
    for k, (ref, lead) in enumerate(sources):
        at = (lambda x: ref[lead, x]) if lead is not None else (lambda x: ref[x])
        rows = ref.shape[-3]
        cols = ref.shape[-2]
        xi = jnp.where(bpar == 0, rows - 1, 0)
        xe_ref[k] = at(xi)
        xo_ref[k] = at(rows - 1 - xi)
        for x in range(rows):
            slab = at(x)
            low = slab[0:1]
            high = slab[cols - 1 : cols]
            ye_ref[k, x : x + 1] = jnp.where(apar == 0, high, low)
            yo_ref[k, x : x + 1] = jnp.where(apar == 0, low, high)


def cell_parts(cells, depth):
    if depth & (depth - 1) == 0:
        shift = depth.bit_length() - 1
        return lax.shift_right_logical(cells, shift), jnp.bitwise_and(cells, depth - 1)
    row = cells // depth
    return row, cells - row * depth


def gather_into(load, rows, depth, map_ref, both_ref, write, place=None):
    for c in range(3):
        high, low = split(load(c))
        both_ref[c * rows : (c + 1) * rows, 0:depth] = high
        both_ref[c * rows : (c + 1) * rows, depth:] = low
    chunks, _, span = map_ref.shape
    depth_iota = lax.broadcasted_iota(I32, (depth, span), 0)
    row_iota = lax.broadcasted_iota(I32, (rows, span), 0)

    def chunk(j, carry):
        row, deep = cell_parts(map_ref[j], depth)
        onehot = jnp.where(depth_iota == deep, 1.0, 0.0).astype(BF16)
        onehot = jnp.concatenate([onehot, onehot], axis=0)
        row = row if place is None else place(row)
        picked = jnp.dot(both_ref[...], onehot, preferred_element_type=F32)
        here = row_iota == row
        for c in range(3):
            part = jnp.where(here, picked[c * rows : (c + 1) * rows], 0.0)
            write(j, c, jnp.sum(part, axis=0, keepdims=True))
        return carry

    lax.fori_loop(0, chunks, chunk, 0, unroll=8)


def open_kernel(
    r_hbm, sh_hbm, la_hbm, in_hbm, pt_hbm, cnt_hbm, pair_hbm, map_hbm,
    r_ref, sh_ref, la_ref, in_ref, map_ref,
    xe_ref, xo_ref, ye_ref, yo_ref, own_ref, move_ref, msg_ref, table_ref,
    pt_ref, cnt_ref, pair_ref, fill_ref, sent_ref, both_ref, sem,
):
    copies = [
        pltpu.make_async_copy(source, target, sem.at[k])
        for k, (source, target) in enumerate([
            (cnt_hbm, cnt_ref), (pair_hbm, pair_ref), (pt_hbm, pt_ref), (map_hbm, map_ref),
            (r_hbm.at[0], r_ref.at[0]), (r_hbm.at[1], r_ref.at[1]), (r_hbm.at[2], r_ref.at[2]),
            (sh_hbm, sh_ref), (la_hbm, la_ref), (in_hbm, in_ref),
        ])
    ]
    for copy in copies:
        copy.start()
    bodies = msg_ref.shape[0]
    blocks = own_ref.shape[0]
    odd_total = blocks // 2
    pairs = table_ref.shape[1]
    cap = pairs // bodies
    slots = cap + odd_total
    points = own_ref.shape[2]
    lane = lax.broadcasted_iota(I32, (1, points), 1)
    edge = lax.broadcasted_iota(I32, (4, points), 0) == 3
    for copy in copies[:4]:
        copy.wait()
    for d in range(bodies):
        fill_ref[d] = 0

    def place(n, carry):
        dest = pair_ref[1, 0, n]
        rank = fill_ref[dest]
        fill_ref[dest] = rank + 1
        table_ref[0, dest * cap + rank] = pair_ref[0, 0, n]
        table_ref[1, dest * cap + rank] = pair_ref[2, 0, n]
        return carry

    lax.fori_loop(0, pairs, place, 0)
    blank = jnp.zeros((1, points), F32)
    for k in range(blocks):
        tile = jnp.concatenate([pt_ref[c, k : k + 1, :] for c in range(3)] + [blank], axis=0)
        own_ref[k] = measured(jnp.where(lane < cnt_ref[k], tile, -FAR), edge)
        tile = jnp.where(lane < cnt_ref[k], tile, FAR)
        sent_ref[k, 1, 1:2, :] = tile[0:1]
        sent_ref[k, 2] = tile[1:3]
        move_ref[k, 3:4, :] = blank + 1.0
    for copy in copies[4:]:
        copy.wait()
    rows, depth = r_ref.shape[1] * r_ref.shape[2], r_ref.shape[3]

    def write(j, c, line):
        per = line.shape[1] // points
        for b in range(per):
            part = line[:, b * points : (b + 1) * points]
            move_ref[j * per + b, c : c + 1, :] = part
            sent_ref[j * per + b, c // 2, c % 2 : c % 2 + 1, :] = part

    gather_into(lambda c: r_ref[c].reshape(rows, depth), rows, depth, map_ref, both_ref, write)

    def pack(d, carry):
        for s in range(cap):
            second = table_ref[1, d * cap + s].astype(F32)
            msg_ref[d, 3 * s : 3 * s + 3] = sent_ref[table_ref[0, d * cap + s]]
            msg_ref[d, 3 * slots + s // 2, s % 2 : s % 2 + 1, :] = jnp.full((1, points), second)
        for j in range(odd_total):
            msg_ref[d, 3 * (cap + j) : 3 * (cap + j) + 3] = sent_ref[2 * j + 1]
        return carry

    lax.fori_loop(0, bodies, pack, 0)
    sources = [(r_ref, 0), (r_ref, 1), (r_ref, 2), (sh_ref, None), (la_ref, None)]
    write_faces(sources, xe_ref, xo_ref, ye_ref, yo_ref)


def measured(tile, edge):
    square = jnp.where(edge, 0.0, tile * tile)
    return jnp.where(edge, jnp.sum(square, axis=0, keepdims=True), tile)


def three_parts(value):
    high = value.astype(BF16).astype(F32)
    rest = value - high
    middle = rest.astype(BF16).astype(F32)
    return high, middle, rest - middle


def source_rows(tile):
    row = lax.broadcasted_iota(I32, (8, tile.shape[1]), 0)
    high, middle, low = three_parts(jnp.concatenate([tile, tile], axis=0))
    first = jnp.where(row == 7, middle, high)
    second = jnp.where(row == 3, low, jnp.where(row < 3, middle, high))
    second = jnp.where(row == 7, 1.0, second)
    third = jnp.where(row < 3, low, middle)
    third = jnp.where((row == 3) | (row == 7), 1.0, third)
    return jnp.concatenate([first, second, third, jnp.zeros_like(first)], axis=0).astype(BF16)


def target_rows(tile):
    row = lax.broadcasted_iota(I32, (8, tile.shape[1]), 0)
    high, middle, low = three_parts(jnp.concatenate([tile, tile], axis=0))
    first = -2.0 * jnp.where(row < 4, high, middle)
    first = jnp.where((row == 3) | (row == 7), 1.0, first)
    second = -2.0 * jnp.where(row < 4, high, low)
    second = jnp.where(row == 3, 1.0, jnp.where(row == 7, high, second))
    third = -2.0 * jnp.where(row < 4, high, middle)
    third = jnp.where(row == 3, middle, jnp.where(row == 7, low, third))
    return jnp.concatenate([first, second, third, jnp.zeros_like(first)], axis=0).astype(BF16)


def weigh(tile, target):
    squared = lax.dot_general(
        source_rows(tile), target, (((0,), (0,)), ((), ())), preferred_element_type=F32
    )
    q = 1.0 - 1.0 / squared
    weight = barrier_scale * (-2.0 * jnp.log(squared) - 4.0 * q + q * q)
    return jnp.where(squared < barrier_reach, weight, 0.0)


def pair_part(moves, weights):
    points = moves.shape[1]
    high = moves.astype(BF16).astype(F32)
    lhs = jnp.concatenate([high, moves - high], axis=0).astype(BF16)
    out = jnp.dot(lhs, weights, preferred_element_type=F32)
    return (out[0:4, :points] + out[4:8, :points]) + (out[0:4, points:] + out[4:8, points:])


def forces_one_kernel(
    got_ref, own_ref, table_ref, move_ref, next_ref,
    force_ref, sum_ref, msg_ref, target_ref, w_hbm, w_ref, acc_ref, right_ref, sem,
):
    bodies = got_ref.shape[0]
    blocks, _, points = move_ref.shape
    cap = table_ref.shape[1] // bodies
    slots = cap + blocks // 2
    one = jnp.ones((1, points), F32)

    def received(d, slot):
        parts = got_ref[d, pl.ds(3 * slot, 3)]
        moves = jnp.concatenate([parts[0], parts[1, 0:1], one], axis=0)
        tile = jnp.concatenate([parts[1, 1:2], parts[2], one], axis=0)
        return moves, measured(tile, edge)

    for k in range(blocks):
        right_ref[k] = target_rows(own_ref[k])
    acc_ref[...] = jnp.zeros_like(acc_ref)

    edge = lax.broadcasted_iota(I32, (4, points), 0) == 3

    def keep(d):
        return pltpu.make_async_copy(w_ref.at[d], w_hbm.at[d], sem.at[d])

    def find(d, carry):
        for s in range(cap):
            target_ref[d * cap + s] = jnp.max(
                got_ref[d, 3 * slots + s // 2, s % 2 : s % 2 + 1, :]
            ).astype(I32)
        return carry

    lax.fori_loop(0, bodies, find, 0, unroll=8)

    def device(d, carry):
        work = []
        for s in range(cap):
            n = d * cap + s
            work.append((received(d, s), target_ref[n]))
            first = table_ref[0, n]
            odd = lax.shift_right_logical(table_ref[1, n], 1)
            work.append((received(d, cap + odd), first))
        parts = []
        for k, ((moves, tile), at) in enumerate(work):
            high, low = split(weigh(tile, right_ref[at]))
            both = jnp.concatenate([high, low], axis=1)
            w_ref[d, k] = both
            parts.append(pair_part(moves, both))
        for (_, at), part in zip(work, parts):
            acc_ref[at] = acc_ref[at] + part
        keep(d).start()
        return carry

    lax.fori_loop(0, bodies, device, 0, unroll=4)
    row = lax.broadcasted_iota(I32, (4, points), 0)
    inner = jnp.zeros((4, points), F32)
    for k in range(blocks):
        acc = acc_ref[k]
        force = move_ref[k] * acc[3:4] - acc
        force_ref[k] = force
        sum_ref[k] = jnp.where(row < 3, next_ref[k] + force, 1.0)
        inner = inner + move_ref[k] * force
    inner = jnp.sum(inner[0:3], axis=0, keepdims=True)
    sum_ref[blocks] = next_ref[blocks] + jnp.where(row == 1, inner, 0.0)

    def pack(d, carry):
        for s in range(cap):
            n = d * cap + s
            msg_ref[d, s] = sum_ref[table_ref[0, n]]
            msg_ref[d, cap + s] = sum_ref[target_ref[n]]
        return carry

    lax.fori_loop(0, bodies, pack, 0)

    def finish(d, carry):
        keep(d).wait()
        return carry

    lax.fori_loop(0, bodies, finish, 0)


def scatter_parts(rows, depth, map_ref, force_ref, left_ref, right_ref):
    span = map_ref.shape[2]
    per = force_ref.shape[0] // map_ref.shape[0]
    depth_iota = lax.broadcasted_iota(I32, (depth, span), 0)
    row_iota = lax.broadcasted_iota(I32, (rows, span), 0)
    chunks = map_ref.shape[0]
    for j in range(chunks):
        row, deep = cell_parts(map_ref[j], depth)
        onehot = jnp.where(depth_iota == deep, 1.0, 0.0).astype(BF16)
        right_ref[:, j * span : (j + 1) * span] = onehot
        right_ref[:, (chunks + j) * span : (chunks + j + 1) * span] = onehot
        here = row_iota == row
        for c in range(3):
            line = jnp.concatenate(
                [force_ref[j * per + b, c : c + 1, :] for b in range(per)], axis=1
            )
            high = line.astype(BF16).astype(F32)
            at = slice(c * rows, (c + 1) * rows)
            left_ref[at, j * span : (j + 1) * span] = jnp.where(here, high, 0.0).astype(BF16)
            left_ref[at, (chunks + j) * span : (chunks + j + 1) * span] = jnp.where(
                here, line - high, 0.0
            ).astype(BF16)
    def spread(c):
        return lax.dot_general(
            left_ref[c * rows : (c + 1) * rows], right_ref[...], (((1,), (1,)), ((), ())),
            preferred_element_type=F32,
        )

    return spread


def scatter_one_kernel(
    e0_ref, e1_ref, e2_ref, face_ref, force_ref, map_ref, sh_hbm, la_hbm, in_hbm_ref,
    w1_ref, xe_ref, xo_ref, ye_ref, yo_ref, sh_ref, la_ref, in_ref, left_ref, right_ref, sem,
):
    cells = [
        pltpu.make_async_copy(source, target, sem.at[k])
        for k, (source, target) in enumerate(
            [(sh_hbm, sh_ref), (la_hbm, la_ref), (in_hbm_ref, in_ref)]
        )
    ]
    for copy in cells:
        copy.start()
    shape = e0_ref.shape
    spread = scatter_parts(shape[0] * shape[1], shape[2], map_ref, force_ref, left_ref, right_ref)
    for c, e_ref in enumerate((e0_ref, e1_ref, e2_ref)):
        w1_ref[c] = e_ref[...] + spread(c).reshape(shape)
    add_faces(w1_ref, face_ref)
    write_faces([(w1_ref, 0), (w1_ref, 1), (w1_ref, 2)], xe_ref, xo_ref, ye_ref, yo_ref)
    for copy in cells:
        copy.wait()


def scatter_two_kernel(
    e_ref, face_ref, force_ref, map_ref, r_hbm,
    w2_ref, r0_ref, r1_ref, r2_ref, left_ref, right_ref, sem,
):
    copies = [
        pltpu.make_async_copy(r_hbm.at[c], target, sem.at[c])
        for c, target in enumerate((r0_ref, r1_ref, r2_ref))
    ]
    for copy in copies:
        copy.start()
    shape = e_ref.shape[1:]
    spread = scatter_parts(shape[0] * shape[1], shape[2], map_ref, force_ref, left_ref, right_ref)
    for c in range(3):
        w2_ref[c] = e_ref[c] + spread(c).reshape(shape)
    add_faces(w2_ref, face_ref)
    for copy in copies:
        copy.wait()


def elastic(v_ref, sh_ref, la_ref, in_ref, vector_halo, stiff_halo, emit, at_shear=3):
    rows, cols, depth = sh_ref.shape
    b, a = lax.axis_index("body"), lax.axis_index("across")
    bodies, acrosses = lax.axis_size("body"), lax.axis_size("across")
    bpar, apar = lax.rem(b, 2), lax.rem(a, 2)
    cut = bodies // 4
    x_low = jnp.where(b != 0, 1.0, 0.0).astype(F32)
    x_high = jnp.where(b != bodies - 1, 1.0, 0.0).astype(F32)
    keep_low = jnp.where(b != cut, 1.0, 0.0).astype(F32)
    keep_high = jnp.where(b + 1 != cut, 1.0, 0.0).astype(F32)
    y_low = jnp.where(a != 0, 1.0, 0.0).astype(F32)
    y_high = jnp.where(a != acrosses - 1, 1.0, 0.0).astype(F32)
    inner = vector_halo is None
    vxe, vxo, vye, vyo = (None,) * 4 if inner else vector_halo
    sxe, sxo, sye, syo = (None,) * 4 if inner else stiff_halo
    row = lax.broadcasted_iota(I32, (cols, depth), 0)
    lane = lax.broadcasted_iota(I32, (cols, depth), 1)
    z_mask = jnp.where(lane == depth - 1, 0.0, 1.0)
    start = lane == 0
    top = row == cols - 1
    bottom = row == 0

    def stiffness(shear, lame):
        return 0.5 * shear, shear + 0.5 * lame

    def pick(parity, even, odd):
        return jnp.where(parity == 0, even, odd)

    def x_halo(high):
        e, o = (sxe, sxo) if high else (sxo, sxe)
        there = x_high if high else x_low
        shear, lame = pick(bpar, e[at_shear], o[at_shear]), pick(bpar, e[at_shear + 1], o[at_shear + 1])
        e, o = (vxe, vxo) if high else (vxo, vxe)
        values = [there * pick(bpar, e[c], o[c]) for c in range(3)]
        return stiffness(there * shear, there * lame), values

    def y_halo(high, x):
        e, o = (sye, syo) if high else (syo, sye)
        there = y_high if high else y_low
        at = slice(x, x + 1)
        shear, lame = pick(apar, e[at_shear, at], o[at_shear, at]), pick(apar, e[at_shear + 1, at], o[at_shear + 1, at])
        e, o = (vye, vyo) if high else (vyo, vye)
        values = [there * pick(apar, e[c, at], o[c, at]) for c in range(3)]
        return stiffness(there * shear, there * lame), values

    def slab(x):
        return stiffness(sh_ref[x], la_ref[x]), [v_ref[c, x] for c in range(3)]

    def flux(near, far, along, mask):
        (off, diag), values = near
        (far_off, far_diag), far_values = far
        side, front = off + far_off, diag + far_diag
        if mask is not None:
            side, front = side * mask, front * mask
        return [
            (front if c == along else side) * (values[c] - far_values[c]) for c in range(3)
        ]

    if in_ref is None:

        def edge_rows(ref, y, lead=None):
            at = (lambda x: ref[x, y : y + 1]) if lead is None else (lambda x: ref[lead, x, y : y + 1])
            return jnp.concatenate([at(x) for x in range(rows)], axis=0)

        def near(y):
            stiff = stiffness(edge_rows(sh_ref, y), edge_rows(la_ref, y))
            return stiff, [edge_rows(v_ref, y, c) for c in range(3)]

        def far(high):
            there = y_high if high else y_low
            e, o = (sye, syo) if high else (syo, sye)
            shear, lame = pick(apar, e[at_shear], o[at_shear]), pick(apar, e[at_shear + 1], o[at_shear + 1])
            e, o = (vye, vyo) if high else (vyo, vye)
            return stiffness(there * shear, there * lame), [there * pick(apar, e[c], o[c]) for c in range(3)]

        x_first = [-value for value in flux(x_halo(False), slab(0), 0, keep_low)]
        x_last = flux(slab(rows - 1), x_halo(True), 0, keep_high)
        y_first, y_last = flux(near(0), far(False), 1, None), flux(near(cols - 1), far(True), 1, None)

        def joined(value, c, x):
            value = value + jnp.where(bottom, y_first[c][x : x + 1], 0.0)
            return value + jnp.where(top, y_last[c][x : x + 1], 0.0)

        x_first = [joined(x_first[c], c, 0) for c in range(3)]
        x_last = [joined(x_last[c], c, rows - 1) for c in range(3)]
        return x_first, x_last, y_first, y_last

    before = None if inner else flux(x_halo(False), slab(0), 0, keep_low)
    here = slab(0)
    for x in range(rows):
        out = after = None
        if x + 1 < rows or not inner:
            after = slab(x + 1) if x + 1 < rows else x_halo(True)
            out = flux(here, after, 0, None if x + 1 < rows else keep_high)
        (off, diag), values = here
        inertia = in_ref[x]
        total = [inertia * values[c] for c in range(3)]
        if out is not None:
            total = [total[c] + out[c] for c in range(3)]
        if before is not None:
            total = [total[c] - before[c] for c in range(3)]
        before = out

        def up(value, edge):
            return jnp.where(top, edge, pltpu.roll(value, cols - 1, 0))

        if inner:

            def down(value):
                return pltpu.roll(value, cols - 1, 0)

            shifted = (down(off), down(diag)), [down(values[c]) for c in range(3)]
            out = [jnp.where(top, 0.0, value) for value in flux(here, shifted, 1, None)]
            total = [total[c] + (out[c] - pltpu.roll(out[c], 1, 0)) for c in range(3)]
        else:
            (h_off, h_diag), h_values = y_halo(True, x)
            shifted = (up(off, h_off), up(diag, h_diag)), [
                up(values[c], h_values[c]) for c in range(3)
            ]
            out = flux(here, shifted, 1, None)
            first = (off[0:1], diag[0:1]), [values[c][0:1] for c in range(3)]
            edge = flux(y_halo(False, x), first, 1, None)
            total = [
                total[c] + (out[c] - jnp.where(bottom, edge[c], pltpu.roll(out[c], 1, 0)))
                for c in range(3)
            ]

        def right(value):
            return z_mask * pltpu.roll(value, depth - 1, 1)

        shifted = (right(off), right(diag)), [right(values[c]) for c in range(3)]
        out = flux(here, shifted, 2, None)
        edge = [-(diag if c == 2 else off) * values[c] for c in range(3)]
        total = [
            total[c] + (out[c] - jnp.where(start, edge[c], pltpu.roll(out[c], 1, 1)))
            for c in range(3)
        ]
        emit(x, total)
        here = after


def stencil_one_kernel(
    r_ref, sh_ref, la_ref, in_ref, map_ref,
    e0_ref, e1_ref, e2_ref, next_ref, both_ref,
):
    e_refs = (e0_ref, e1_ref, e2_ref)
    sums = [jnp.zeros((8, 128), F32) for _ in range(2)]

    def emit(x, total):
        for c in range(3):
            e_refs[c][x] = total[c]
            r = r_ref[c, x]
            sums[0] = sums[0] + fold(r * r)
            sums[1] = sums[1] + fold(r * total[c])

    elastic(r_ref, sh_ref, la_ref, in_ref, None, None, emit)
    rows, depth = e0_ref.shape[0] * e0_ref.shape[1], e0_ref.shape[2]
    points = next_ref.shape[2]

    def write(j, c, line):
        per = line.shape[1] // points
        for b in range(per):
            next_ref[j * per + b, c : c + 1, :] = line[:, b * points : (b + 1) * points]

    blocks = next_ref.shape[0] - 1
    for k in range(blocks):
        next_ref[k, 3:4, :] = jnp.zeros((1, points), F32)
    lines = [jnp.sum(value, axis=0, keepdims=True) for value in sums]
    next_ref[blocks] = jnp.concatenate(lines + [jnp.zeros((2, points), F32)], axis=0)
    gather_into(lambda c: e_refs[c][...].reshape(rows, depth), rows, depth, map_ref, both_ref, write)


def store_faces(v_ref, parts, face_ref):
    _, rows, cols, depth = v_ref.shape
    x_first, x_last, y_first, y_last = parts
    between = lax.broadcasted_iota(I32, (rows, depth), 0)
    between = (between > 0) & (between < rows - 1)
    product = jnp.zeros((1, 128), F32)
    for c in range(3):
        face_ref[c, 0:cols] = x_first[c]
        face_ref[c, cols : 2 * cols] = x_last[c]
        face_ref[c, 2 * cols : 2 * cols + rows] = y_first[c]
        face_ref[c, 2 * cols + rows :] = y_last[c]
        ends = v_ref[c, 0] * x_first[c] + v_ref[c, rows - 1] * x_last[c]
        low = jnp.concatenate([v_ref[c, x, 0:1] for x in range(rows)], axis=0)
        high = jnp.concatenate([v_ref[c, x, cols - 1 : cols] for x in range(rows)], axis=0)
        sides = jnp.where(between, low * y_first[c] + high * y_last[c], 0.0)
        for value in (ends, sides):
            line = jnp.sum(value, axis=0, keepdims=True)
            for k in range(depth // 128):
                product = product + line[:, k * 128 : (k + 1) * 128]
    return product


def add_faces(out_ref, face_ref):
    _, rows, cols, _ = out_ref.shape
    for c in range(3):
        out_ref[c, 0] = out_ref[c, 0] + face_ref[c, 0:cols]
        out_ref[c, rows - 1] = out_ref[c, rows - 1] + face_ref[c, cols : 2 * cols]
        for x in range(1, rows - 1):
            for y, at in ((0, 2 * cols + x), (cols - 1, 2 * cols + rows + x)):
                out_ref[c, x, y : y + 1] = out_ref[c, x, y : y + 1] + face_ref[c, at : at + 1]


def faces_one_kernel(
    r_ref, sh_ref, la_ref, xe, xo, ye, yo, map_ref, inner_ref,
    face_ref, next_ref, sxe, sxo, sye, syo, both_ref,
):
    _, rows, cols, depth = r_ref.shape
    halo = (xe, xo, ye, yo)
    for source, target in zip(halo, (sxe, sxo, sye, syo)):
        for k in range(2):
            target[k] = source[3 + k]
    parts = elastic(r_ref, sh_ref, la_ref, None, halo, halo, None)
    blocks, points = next_ref.shape[0] - 1, next_ref.shape[2]
    product = store_faces(r_ref, parts, face_ref)

    def place(row):
        x, y = cell_parts(row, cols)
        at = jnp.where(y == cols - 1, 2 * cols + rows + x, -1)
        at = jnp.where(y == 0, 2 * cols + x, at)
        at = jnp.where(x == rows - 1, cols + y, at)
        return jnp.where(x == 0, y, at)

    def write(j, c, line):
        per = line.shape[1] // points
        for b in range(per):
            k = j * per + b
            next_ref[k, c : c + 1, :] = inner_ref[k, c : c + 1, :] + line[:, b * points : (b + 1) * points]

    for k in range(blocks):
        next_ref[k, 3:4, :] = jnp.zeros((1, points), F32)
    line = lax.broadcasted_iota(I32, (4, points), 0)
    next_ref[blocks] = inner_ref[blocks] + jnp.where(line == 1, product, 0.0)
    gather_into(
        lambda c: face_ref[c], face_ref.shape[1], depth, map_ref, both_ref, write, place
    )


def fold(value):
    cols, depth = value.shape
    total = None
    for k in range(depth // 128):
        part = value[:, k * 128 : (k + 1) * 128]
        part = jnp.sum(part.reshape(cols // 8, 8, 128), axis=0)
        total = part if total is None else total + part
    return total


def apply_two_kernel(
    w1_ref, sh_ref, la_ref, in_ref, got_ref, target_ref, table_ref, move_ref, w_hbm,
    e_ref, force_ref, dots_ref, w_ref, acc_ref, sem,
):
    bodies, width = got_ref.shape[0], got_ref.shape[1]
    cap = width // 2
    blocks, points = move_ref.shape[0] - 1, move_ref.shape[2]

    def fetch(d):
        return pltpu.make_async_copy(w_hbm.at[d], w_ref.at[d], sem.at[d])

    def begin(d, carry):
        fetch(d).start()
        return carry

    lax.fori_loop(0, bodies, begin, 0)
    sums = [jnp.zeros((8, 128), F32) for _ in range(2)]

    def emit(x, total):
        for c in range(3):
            e_ref[c, x] = total[c]
            w = w1_ref[c, x]
            sums[0] = sums[0] + fold(w * w)
            sums[1] = sums[1] + fold(w * total[c])

    elastic(w1_ref, sh_ref, la_ref, in_ref, None, None, emit)
    acc_ref[...] = jnp.zeros_like(acc_ref)

    def device(d, carry):
        fetch(d).wait()
        work = []
        for s in range(cap):
            n = d * cap + s
            work.append((target_ref[n], pair_part(got_ref[d, s], w_ref[d, 2 * s])))
            work.append((table_ref[0, n], pair_part(got_ref[d, cap + s], w_ref[d, 2 * s + 1])))
        for at, part in work:
            acc_ref[at] = acc_ref[at] + part
        return carry

    lax.fori_loop(0, bodies, device, 0, unroll=4)
    inner = jnp.zeros((4, points), F32)
    for k in range(blocks):
        acc = acc_ref[k]
        moved = move_ref[k]
        force = moved * acc[3:4] - acc
        force_ref[k] = force
        inner = inner + moved * force
    lines = [jnp.sum(value, axis=0, keepdims=True) for value in sums]
    lines[1] = lines[1] + jnp.sum(inner[0:3], axis=0, keepdims=True)
    dots_ref[...] = jnp.concatenate([move_ref[blocks][0:2]] + lines, axis=0)


def faces_two_kernel(
    w1_ref, sh_ref, la_ref, xe, xo, ye, yo, cxe, cxo, cye, cyo, dots_ref, face_ref, red_ref
):
    parts = elastic(
        w1_ref, sh_ref, la_ref, None, (xe, xo, ye, yo), (cxe, cxo, cye, cyo), None, 0
    )
    product = store_faces(w1_ref, parts, face_ref)
    line = dots_ref[...]
    line = line + jnp.where(lax.broadcasted_iota(I32, line.shape, 0) == 3, product, 0.0)
    for d in range(red_ref.shape[0]):
        red_ref[d] = line


def final_kernel(
    r0_ref, r1_ref, r2_ref, w1_ref, w2_ref, red_ref, x_hbm, res_hbm, x_ref, res_ref, sem
):
    r_refs = (r0_ref, r1_ref, r2_ref)
    line = jnp.sum(red_ref[...], axis=0)
    moment = [
        jnp.broadcast_to(jnp.sum(line[k : k + 1], axis=1, keepdims=True), (8, 128)) for k in range(4)
    ]
    m0, m1, m2, m3 = moment
    step = m0 / m1
    norm = (m0 - step * m1) + step * (step * m2 - m1)
    ratio = norm / m0
    grown = 1.0 + ratio
    curve = grown * (grown * m1 - 2.0 * step * m2) + step * step * m3
    next_step = norm / curve
    alpha = step + next_step * grown
    gamma = next_step * step
    _, rows, cols, depth = w1_ref.shape
    alpha = jnp.broadcast_to(alpha[0:1, 0:1], (cols, depth))
    gamma = jnp.broadcast_to(gamma[0:1, 0:1], (cols, depth))
    copies = []
    for c in range(3):
        for x in range(rows):
            r, w1 = r_refs[c][x], w1_ref[c, x]
            x_ref[c, x] = alpha * r - gamma * w1
            res_ref[c, x] = r - alpha * w1 + gamma * w2_ref[c, x]
        copies.append(pltpu.make_async_copy(x_ref.at[c], x_hbm.at[c], sem.at[0, c]))
        copies.append(pltpu.make_async_copy(res_ref.at[c], res_hbm.at[c], sem.at[1, c]))
        for copy in copies[-2:]:
            copy.start()
    for copy in copies:
        copy.wait()


def exchange(xe, xo, ye, yo):
    def pairs(axis, start):
        count = lax.axis_size(axis)
        chosen = []
        for i in range(count):
            partner = i + 1 if (i - start) % 2 == 0 else i - 1
            chosen.append((i, partner % count))
        return chosen

    got_xo = lax.ppermute(xo, "body", pairs("body", 1))
    got_xe = lax.ppermute(xe, "body", pairs("body", 0))
    got_yo = lax.ppermute(yo, "across", pairs("across", 1))
    got_ye = lax.ppermute(ye, "across", pairs("across", 0))
    return (
        got_xe, got_xo, got_ye, got_yo
    )


def on_device(
    cotangent, shear, lame, inertia, surface_points, point_counts, surface_maps, contact_pairs
):
    rows, cols, depth = shear.shape
    points = jnp.transpose(surface_points[0, 0], (1, 0, 2))
    counts = point_counts[0, 0]
    cell_maps = surface_maps[0, 0]
    pair_table = contact_pairs[0, 0][:, None, :]
    _, blocks, width = points.shape
    pairs = pair_table.shape[2]
    bodies, acrosses = lax.axis_size("body"), lax.axis_size("across")
    devices = bodies * acrosses
    cap = pairs // bodies
    slots = cap + blocks // 2
    chunks = blocks // 2
    cell_maps = cell_maps.reshape(chunks, 1, 2 * width)
    flat = rows * cols
    vector = sds((3, rows, cols, depth))

    def faces(count):
        return (
            sds((count, cols, depth)), sds((count, cols, depth)),
            sds((count, rows, depth)), sds((count, rows, depth)),
        )

    moves = sds((blocks, 4, width))
    both = pltpu.VMEM((3 * flat, 2 * depth), BF16)
    wide = 2 * blocks * width
    sides = (pltpu.VMEM((3 * flat, wide), BF16), pltpu.VMEM((depth, wide), BF16))
    total = pltpu.VMEM((blocks, 4, width), F32)
    kept = (bodies, 2 * cap, width, 2 * width)
    kept_mib = 10 + (8 * pairs * width * width >> 20) + (bodies >> 2)
    dma = pltpu.SemaphoreType.DMA
    cells = (sds((rows, cols, depth)),) * 3

    given = (shear, lame, inertia)
    r, shear, lame, inertia, cell_maps, xe, xo, ye, yo, own, first_moves, message, table = call(
        open_kernel, "open", [HBM] * 8, [VMEM] * 12 + [SMEM],
        (vector,) + cells + (sds(cell_maps.shape, I32),) + faces(5)
        + (moves, moves)
        + (sds((bodies, 3 * slots + (cap + 1) // 2, 2, width)), sds((2, pairs), I32)),
        scratch=(
            pltpu.VMEM(points.shape, F32), pltpu.SMEM(counts.shape, I32),
            pltpu.SMEM(pair_table.shape, I32), pltpu.SMEM((bodies,), I32),
            pltpu.VMEM((blocks, 3, 2, width), F32), both, dma((10,)),
        ), cost=4.0,
    )(*in_hbm(cotangent, shear, lame, inertia, points, counts, pair_table, cell_maps))
    got = lax.all_to_all(message, "body", 0, 0, tiled=True)
    halo = exchange(xe, xo, ye, yo)
    grown = sds((blocks + 1, 4, width))
    *elastic_one, inner_moves = call(
        stencil_one_kernel, "stencil_one", [VMEM] * 5, [VMEM] * 4, cells + (grown,),
        scratch=(both,), cost=5.0,
    )(r, shear, lame, inertia, cell_maps)
    rim = 2 * (rows + cols)
    face_one, next_moves, *stiff = call(
        faces_one_kernel, "faces_one", [VMEM] * 9, [VMEM] * 6,
        (sds((3, rim, depth)), grown) + faces(2),
        scratch=(pltpu.VMEM((3 * rim, 2 * depth), BF16),), cost=1.0,
    )(r, shear, lame, *halo, cell_maps, inner_moves)
    force_one, second_moves, message, targets, weights = call(
        forces_one_kernel, "forces_one", [VMEM] * 2 + [SMEM] + [VMEM] * 2,
        [VMEM] * 3 + [SMEM, HBM],
        (moves, grown, sds((bodies, 2 * cap, 4, width)), sds((pairs,), I32), pltpu.HBM(kept, BF16)),
        scratch=(
            pltpu.VMEM(kept, BF16), total, pltpu.VMEM((blocks, 32, width), BF16), dma((bodies,))
        ), cost=6.0, mib=kept_mib,
    )(got, own, table, first_moves, next_moves)
    got = lax.all_to_all(message, "body", 0, 0, tiled=True)
    w1, xe, xo, ye, yo, shear, lame, inertia = call(
        scatter_one_kernel, "scatter_one", [VMEM] * 6 + [HBM] * 3, [VMEM] * 8,
        (vector,) + faces(3) + cells, scratch=sides + (dma((3,)),), cost=3.0, mib=16,
    )(*elastic_one, face_one, force_one, cell_maps, *in_hbm(*given))
    halo_two = exchange(xe, xo, ye, yo)
    elastic_two, force_two, dots = call(
        apply_two_kernel, "apply_two", [VMEM] * 5 + [SMEM] * 2 + [VMEM, HBM], [VMEM] * 3,
        (vector, moves, sds((4, 128))),
        scratch=(pltpu.VMEM(kept, BF16), total, dma((bodies,))), cost=3.0, mib=kept_mib,
    )(w1, shear, lame, inertia, got, targets, table, second_moves, *in_hbm(weights))
    face_two, partial = call(
        faces_two_kernel, "faces_two", [VMEM] * 12, [VMEM] * 2,
        (sds((3, rim, depth)), sds((devices, 4, 128))), cost=1.0,
    )(w1, shear, lame, *halo_two, *stiff, dots)
    sums = lax.all_to_all(partial, ("body", "across"), 0, 0, tiled=True)
    w2, *parts = call(
        scatter_two_kernel, "scatter_two", [VMEM] * 4 + [HBM], [VMEM] * 4, (vector,) + cells,
        scratch=sides + (dma((3,)),), cost=3.0, mib=16,
    )(elastic_two, face_two, force_two, cell_maps, *in_hbm(cotangent))
    out = pltpu.VMEM((3, rows, cols, depth), F32)
    return call(
        final_kernel, "final", [VMEM] * 6, [HBM] * 2, (vector, vector),
        scratch=(out, out, dma((2, 3))), cost=1.0,
    )(*parts, w1, w2, sums)


def solution(mesh):
    placed = (
        P(None, "body", "across", None),
        P("body", "across", None),
        P("body", "across", None),
        P("body", "across", None),
        P("body", "across", None, None, None),
        P("body", "across", None),
        P("body", "across", None, None),
        P("body", "across", None, None),
    )
    return jax.shard_map(
        on_device,
        mesh=mesh,
        in_specs=placed,
        out_specs=(P(None, "body", "across", None), P(None, "body", "across", None)),
        check_vma=False,
    )
```
